32 devices in a mesh: dp: 16 (over z, y, core), mp: 2 (over x).
Axes of the slice: x: 2, y: 2, z: 4, core: 2. Of those that a mesh axis runs over, the one named last changes fastest.
Arguments:
- tokens: bfloat16 [16, 448, 768], P('dp'), may hold values from -6 to 6
- frames: bfloat16 [16, 1500, 768], P('dp'), may hold values from -6 to 6
- lengths: int32 [16], P('dp'), may hold values from 1 to 448, as said below
- out_cot: bfloat16 [16, 448, 768], P('dp'), may hold values from -6 to 6
- self_query_key_value: bfloat16 [768, 3, 768], P(None, None, 'mp'), may hold values from -0.21875 to 0.21875
- self_qv_bias: float32 [2, 768], P(None, 'mp'), may hold values from -1.75 to 1.75
- self_output_weight: bfloat16 [768, 768], P('mp'), may hold values from -0.875 to 0.875
- cross_query_weight: bfloat16 [768, 768], P(None, 'mp'), may hold values from -0.21875 to 0.21875
- cross_kv: bfloat16 [768, 2, 768], P(None, None, 'mp'), may hold values from -0.21875 to 0.21875
- cross_bias: float32 [2, 768], P(None, 'mp'), may hold values from -1.75 to 1.75
- cross_output_weight: bfloat16 [768, 768], P('mp'), may hold values from -1.25 to 1.25
- first_dense_weight: bfloat16 [768, 3072], P(None, 'mp'), may hold values from -0.21875 to 0.21875
- first_dense_bias: float32 [3072], P('mp'), may hold values from -1.75 to 1.75
- second_dense_weight: bfloat16 [3072, 768], P('mp'), may hold values from -0.109375 to 0.109375
- out_biases: float32 [3, 768], replicated, may hold values from -1.75 to 1.75
- norm_gains: float32 [4, 768], replicated, may hold values from 0.25 to 1.75
- norm_biases: float32 [4, 768], replicated, may hold values from -1.75 to 1.75
Outputs:
- out: bfloat16 [16, 448, 768], P('dp')
- tokens_grad: float32 [16, 448, 768], P('dp')
- frames_grad: float32 [16, 1500, 768], P('dp', None, 'mp')
- self_qkv_grad: float32 [768, 3, 768], P('dp', None, 'mp')
- self_qv_bias_grad: float32 [2, 768], P(None, 'mp')
- self_out_grad: float32 [768, 768], P('mp', 'dp')
- cross_q_grad: float32 [768, 768], P('dp', 'mp')
- cross_kv_grad: float32 [768, 2, 768], P('dp', None, 'mp')
- cross_bias_grad: float32 [2, 768], P(None, 'mp')
- cross_out_grad: float32 [768, 768], P('mp', 'dp')
- fc1_grad: float32 [768, 3072], P('dp', 'mp')
- fc1_bias_grad: float32 [3072], P('mp')
- second_dense_gradient: float32 [3072, 768], P('mp', 'dp')
- out_biases_grad: float32 [3, 768], replicated
- norm_gains_grad: float32 [4, 768], replicated
- norm_biases_grad: float32 [4, 768], replicated
The draws below stay inside these ranges and needn't reach their ends.
Inputs may be any that keep to these rules, and one draw needn't show every extreme that they name: `lengths`: each transcript has at least one token; some transcript fills all 448 slots.
All inputs are finite; a program needn't handle non-finite values.
Results may differ from the reference program's by a relative error of at most 0.024.
Values sent between devices are 32-bit elements; how exact they have to be, the bound alone decides.
No kernel may reach another device: no remote copies, remote signals or barrier semaphores. Data moves between devices by JAX's collectives and lax.ppermute only.
A program may use at most 192 MiB of HBM per device.

```python
import jax
import jax.numpy as jnp
from jax import lax

D = 768
HEADS = 12
HEAD_DIM = 64
FF = 3072
SLOT = 448
FRAMES = 1500
SEQ_DEV = 1
SEQS = 16
N_DP = 16


def draw_lengths(key, part):
    key_short, key_long, key_pick, key_top = jax.random.split(key, 4)
    short_len = jax.random.randint(key_short, (SEQS,), 1, max(2, SLOT // 7) + 1)
    longer = jax.random.randint(key_long, (SEQS,), SLOT // 2, SLOT + 1)
    choose = jax.random.randint(key_pick, (SEQS,), 0, 2)
    result = jnp.where(choose == 1, longer, short_len)
    top_place = jax.random.randint(key_top, (), 0, SEQS)
    result = result.at[top_place].set(SLOT)
    return result.astype(jnp.int32)


def spiked(array, rng, source, target, shards_of, factor):
    def block_of(position):
        return (jnp.arange(array.shape[position]) // (array.shape[position] // shards_of)).reshape((-1,) + (1,) * (array.ndim - 1 - position))

    first = jax.random.permutation(rng, shards_of)[block_of(target)]
    other_side = (block_of(target) + shards_of // 2) % shards_of
    return jnp.where((block_of(source) == first) | (block_of(source) == other_side), factor * array, array)


def levels(key, dims, cuts, low, top_value):
    def one(dim, blocks):
        draws = jax.random.uniform(jax.random.fold_in(jax.random.fold_in(key, 6), dim), (blocks,), jnp.float32, low / len(cuts), top_value / len(cuts))
        return jnp.repeat(jnp.exp(draws), dims[dim] // blocks).reshape((-1,) + (1,) * (len(dims) - dim - 1))

    factor_of = one(*cuts[0])
    for cut in cuts[1:]:
        factor_of = factor_of * one(*cut)
    return factor_of


def gaussian(rng, extent, scale, limit, cuts=(), held_as=jnp.bfloat16):
    array = jax.random.normal(rng, extent, jnp.float32) * scale
    if len(cuts) > 0:
        array = levels(rng, extent, cuts, -0.22, 0.18) * array
    return jnp.clip(array, min=-limit, max=limit).astype(held_as)


def gaussian_with(stream_key, dims, scale, reach, cuts, heavy, held_as=jnp.bfloat16):
    array = scale * jax.random.normal(stream_key, dims, jnp.float32)
    if cuts:
        array = array * levels(stream_key, dims, cuts, -0.22, 0.18)
    return jnp.clip(spiked(array, jax.random.fold_in(stream_key, 3), *heavy), -reach, reach).astype(held_as)


def setup_inputs(seed: int = 0) -> dict:
    splits = jax.random.split(jax.random.key(seed), 18)
    return {
        "tokens": gaussian_with(splits[0], (SEQS, SLOT, D), 1.0, 6.0, ((0, 16),), (0, 2, 16, 2.0)),
        "frames": gaussian(splits[1], (SEQS, FRAMES, D), 1.0, 6.0, ((0, 16),)),
        "lengths": draw_lengths(jax.random.fold_in(splits[17], 71), 0),
        "out_cot": gaussian_with(splits[3], (SEQS, SLOT, D), 1.0, 6.0, ((0, 16),), (0, 2, 16, 2.0)),
        "self_query_key_value": gaussian(splits[4], (D, 3, D), D ** -0.5, 0.21875, ((2, 2),)),
        "self_qv_bias": gaussian(splits[5], (2, D), 0.3, 1.75, ((1, 2),), jnp.float32),
        "self_output_weight": gaussian(splits[6], (D, D), (D // 16) ** -0.5, 0.875, ((0, 2),)),
        "cross_query_weight": gaussian(splits[7], (D, D), D ** -0.5, 0.21875, ((1, 2),)),
        "cross_kv": gaussian(splits[8], (D, 2, D), D ** -0.5, 0.21875, ((2, 2),)),
        "cross_bias": gaussian(splits[9], (2, D), 0.3, 1.75, ((1, 2),), jnp.float32),
        "cross_output_weight": gaussian(splits[10], (D, D), (D // 32) ** -0.5, 1.25, ((0, 2),)),
        "first_dense_weight": gaussian(splits[11], (D, FF), D ** -0.5, 0.21875, ((1, 2),)),
        "first_dense_bias": gaussian(splits[12], (FF,), 0.3, 1.75, ((0, 2),), jnp.float32),
        "second_dense_weight": gaussian(splits[13], (FF, D), FF ** -0.5, 0.109375, ((0, 2),)),
        "out_biases": gaussian(splits[14], (3, D), 0.3, 1.75, (), jnp.float32),
        "norm_gains": jnp.clip(1.0 + 0.15 * jax.random.normal(splits[15], (4, D), jnp.float32), 0.25, 1.75),
        "norm_biases": gaussian(splits[16], (4, D), 0.3, 1.75, (), jnp.float32),
    }


@jax.custom_vjp
def low(v):
    return lax.optimization_barrier(v.astype(jnp.bfloat16)).astype(jnp.float32)

@jax.custom_vjp
def low_back(v):
    return v

def low_keep(v):
    return (low(v), None)

def low_pass(kept, grad):
    return (grad,)

def back_keep(v):
    return (v, None)

def back_low(kept, grad):
    return (low(grad),)
low.defvjp(low_keep, low_pass)
low_back.defvjp(back_keep, back_low)
highest = lax.Precision.HIGHEST

def product(left, right):
    return jnp.dot(left, right, precision=highest)

def norm_rows(stream, norm_gain, norm_shift):
    centred = stream - lax.optimization_barrier(jnp.mean(stream, axis=-1, keepdims=True))
    spread = lax.optimization_barrier(jnp.mean(centred * centred, axis=-1, keepdims=True))
    return centred * lax.rsqrt(spread + 1e-05) * norm_gain + norm_shift

def attend(query_rows, key_rows, value_rows, key_mask):
    query_heads = query_rows.reshape(query_rows.shape[0], query_rows.shape[1], HEADS, HEAD_DIM)
    key_heads = key_rows.reshape(key_rows.shape[0], key_rows.shape[1], HEADS, HEAD_DIM)
    value_heads = value_rows.reshape(value_rows.shape[0], value_rows.shape[1], HEADS, HEAD_DIM)
    scores = low_back(jnp.einsum('sqhd,skhd->shqk', query_heads, key_heads, precision=highest))
    if key_mask is not None:
        scores = jnp.where(key_mask, scores, -1e+30)
    weights = low(jax.nn.softmax(scores, axis=-1))
    mixed_heads = jnp.einsum('shqk,skhd->sqhd', weights, value_heads, precision=highest)
    return mixed_heads.reshape(query_rows.shape)

def layer_forward(tokens, frames, valid, key_mask, self_query_key_value, self_qv_bias, self_output_weight, cross_query_weight, cross_kv, cross_bias, cross_output_weight, first_dense_weight, first_dense_bias, second_dense_weight, out_biases, norm_gains, norm_biases):
    seq_count = tokens.shape[0]
    first_input = low(norm_rows(tokens, norm_gains[0], norm_biases[0]))
    merged_heads = product(first_input, self_query_key_value.reshape(D, 3 * D)).reshape(seq_count, SLOT, 3, D)
    queries_self = low(low_back((merged_heads[:, :, 0] + self_qv_bias[0]) * 0.125))
    keys_self = low(low_back(merged_heads[:, :, 1]))
    values_self = low(low_back(merged_heads[:, :, 2] + self_qv_bias[1]))
    self_mixture = low(low_back(attend(queries_self, keys_self, values_self, key_mask)))
    stream_one = tokens + low_back(product(self_mixture, self_output_weight)) + out_biases[0]
    second_input = low(norm_rows(stream_one, norm_gains[1], norm_biases[1]))
    queries_cross = low(low_back((product(second_input, cross_query_weight) + cross_bias[0]) * 0.125))
    frame_pair = product(frames, cross_kv.reshape(D, 2 * D)).reshape(seq_count, FRAMES, 2, D)
    keys_cross = low(low_back(frame_pair[:, :, 0]))
    values_cross = low(low_back(frame_pair[:, :, 1] + cross_bias[1]))
    cross_mixture = low(low_back(attend(queries_cross, keys_cross, values_cross, None)))
    stream_two = stream_one + low_back(product(cross_mixture, cross_output_weight)) + out_biases[1]
    third_input = low(norm_rows(stream_two, norm_gains[2], norm_biases[2]))
    hidden = low_back(product(third_input, first_dense_weight) + first_dense_bias)
    active = low(jax.nn.gelu(hidden, approximate=False))
    stream_three = stream_two + low_back(product(active, second_dense_weight)) + out_biases[2]
    return norm_rows(stream_three, norm_gains[3], norm_biases[3]) * valid

def reference(tokens, frames, lengths, out_cot, self_query_key_value, self_qv_bias, self_output_weight, cross_query_weight, cross_kv, cross_bias, cross_output_weight, first_dense_weight, first_dense_bias, second_dense_weight, out_biases, norm_gains, norm_biases):
    params = tuple((item_weight.astype(jnp.float32) for item_weight in (self_query_key_value, self_qv_bias, self_output_weight, cross_query_weight, cross_kv, cross_bias, cross_output_weight, first_dense_weight, first_dense_bias, second_dense_weight, out_biases, norm_gains, norm_biases)))
    positions = jnp.arange(SLOT, dtype=jnp.int32)
    group_tokens = tokens.reshape(N_DP, SEQ_DEV, SLOT, D)
    group_frames = frames.reshape(N_DP, SEQ_DEV, FRAMES, D)
    group_lengths = lengths.reshape(N_DP, SEQ_DEV)
    group_cot = out_cot.reshape(N_DP, SEQ_DEV, SLOT, D)

    def group_step(totals, group):
        tok_group, frame_group, len_group, cot_group = group
        valid = (positions[None, :] < len_group[:, None]).astype(jnp.float32)[:, :, None]
        causal = positions[None, :] <= positions[:, None]
        key_mask = (causal[None] & (positions[None, None, :] < len_group[:, None, None]))[:, None]

        def forward(tok_float, frame_float, *weight_list):
            return layer_forward(tok_float, frame_float, valid, key_mask, *weight_list)
        output, pullback = jax.vjp(forward, tok_group.astype(jnp.float32), frame_group.astype(jnp.float32), *params)
        grads = pullback(cot_group.astype(jnp.float32))
        totals = tuple((total_item + grad_item for total_item, grad_item in zip(totals, grads[2:])))
        return (totals, (output.astype(jnp.bfloat16), grads[0], grads[1]))
    start = tuple((jnp.zeros(item_weight.shape, jnp.float32) for item_weight in params))
    totals, stacked = lax.scan(group_step, start, (group_tokens, group_frames, group_lengths, group_cot))
    output = stacked[0].reshape(SEQS, SLOT, D)
    tokens_grad = stacked[1].reshape(SEQS, SLOT, D)
    frames_grad = stacked[2].reshape(SEQS, FRAMES, D)
    return (output, tokens_grad, frames_grad, totals[0], totals[1], totals[2], totals[3], totals[4], totals[5], totals[6], totals[7], totals[8], totals[9], totals[10], totals[11], totals[12])
```

```python
from functools import partial

import jax
import jax.numpy as jnp
from jax import lax
from jax.sharding import PartitionSpec as P

HEAD_DIM = 64


def norm_rows(stream, norm_gain, norm_shift):
    centred = stream - jnp.mean(stream, axis=-1, keepdims=True)
    spread = jnp.mean(centred * centred, axis=-1, keepdims=True)
    return centred * lax.rsqrt(spread + 1e-05) * norm_gain + norm_shift


def split_heads(flat_rows):
    return flat_rows.reshape(flat_rows.shape[0], -1, HEAD_DIM)


def join_heads(headed):
    return headed.reshape(headed.shape[0], -1)


def dot(a, b):
    return lax.dot_general(a, b, (((1,), (0,)), ((), ())), preferred_element_type=jnp.float32)


def dot_nt(a, b):
    return lax.dot_general(a, b, (((1,), (1,)), ((), ())), preferred_element_type=jnp.float32)


def dot_tn(a, b):
    return lax.dot_general(a, b, (((0,), (0,)), ((), ())), preferred_element_type=jnp.float32)


def score_block(query_rows, key_rows, key_mask):
    scores = jnp.einsum("qhd,khd->hqk", query_rows, key_rows, preferred_element_type=jnp.float32)
    if key_mask is not None:
        scores = jnp.where(key_mask, scores, -1e30)
    return scores


def attend_forward(query_rows, key_rows, value_rows, key_mask):
    scores = score_block(query_rows, key_rows, key_mask)
    highest = jnp.max(scores, axis=-1, keepdims=True)
    log_total = highest + jnp.log(jnp.sum(jnp.exp(scores - highest), axis=-1, keepdims=True))
    weights = jnp.exp(scores - log_total).astype(jnp.bfloat16)
    mixed_heads = jnp.einsum("hqk,khd->qhd", weights, value_rows, preferred_element_type=jnp.float32)
    return (join_heads(mixed_heads).astype(jnp.bfloat16), log_total)


def attend_backward(query_rows, key_rows, value_rows, key_mask, log_total, grad_mixed):
    grad_heads = split_heads(grad_mixed)
    softmax_out = jnp.exp(score_block(query_rows, key_rows, key_mask) - log_total)
    weights = softmax_out.astype(jnp.bfloat16)
    grad_probs = jnp.einsum("qhd,khd->hqk", grad_heads, value_rows, preferred_element_type=jnp.float32)
    inner_sum = jnp.sum(softmax_out * grad_probs, axis=-1, keepdims=True)
    grad_scores = (softmax_out * (grad_probs - inner_sum)).astype(jnp.bfloat16)
    grad_queries = jnp.einsum("hqk,khd->qhd", grad_scores, key_rows, preferred_element_type=jnp.float32)
    grad_keys = jnp.einsum("hqk,qhd->khd", grad_scores, query_rows, preferred_element_type=jnp.float32)
    grad_values = jnp.einsum("hqk,qhd->khd", weights, grad_heads, preferred_element_type=jnp.float32)
    return (
        join_heads(grad_queries).astype(jnp.bfloat16),
        join_heads(grad_keys).astype(jnp.bfloat16),
        join_heads(grad_values).astype(jnp.bfloat16),
    )


def row_total(matrix_rows):
    return jnp.sum(matrix_rows, axis=0, dtype=jnp.float32)


def swap_mp(v):
    return lax.ppermute(v, "mp", [(0, 1), (1, 0)])


def swap_dp(v, bit, dp_size):
    return lax.ppermute(v, "dp", [(i, i ^ bit) for i in range(dp_size)])


def relative_order(width, dp_size):
    shard = width // dp_size
    bits = dp_size.bit_length() - 1
    me = lax.axis_index("dp")
    place = jnp.arange(width, dtype=jnp.int32)
    block = place // shard
    flipped = jnp.zeros_like(block)
    for step in range(bits):
        flipped = flipped + (((block >> step) & 1) << (bits - 1 - step))
    source = (flipped ^ me) * shard + place % shard
    rows = jnp.arange(width, dtype=jnp.int32)
    return (rows[:, None] == source[None, :]).astype(jnp.bfloat16)


def halving(lhs, rhs, dp_size):
    width = lhs.shape[1]
    half = width // 2
    sent = swap_dp(dot_tn(lhs[:, half:], rhs), 1, dp_size)
    kept = dot_tn(lhs[:, :half], rhs) + sent
    bit = 2
    while bit < dp_size:
        half = kept.shape[0] // 2
        kept = kept[:half] + swap_dp(kept[half:], bit, dp_size)
        bit *= 2
    return kept


def on_device(
    dp_size,
    tokens,
    frames,
    lengths,
    out_cot,
    self_query_key_value,
    self_qv_bias,
    self_output_weight,
    cross_query_weight,
    cross_kv,
    cross_bias,
    cross_output_weight,
    first_dense_weight,
    first_dense_bias,
    second_dense_weight,
    out_biases,
    norm_gains,
    norm_biases,
):
    _, slot_len, model_width = tokens.shape
    tokens, frames, out_cot = tokens[0], frames[0], out_cot[0]
    own = self_output_weight.shape[0]
    order = relative_order(model_width, dp_size)

    def reorder(lhs):
        return dot(lhs, order).astype(jnp.bfloat16)

    positions = jnp.arange(slot_len, dtype=jnp.int32)
    valid = (positions < lengths[0]).astype(jnp.float32)[:, None]
    causal = positions[None, :] <= positions[:, None]
    key_mask = (causal & (positions[None, :] < lengths[0]))[None]
    qkv_weight = self_query_key_value.reshape(model_width, -1)
    kv_weight = cross_kv.reshape(model_width, -1)
    stream_zero = tokens.astype(jnp.float32)
    normed_one, pull_one = jax.vjp(norm_rows, stream_zero, norm_gains[0], norm_biases[0])
    first_input = normed_one.astype(jnp.bfloat16)
    merged = dot(first_input, qkv_weight)
    queries_self = split_heads(((merged[:, :own] + self_qv_bias[0]) * 0.125).astype(jnp.bfloat16))
    keys_self = split_heads(merged[:, own : 2 * own].astype(jnp.bfloat16))
    values_self = split_heads((merged[:, 2 * own :] + self_qv_bias[1]).astype(jnp.bfloat16))
    self_mixture, lse_self = attend_forward(queries_self, keys_self, values_self, key_mask)
    self_portion = dot(self_mixture, self_output_weight)
    stream_one = stream_zero + (self_portion + swap_mp(self_portion)) + out_biases[0]
    normed_two, pull_two = jax.vjp(norm_rows, stream_one, norm_gains[1], norm_biases[1])
    second_input = normed_two.astype(jnp.bfloat16)
    query_projected = dot(second_input, cross_query_weight)
    queries_cross = split_heads(((query_projected + cross_bias[0]) * 0.125).astype(jnp.bfloat16))
    frame_pair = dot(frames, kv_weight)
    keys_cross = split_heads(frame_pair[:, :own].astype(jnp.bfloat16))
    values_cross = split_heads((frame_pair[:, own:] + cross_bias[1]).astype(jnp.bfloat16))
    cross_mixture, lse_cross = attend_forward(queries_cross, keys_cross, values_cross, None)
    part_cross = dot(cross_mixture, cross_output_weight)
    stream_two = stream_one + (part_cross + swap_mp(part_cross)) + out_biases[1]
    normed_three, pull_three = jax.vjp(norm_rows, stream_two, norm_gains[2], norm_biases[2])
    third_input = normed_three.astype(jnp.bfloat16)
    hidden = dot(third_input, first_dense_weight) + first_dense_bias
    active, gelu_pull = jax.vjp(partial(jax.nn.gelu, approximate=False), hidden)
    active_reduced = active.astype(jnp.bfloat16)
    dense_portion = dot(active_reduced, second_dense_weight)
    stream_three = stream_two + (dense_portion + swap_mp(dense_portion)) + out_biases[2]
    final_norm, pull_four = jax.vjp(norm_rows, stream_three, norm_gains[3], norm_biases[3])
    output = (final_norm * valid).astype(jnp.bfloat16)
    grad_three, gain_four, shift_four = pull_four(out_cot.astype(jnp.float32) * valid)
    reduced_third = grad_three.astype(jnp.bfloat16)
    active_gradient = dot_nt(reduced_third, second_dense_weight)
    reduced_hidden = gelu_pull(active_gradient)[0].astype(jnp.bfloat16)
    reverse_third = dot_nt(reduced_hidden, first_dense_weight)
    swapped_third = swap_mp(reverse_third)
    second_dense_gradient = halving(reorder(reduced_third), active_reduced, dp_size)
    fc1_grad = halving(reorder(third_input), reduced_hidden, dp_size)
    fc1_bias_grad = row_total(reduced_hidden)
    grad_part_two, gain_three, shift_three = pull_three(reverse_third + swapped_third)
    grad_two = grad_three + grad_part_two
    reduced_second = grad_two.astype(jnp.bfloat16)
    cross_out_grad = halving(reorder(reduced_second), cross_mixture, dp_size)
    grad_mixed_cross = dot_nt(reduced_second, cross_output_weight).astype(jnp.bfloat16)
    grad_qc, grad_kc, grad_vc = attend_backward(
        queries_cross, keys_cross, values_cross, None, lse_cross, grad_mixed_cross
    )
    reduced_cross_query = grad_qc * 0.125
    back_two = dot_nt(reduced_cross_query, cross_query_weight)
    swapped_two = swap_mp(back_two)
    low_frame_pair = jnp.concatenate([grad_kc, grad_vc], axis=1)
    cross_q_grad = halving(reorder(second_input), reduced_cross_query, dp_size)
    cross_kv_grad = halving(reorder(frames), low_frame_pair, dp_size)
    my_part = lax.axis_index("mp")
    frame_width = model_width // 2
    other_weight = lax.dynamic_slice_in_dim(kv_weight, (1 - my_part) * frame_width, frame_width, 0)
    own_weight = lax.dynamic_slice_in_dim(kv_weight, my_part * frame_width, frame_width, 0)
    sent_frames = swap_mp(dot_nt(low_frame_pair, other_weight))
    frames_grad = dot_nt(low_frame_pair, own_weight) + sent_frames
    grad_part_one, gain_two, shift_two = pull_two(back_two + swapped_two)
    grad_one = grad_two + grad_part_one
    reduced_first = grad_one.astype(jnp.bfloat16)
    self_out_grad = halving(reorder(reduced_first), self_mixture, dp_size)
    grad_mixed_self = dot_nt(reduced_first, self_output_weight).astype(jnp.bfloat16)
    grad_qs, grad_ks, grad_vs = attend_backward(
        queries_self, keys_self, values_self, key_mask, lse_self, grad_mixed_self
    )
    low_query_self = grad_qs * 0.125
    reduced_merged = jnp.concatenate([low_query_self, grad_ks, grad_vs], axis=1)
    reverse_first = dot_nt(reduced_merged, qkv_weight)
    swapped_first = swap_mp(reverse_first)
    self_qkv_grad = halving(reorder(first_input), reduced_merged, dp_size)
    grad_part_zero, gain_one, shift_one = pull_one(reverse_first + swapped_first)
    tokens_grad = grad_one + grad_part_zero
    small = [
        row_total(low_query_self),
        row_total(grad_vs),
        row_total(reduced_cross_query),
        row_total(grad_vc),
        fc1_bias_grad,
        row_total(grad_one),
        row_total(grad_two),
        row_total(grad_three),
        gain_one,
        gain_two,
        gain_three,
        gain_four,
        shift_one,
        shift_two,
        shift_three,
        shift_four,
    ]
    total = jnp.concatenate(small)
    bit = 1
    while bit < dp_size:
        total = total + swap_dp(total, bit, dp_size)
        bit *= 2
    pieces = []
    at = 0
    for item in small:
        pieces.append(total[at : at + item.shape[0]])
        at += item.shape[0]
    shard = model_width // dp_size
    return (
        output[None],
        tokens_grad[None],
        frames_grad[None],
        self_qkv_grad.reshape(shard, 3, own),
        jnp.stack(pieces[0:2]),
        self_out_grad.T,
        cross_q_grad,
        cross_kv_grad.reshape(shard, 2, own),
        jnp.stack(pieces[2:4]),
        cross_out_grad.T,
        fc1_grad,
        pieces[4],
        second_dense_gradient.T,
        jnp.stack(pieces[5:8]),
        jnp.stack(pieces[8:12]),
        jnp.stack(pieces[12:16]),
    )


def solution(mesh):
    in_specs = (
        P("dp", None, None),
        P("dp", None, None),
        P("dp"),
        P("dp", None, None),
        P(None, None, "mp"),
        P(None, "mp"),
        P("mp", None),
        P(None, "mp"),
        P(None, None, "mp"),
        P(None, "mp"),
        P("mp", None),
        P(None, "mp"),
        P("mp"),
        P("mp", None),
        P(),
        P(),
        P(),
    )
    out_specs = (
        P("dp", None, None),
        P("dp", None, None),
        P("dp", None, "mp"),
        P("dp", None, "mp"),
        P(None, "mp"),
        P("mp", "dp"),
        P("dp", "mp"),
        P("dp", None, "mp"),
        P(None, "mp"),
        P("mp", "dp"),
        P("dp", "mp"),
        P("mp"),
        P("mp", "dp"),
        P(),
        P(),
        P(),
    )
    return jax.shard_map(
        partial(on_device, mesh.shape["dp"]),
        mesh=mesh,
        in_specs=in_specs,
        out_specs=out_specs,
        check_vma=False,
    )
```

```python
from functools import partial

import jax
import jax.numpy as jnp
from jax import lax
from jax.experimental import pallas as pl
from jax.experimental.pallas import tpu as pltpu
from jax.sharding import PartitionSpec as P

F32 = jnp.float32
BF = jnp.bfloat16
HEAD_DIM = 64
LANES = 128
NEG = -1e30
VMEM = pl.BlockSpec(memory_space=pltpu.VMEM)
SMEM = pl.BlockSpec(memory_space=pltpu.SMEM)


def shaped(shape, dtype):
    return jax.ShapeDtypeStruct(shape, dtype)


def call(kernel, outs, args, flops, in_specs=None, scratch=(), name=None):
    moved = sum(a.size * a.dtype.itemsize for a in args)
    moved += sum(math_size(o) for o in outs)
    return pl.pallas_call(
        kernel,
        out_shape=tuple(outs),
        in_specs=in_specs or [VMEM] * len(args),
        out_specs=tuple(VMEM for _ in outs),
        scratch_shapes=scratch,
        compiler_params=pltpu.CompilerParams(vmem_limit_bytes=48 * 1024 * 1024),
        cost_estimate=pl.CostEstimate(flops=int(flops), transcendentals=0, bytes_accessed=int(moved)),
        name=name,
    )(*args)


def math_size(o):
    total = jnp.dtype(o.dtype).itemsize
    for d in o.shape:
        total *= d
    return total


def dg(a, b, ca, cb):
    return lax.dot_general(a, b, (((ca,), (cb,)), ((), ())), preferred_element_type=F32)


def nn(a, b):
    return dg(a, b, 1, 0)


def nt(a, b):
    return dg(a, b, 1, 1)


def tn(a, b):
    return dg(a, b, 0, 0)


def standard(stream):
    centred = stream - jnp.mean(stream, axis=1, keepdims=True)
    spread = jnp.mean(centred * centred, axis=1, keepdims=True)
    scale = lax.rsqrt(spread + 1e-05)
    return centred * scale, scale


def norm_back(grad, unit, scale, gain):
    lifted = grad * gain
    mean_plain = jnp.mean(lifted, axis=1, keepdims=True)
    mean_cross = jnp.mean(lifted * unit, axis=1, keepdims=True)
    return scale * (lifted - mean_plain - unit * mean_cross)


def column_sums(values):
    return jnp.sum(values, axis=0, keepdims=True)


def head_lanes(which):
    lane = lax.broadcasted_iota(jnp.int32, (1, LANES), 1)
    return (lane < HEAD_DIM) if which == 0 else (lane >= HEAD_DIM)


def only(mask, values):
    return jnp.where(mask, values, jnp.zeros_like(values))


def pair_slice(pair):
    return pl.ds(pl.multiple_of(pair * LANES, LANES), LANES)


def attend_rows(q_ref, k_ref, v_ref, rows, keys, bias, mixed_ref, out_ref, lse_ref):
    lane = lax.broadcasted_iota(jnp.int32, (1, LANES), 1)
    count = rows.stop - rows.start

    def body(pair, lse):
        at = pair_slice(pair)
        k_pair, v_pair, q_pair = k_ref[0:keys, at], v_ref[0:keys, at], q_ref[rows, at]
        result = None
        for which in range(2):
            mask = head_lanes(which)
            scores = nt(only(mask, q_pair), k_pair) + bias
            top = jnp.max(scores, axis=1, keepdims=True)
            raised = jnp.exp(scores - top)
            total = jnp.sum(raised, axis=1, keepdims=True)
            value = nn(raised.astype(BF), v_pair) * (1.0 / total)
            result = value if which == 0 else jnp.where(mask, value, result)
            lse = jnp.where(lane == 2 * pair + which, top + jnp.log(total), lse)
        out_ref[:, at] = result
        mixed_ref[:, at] = result.astype(BF)
        return lse

    lse = lax.fori_loop(0, q_ref.shape[1] // LANES, body, jnp.zeros((count, LANES), F32))
    lse_ref[...] = lse.T[0 : lse_ref.shape[0]]


def attend_back(q_ref, g_ref, o_ref, lse_ref, k_ref, v_ref, rows, keys, bias, first, dq_ref, dk_ref, dv_ref):
    def body(pair, carry):
        at = pair_slice(pair)
        k_pair, v_pair = k_ref[0:keys, at], v_ref[0:keys, at]
        q_pair, g_pair = q_ref[rows, at], g_ref[:, at]
        product = (g_pair.astype(F32) * o_ref[:, at]).T
        k_turned = k_pair.T
        parts = []
        for which in range(2):
            mask = head_lanes(which)
            q_head, g_head = only(mask, q_pair), only(mask, g_pair)
            inner = column_sums(product[which * HEAD_DIM : (which + 1) * HEAD_DIM])
            scores = nt(k_pair, q_head) + bias
            probs = jnp.exp(scores - lse_ref[pl.ds(2 * pair + which, 1), :])
            grad_probs = nt(v_pair, g_head)
            grad_scores = (probs * (grad_probs - inner)).astype(BF)
            grad_v = nn(probs.astype(BF), g_head)
            grad_k = nn(grad_scores, q_head)
            if which == 0 and first:
                dk_ref[0:keys, at] = grad_k
                dv_ref[0:keys, at] = grad_v
            else:
                dk_ref[0:keys, at] += grad_k
                dv_ref[0:keys, at] += grad_v
            parts.append(nn(k_turned[which * HEAD_DIM : (which + 1) * HEAD_DIM], grad_scores))
        dq_ref[:, at] = jnp.concatenate(parts, axis=0).T
        return carry

    lax.fori_loop(0, q_ref.shape[1] // LANES, body, 0)


def causal_bias(rows, keys, length, turned):
    count = rows.stop - rows.start
    shape = (keys, count) if turned else (count, keys)
    query = lax.broadcasted_iota(jnp.int32, shape, 1 if turned else 0) + rows.start
    key = lax.broadcasted_iota(jnp.int32, shape, 0 if turned else 1)
    return jnp.where((key <= query) & (key < length), 0.0, NEG).astype(F32)


def tail_bias(keys, real, turned):
    shape = (keys, 1) if turned else (1, keys)
    key = lax.broadcasted_iota(jnp.int32, shape, 0 if turned else 1)
    return jnp.where(key < real, 0.0, NEG).astype(F32)


def self_start(rows, tok, w, vb, gains, shifts, length, wo, x_ref, q_ref, k_ref, v_ref, mixed, out, lse, part):
    unit, _ = standard(tok[...].astype(F32))
    x = (unit * gains[0:1] + shifts[0:1]).astype(BF)
    x_ref[...] = x
    q_ref[...] = ((nn(x, w[0]) + vb[0:1]) * 0.125).astype(BF)
    k_ref[...] = nn(x, w[1]).astype(BF)
    v_ref[...] = (nn(x, w[2]) + vb[1:2]).astype(BF)
    bias = causal_bias(rows, rows.stop, length[0], False)
    attend_rows(q_ref, k_ref, v_ref, rows, rows.stop, bias, mixed, out, lse)
    part[...] = nn(mixed[...], wo[...])


def self_next(rows, q_ref, k_ref, v_ref, length, wo, mixed, out, lse, part):
    bias = causal_bias(rows, rows.stop, length[0], False)
    attend_rows(q_ref, k_ref, v_ref, rows, rows.stop, bias, mixed, out, lse)
    part[...] = nn(mixed[...], wo[...])


def frames_start(frames, w, vb, k_ref, v_ref):
    real, padded = frames.shape[0], k_ref.shape[0]
    if padded > real:
        low = real // 16 * 16
        k_ref[low:padded] = jnp.zeros((padded - low, k_ref.shape[1]), BF)
        v_ref[low:padded] = jnp.zeros((padded - low, v_ref.shape[1]), BF)
    k_ref[0:real] = nn(frames[...], w[0]).astype(BF)
    v_ref[0:real] = (nn(frames[...], w[1]) + vb[1:2]).astype(BF)


def cross_start(rows, real, tok, mine, other, ob, gains, shifts, wq, vb, k_ref, v_ref, wo,
                s_ref, x_ref, q_ref, mixed, out, lse, part):
    stream = tok[rows].astype(F32) + (mine[...] + other[...]) + ob[0:1]
    s_ref[...] = stream
    unit, _ = standard(stream)
    x = (unit * gains[1:2] + shifts[1:2]).astype(BF)
    x_ref[...] = x
    q_ref[...] = ((nn(x, wq[...]) + vb[0:1]) * 0.125).astype(BF)
    keys = k_ref.shape[0]
    attend_rows(q_ref, k_ref, v_ref, slice(0, x.shape[0]), keys, tail_bias(keys, real, False), mixed, out, lse)
    part[...] = nn(mixed[...], wo[...])


def dense_start(s_in, mine, other, ob, gains, shifts, w1, fb, w2, s_ref, x_ref, active, slope, part):
    stream = s_in[...] + (mine[...] + other[...]) + ob[1:2]
    s_ref[...] = stream
    unit, _ = standard(stream)
    x_ref[...] = (unit * gains[2:3] + shifts[2:3]).astype(BF)
    wide = 3 * LANES

    def body(step, carry):
        at = pl.ds(pl.multiple_of(step * wide, wide), wide)
        hidden = nn(x_ref[...], w1[:, at]) + fb[:, at]
        below = 0.5 + 0.5 * lax.erf(hidden * 0.7071067811865476)
        slope[:, at] = below + hidden * (0.3989422804014327 * jnp.exp(-0.5 * hidden * hidden))
        value = (hidden * below).astype(BF)
        active[:, at] = value
        part[...] += nn(value, w2[at, :])
        return carry

    part[...] = jnp.zeros_like(part)
    lax.fori_loop(0, w1.shape[1] // wide, body, 0)


def dense_back(rows, s_in, mine, other, ob, gains, shifts, cot, length, slope, w1, w2,
               out_ref, g_ref, low_ref, hid_ref, part, sums, hid_sums):
    stream = s_in[...] + (mine[...] + other[...]) + ob[2:3]
    unit, scale = standard(stream)
    row = lax.broadcasted_iota(jnp.int32, (stream.shape[0], 1), 0) + rows.start
    valid = (row < length[0]).astype(F32)
    out_ref[...] = ((unit * gains[3:4] + shifts[3:4]) * valid).astype(BF)
    incoming = cot[rows].astype(F32) * valid
    grad = norm_back(incoming, unit, scale, gains[3:4])
    g_ref[...] = grad
    low_ref[...] = grad.astype(BF)
    sums[0:1] = column_sums(incoming * unit)
    sums[1:2] = column_sums(incoming)
    sums[2:3] = column_sums(grad)
    wide = 3 * LANES

    def body(step, carry):
        at = pl.ds(pl.multiple_of(step * wide, wide), wide)
        low = (slope[:, at] * nt(low_ref[...], w2[at, :])).astype(BF)
        hid_ref[:, at] = low
        hid_sums[0:1, at] = column_sums(low.astype(F32))
        part[...] += nt(low, w1[:, at])
        return carry

    part[...] = jnp.zeros_like(part)
    lax.fori_loop(0, w1.shape[1] // wide, body, 0)


def cross_back(first, real, s_in, g_in, mine, other, gains, wo, q_ref, out_in, lse, k_ref, v_ref, wq, *refs):
    if first:
        g_ref, low_ref, lq_ref, part, sums, dk, dv, gm, dq = refs
    else:
        dk_in, dv_in, g_ref, low_ref, lq_ref, part, sums, lk_ref, lv_ref, gm, dq, dk, dv = refs
        dk[...] = dk_in[...]
        dv[...] = dv_in[...]
    unit, scale = standard(s_in[...])
    incoming = mine[...] + other[...]
    grad = g_in[...] + norm_back(incoming, unit, scale, gains[2:3])
    g_ref[...] = grad
    low = grad.astype(BF)
    low_ref[...] = low
    sums[0:1] = column_sums(incoming * unit)
    sums[1:2] = column_sums(incoming)
    sums[2:3] = column_sums(grad)
    gm[...] = nt(low, wo[...]).astype(BF)
    keys, width = k_ref.shape
    attend_back(q_ref, gm, out_in, lse, k_ref, v_ref, slice(0, low.shape[0]), keys,
                tail_bias(keys, real, True), first, dq, dk, dv)
    low_q = (dq[...].astype(BF).astype(F32) * 0.125).astype(BF)
    lq_ref[...] = low_q
    part[...] = nt(low_q, wq[...])
    sums[3:4, 0:width] = column_sums(low_q.astype(F32))
    if not first:
        lk_ref[...] = dk[...].astype(BF)
        low_v = dv[...].astype(BF)
        lv_ref[...] = low_v
        sums[3:4, width : 2 * width] = column_sums(low_v[0:real].astype(F32))


def frames_sent(which, lk, lv, w, out):
    real, width = out.shape
    at = pl.ds(pl.multiple_of((1 - which[0]) * width, width), width)
    out[...] = nt(lk[0:real], w[0, at, :]) + nt(lv[0:real], w[1, at, :])


def frames_kept(which, lk, lv, w, other, out):
    real, width = other.shape
    at = pl.ds(pl.multiple_of(which[0] * width, width), width)
    out[...] = nt(lk[0:real], w[0, at, :]) + nt(lv[0:real], w[1, at, :]) + other[...]


def self_back(rows, first, keep, s_in, g_in, mine, other, gains, wo, q_ref, out_in, lse, k_ref, v_ref, w, length, *refs):
    if first:
        g_ref, low_ref, l3_ref, part, sums, dk_out, dv_out, gm, dq, dk, dv = refs
    else:
        dk_in, dv_in, g_ref, low_ref, l3_ref, part, sums, gm, dq, dk, dv = refs
        dk[...] = dk_in[...]
        dv[...] = dv_in[...]
    unit, scale = standard(s_in[...])
    incoming = mine[...] + other[...]
    grad = g_in[...] + norm_back(incoming, unit, scale, gains[1:2])
    g_ref[...] = grad
    low = grad.astype(BF)
    low_ref[...] = low
    sums[0:1] = column_sums(incoming * unit)
    sums[1:2] = column_sums(incoming)
    sums[2:3] = column_sums(grad)
    gm[...] = nt(low, wo[...]).astype(BF)
    width = k_ref.shape[1]
    bias = causal_bias(rows, rows.stop, length[0], True)
    attend_back(q_ref, gm, out_in, lse, k_ref, v_ref, rows, rows.stop, bias, first, dq, dk, dv)
    low_q = (dq[...].astype(BF).astype(F32) * 0.125).astype(BF)
    low_k = dk[rows].astype(BF)
    low_v = dv[rows].astype(BF)
    l3_ref[0] = low_q
    l3_ref[1] = low_k
    l3_ref[2] = low_v
    part[...] = nt(low_q, w[0]) + nt(low_k, w[1]) + nt(low_v, w[2])
    sums[3:4, 0:width] = column_sums(low_q.astype(F32))
    sums[3:4, width : 2 * width] = column_sums(low_v.astype(F32))
    if first:
        dk_out[...] = dk[0:keep]
        dv_out[...] = dv[0:keep]


def tokens_end(cut, tok, gains, g_low, g_high, mine_low, other_low, mine_high, other_high, out, sums):
    total = None
    for rows, g, mine, other in (
        (slice(0, cut), g_low, mine_low, other_low),
        (slice(cut, tok.shape[0]), g_high, mine_high, other_high),
    ):
        unit, scale = standard(tok[rows].astype(F32))
        incoming = mine[...] + other[...]
        out[rows] = g[...] + norm_back(incoming, unit, scale, gains[0:1])
        here = (column_sums(incoming * unit), column_sums(incoming))
        total = here if total is None else (total[0] + here[0], total[1] + here[1])
    sums[0:1] = total[0]
    sums[1:2] = total[1]


def grads_sent(layout, *refs):
    order = refs[0]
    at = 1
    ins, col = [], 0
    for parts, blocks in layout:
        lhs = refs[at : at + parts]
        at += parts
        rhs = refs[at : at + parts]
        at += parts
        ins.append((lhs, rhs, blocks))
    out = refs[at]
    turned = refs[at + 1 :]
    half = out.shape[0]
    n = 0
    for lhs, rhs, blocks in ins:
        for part in range(len(lhs)):
            turned[n + part][...] = nn(lhs[part][...], order[...]).astype(BF)
        width = rhs[0].shape[-1]
        for block in range(blocks):
            total = None
            for part in range(len(lhs)):
                right = rhs[part][block] if len(rhs[part].shape) == 3 else rhs[part][...]
                term = tn(turned[n + part][:, half:], right)
                total = term if total is None else total + term
            out[:, col : col + width] = total
            col += width
        n += len(lhs)


def grads_kept(layout, *refs):
    at = 0
    ins, col = [], 0
    for parts, blocks in layout:
        lhs = refs[at : at + parts]
        at += parts
        rhs = refs[at : at + parts]
        at += parts
        ins.append((lhs, rhs, blocks))
    other = refs[at]
    sent, kept = refs[at + 1 :]
    half, low = other.shape[0], kept.shape[0]
    for lhs, rhs, blocks in ins:
        width = rhs[0].shape[-1]
        for block in range(blocks):
            total = other[:, col : col + width]
            for part in range(len(lhs)):
                right = rhs[part][block] if len(rhs[part].shape) == 3 else rhs[part][...]
                total = total + tn(lhs[part][:, :half], right)
            kept[:, col : col + width] = total[:low]
            sent[:, col : col + width] = total[low:]
            col += width


def swap_mp(v):
    return lax.ppermute(v, "mp", [(0, 1), (1, 0)])


def swap_dp(v, bit, dp_size):
    return lax.ppermute(v, "dp", [(i, i ^ bit) for i in range(dp_size)])


def relative_order(width, dp_size):
    shard = width // dp_size
    bits = dp_size.bit_length() - 1
    me = lax.axis_index("dp")
    place = jnp.arange(width, dtype=jnp.int32)
    block = place // shard
    flipped = jnp.zeros_like(block)
    for step in range(bits):
        flipped = flipped + (((block >> step) & 1) << (bits - 1 - step))
    source = (flipped ^ me) * shard + place % shard
    rows = jnp.arange(width, dtype=jnp.int32)
    return (rows[:, None] == source[None, :]).astype(BF)


def halving(order, groups, dp_size, name):
    layout = tuple((len(lhs), blocks) for lhs, rhs, blocks in groups)
    model = order.shape[0]
    columns = sum(rhs[0].shape[-1] * blocks for lhs, rhs, blocks in groups)
    flat = []
    for lhs, rhs, blocks in groups:
        flat += list(lhs) + list(rhs)
    rows = sum(p.shape[0] for p in groups[0][0])
    flops = rows * model * columns
    turned = [shaped(p.shape, BF) for lhs, rhs, blocks in groups for p in lhs]
    made = call(partial(grads_sent, layout), [shaped((model // 2, columns), F32)] + turned, [order] + flat, flops,
                name=name + "_sent")
    other = swap_dp(made[0], 1, dp_size)
    turned = list(made[1:])
    flat = []
    for lhs, rhs, blocks in groups:
        flat += turned[: len(lhs)] + list(rhs)
        turned = turned[len(lhs) :]
    half = shaped((model // 4, columns), F32)
    sent, kept = call(partial(grads_kept, layout), [half, half], flat + [other], flops, name=name + "_kept")
    kept = kept + swap_dp(sent, 2, dp_size)
    bit = 4
    while bit < dp_size:
        half = kept.shape[0] // 2
        kept = kept[:half] + swap_dp(kept[half:], bit, dp_size)
        bit *= 2
    return kept


def on_device(
    dp_size,
    tokens,
    frames,
    lengths,
    out_cot,
    self_query_key_value,
    self_qv_bias,
    self_output_weight,
    cross_query_weight,
    cross_kv,
    cross_bias,
    cross_output_weight,
    first_dense_weight,
    first_dense_bias,
    second_dense_weight,
    out_biases,
    norm_gains,
    norm_biases,
):
    _, slot, model = tokens.shape
    tok, frames, cot = tokens[0], frames[0], out_cot[0]
    real = frames.shape[0]
    padded = -(-real // 256) * 256
    own = self_output_weight.shape[0]
    ff = second_dense_weight.shape[0]
    cut = slot // 2 // 64 * 64
    low_rows, high_rows = slice(0, cut), slice(cut, slot)
    w3 = self_query_key_value.transpose(1, 0, 2)
    w2kv = cross_kv.transpose(1, 0, 2)
    fb = first_dense_bias[None]
    gains, shifts, ob = norm_gains, norm_biases, out_biases
    order = relative_order(model, dp_size)

    def count(rows):
        return rows.stop - rows.start

    def sized(rows, width, dtype=F32):
        return shaped((count(rows), width), dtype)

    def attended(rows):
        return [sized(rows, own, BF), sized(rows, own), shaped((8, count(rows)), F32), sized(rows, model)]

    x1, q1, k1, v1, mix1_h, out1_h, lse1_h, part1_h = call(
        partial(self_start, high_rows),
        [shaped((slot, model), BF)] + [shaped((slot, own), BF)] * 3 + attended(high_rows),
        [tok, w3, self_qv_bias, gains, shifts, lengths, self_output_weight],
        2 * slot * model * own * 3 + 8 * count(high_rows) * slot * own,
        in_specs=[VMEM] * 5 + [SMEM, VMEM],
        name="self_start",
    )
    other1_h = swap_mp(part1_h)
    mix1_l, out1_l, lse1_l, part1_l = call(
        partial(self_next, low_rows),
        attended(low_rows),
        [q1, k1, v1, lengths, self_output_weight],
        8 * count(low_rows) * cut * own,
        in_specs=[VMEM] * 3 + [SMEM, VMEM],
        name="self_next",
    )
    other1_l = swap_mp(part1_l)
    k2, v2 = call(
        frames_start,
        [shaped((padded, own), BF)] * 2,
        [frames, w2kv, cross_bias],
        4 * real * model * own,
        name="frames_start",
    )

    def cross(rows, mine, other):
        return call(
            partial(cross_start, rows, real),
            [sized(rows, model), sized(rows, model, BF), sized(rows, own, BF)] + attended(rows),
            [tok, mine, other, ob, gains, shifts, cross_query_weight, cross_bias, k2, v2, cross_output_weight],
            4 * count(rows) * model * own + 12 * count(rows) * padded * own,
            name="cross_start",
        )

    s1_h, x2_h, q2_h, mix2_h, out2_h, lse2_h, part2_h = cross(high_rows, part1_h, other1_h)
    other2_h = swap_mp(part2_h)
    s1_l, x2_l, q2_l, mix2_l, out2_l, lse2_l, part2_l = cross(low_rows, part1_l, other1_l)
    other2_l = swap_mp(part2_l)

    def dense(rows, s1, mine, other):
        return call(
            dense_start,
            [sized(rows, model), sized(rows, model, BF), sized(rows, ff, BF), sized(rows, ff), sized(rows, model)],
            [s1, mine, other, ob, gains, shifts, first_dense_weight, fb, second_dense_weight],
            8 * count(rows) * model * ff,
            name="dense_start",
        )

    s2_h, x3_h, act_h, slope_h, part3_h = dense(high_rows, s1_h, part2_h, other2_h)
    other3_h = swap_mp(part3_h)
    s2_l, x3_l, act_l, slope_l, part3_l = dense(low_rows, s1_l, part2_l, other2_l)
    other3_l = swap_mp(part3_l)

    def dense_b(rows, s2, mine, other, slope):
        return call(
            partial(dense_back, rows),
            [sized(rows, model, BF), sized(rows, model), sized(rows, model, BF), sized(rows, ff, BF),
             sized(rows, model), shaped((8, model), F32), shaped((8, ff), F32)],
            [s2, mine, other, ob, gains, shifts, cot, lengths, slope, first_dense_weight, second_dense_weight],
            6 * count(rows) * model * ff,
            in_specs=[VMEM] * 7 + [SMEM] + [VMEM] * 3,
            name="dense_back",
        )

    y_h, g3_h, low3_h, hid_h, part4_h, sum3_h, hsum_h = dense_b(high_rows, s2_h, part3_h, other3_h, slope_h)
    other4_h = swap_mp(part4_h)
    y_l, g3_l, low3_l, hid_l, part4_l, sum3_l, hsum_l = dense_b(low_rows, s2_l, part3_l, other3_l, slope_l)
    other4_l = swap_mp(part4_l)

    second_turned = halving(order, [((low3_h, low3_l), (act_h, act_l), 1)], dp_size, "second")
    fc1_grad = halving(order, [((x3_h, x3_l), (hid_h, hid_l), 1)], dp_size, "first")

    def cross_b(rows, first, s2, g3, mine, other, q2, out2, lse2, earlier):
        wide = [shaped((padded, own), F32)] * 2
        outs = [sized(rows, model), sized(rows, model, BF), sized(rows, own, BF), sized(rows, model),
                shaped((8, model), F32)]
        scratch = [pltpu.VMEM((count(rows), own), BF), pltpu.VMEM((count(rows), own), F32)]
        if first:
            outs += wide
        else:
            outs += [shaped((padded, own), BF)] * 2
            scratch += [pltpu.VMEM((padded, own), F32)] * 2
        return call(
            partial(cross_back, first, real),
            outs,
            [s2, g3, mine, other, gains, cross_output_weight, q2, out2, lse2, k2, v2, cross_query_weight] + earlier,
            4 * count(rows) * model * own + 24 * count(rows) * padded * own,
            scratch=scratch,
            name="cross_back",
        )

    g2_h, low2_h, lq2_h, part5_h, sum2_h, dk_h, dv_h = cross_b(
        high_rows, True, s2_h, g3_h, part4_h, other4_h, q2_h, out2_h, lse2_h, []
    )
    other5_h = swap_mp(part5_h)
    g2_l, low2_l, lq2_l, part5_l, sum2_l, lk2, lv2 = cross_b(
        low_rows, False, s2_l, g3_l, part4_l, other4_l, q2_l, out2_l, lse2_l, [dk_h, dv_h]
    )
    other5_l = swap_mp(part5_l)

    which = lax.axis_index("mp").astype(jnp.int32).reshape(1)
    half_width = model // 2
    (frames_part,) = call(
        frames_sent, [shaped((real, half_width), F32)], [which, lk2, lv2, w2kv], 4 * real * own * half_width,
        in_specs=[SMEM] + [VMEM] * 3, name="frames_sent",
    )
    frames_other = swap_mp(frames_part)

    def self_b(rows, first, s1, g2, mine, other, out1, lse1, earlier):
        outs = [sized(rows, model), sized(rows, model, BF), shaped((3, count(rows), own), BF), sized(rows, model),
                shaped((8, model), F32)]
        if first:
            outs += [shaped((cut, own), F32)] * 2
        keys = rows.stop
        return call(
            partial(self_back, rows, first, cut),
            outs,
            [s1, g2, mine, other, gains, self_output_weight, q1, out1, lse1, k1, v1, w3, lengths] + earlier,
            8 * count(rows) * model * own + 24 * count(rows) * keys * own,
            in_specs=[VMEM] * 12 + [SMEM] + [VMEM] * len(earlier),
            scratch=[pltpu.VMEM((count(rows), own), BF), pltpu.VMEM((count(rows), own), F32),
                     pltpu.VMEM((keys, own), F32), pltpu.VMEM((keys, own), F32)],
            name="self_back",
        )

    g1_h, low1_h, l3_h, part6_h, sum1_h, dk1, dv1 = self_b(
        high_rows, True, s1_h, g2_h, part5_h, other5_h, out1_h, lse1_h, []
    )
    other6_h = swap_mp(part6_h)
    g1_l, low1_l, l3_l, part6_l, sum1_l = self_b(
        low_rows, False, s1_l, g2_l, part5_l, other5_l, out1_l, lse1_l, [dk1, dv1]
    )
    other6_l = swap_mp(part6_l)

    cross_all = halving(
        order,
        [
            ((low2_h, low2_l), (mix2_h, mix2_l), 1),
            ((x2_h, x2_l), (lq2_h, lq2_l), 1),
            ((frames,), (lk2[:real],), 1),
            ((frames,), (lv2[:real],), 1),
        ],
        dp_size,
        "cross",
    )
    self_all = halving(
        order,
        [
            ((low1_h, low1_l), (mix1_h, mix1_l), 1),
            ((x1[cut:], x1[:cut]), (l3_h, l3_l), 3),
        ],
        dp_size,
        "self",
    )
    (frames_grad,) = call(
        frames_kept, [shaped((real, half_width), F32)], [which, lk2, lv2, w2kv, frames_other],
        4 * real * own * half_width, in_specs=[SMEM] + [VMEM] * 4, name="frames_kept",
    )
    tokens_grad, sum0 = call(
        partial(tokens_end, cut),
        [shaped((slot, model), F32), shaped((8, model), F32)],
        [tok, gains, g1_l, g1_h, part6_l, other6_l, part6_h, other6_h],
        40 * slot * model,
        name="tokens_end",
    )
    sum1, sum2, sum3 = sum1_h + sum1_l, sum2_h + sum2_l, sum3_h + sum3_l
    cross_row = jnp.concatenate([sum2[3:4, :own], sum2_l[3:4, own:]], axis=1)
    total = jnp.concatenate(
        [
            sum0[0:1], sum1[0:1], sum2[0:1], sum3[0:1],
            sum0[1:2], sum1[1:2], sum2[1:2], sum3[1:2],
            sum1[2:3], sum2[2:3], sum3[2:3],
            sum1[3:4], cross_row,
            (hsum_h + hsum_l)[0:1].reshape(ff // model, model),
        ],
        axis=0,
    )
    bit = 1
    while bit < dp_size:
        total = total + swap_dp(total, bit, dp_size)
        bit *= 2
    shard = model // dp_size
    return (
        jnp.concatenate([y_l, y_h], axis=0)[None],
        tokens_grad[None],
        frames_grad[None],
        self_all[:, own:].reshape(shard, 3, own),
        total[11].reshape(2, own),
        self_all[:, :own].T,
        cross_all[:, own : 2 * own],
        cross_all[:, 2 * own :].reshape(shard, 2, own),
        total[12].reshape(2, own),
        cross_all[:, :own].T,
        fc1_grad,
        total[13:].reshape(ff),
        second_turned.T,
        total[8:11],
        total[0:4],
        total[4:8],
    )


def solution(mesh):
    in_specs = (
        P("dp", None, None),
        P("dp", None, None),
        P("dp"),
        P("dp", None, None),
        P(None, None, "mp"),
        P(None, "mp"),
        P("mp", None),
        P(None, "mp"),
        P(None, None, "mp"),
        P(None, "mp"),
        P("mp", None),
        P(None, "mp"),
        P("mp"),
        P("mp", None),
        P(),
        P(),
        P(),
    )
    out_specs = (
        P("dp", None, None),
        P("dp", None, None),
        P("dp", None, "mp"),
        P("dp", None, "mp"),
        P(None, "mp"),
        P("mp", "dp"),
        P("dp", "mp"),
        P("dp", None, "mp"),
        P(None, "mp"),
        P("mp", "dp"),
        P("dp", "mp"),
        P("mp"),
        P("mp", "dp"),
        P(),
        P(),
        P(),
    )
    return jax.shard_map(
        partial(on_device, mesh.shape["dp"]),
        mesh=mesh,
        in_specs=in_specs,
        out_specs=out_specs,
        check_vma=False,
    )
```

```python
from functools import partial

import jax
import jax.numpy as jnp
from jax import lax
from jax.experimental import pallas as pl
from jax.experimental.pallas import tpu as pltpu
from jax.sharding import PartitionSpec as P

F32 = jnp.float32
BF = jnp.bfloat16
HEAD_DIM = 64
LANES = 128
NEG = -1e30
COST = {"place_query": 1.0, "pair_sent": 4.0, "pair_kept": 3.0, "self_start": 6.0, "self_next": 4.0, "frames_start": 9.0, "place_self": 1.0, "place_cross": 1.0, "cross_start": 8.0,
        "dense_start": 7.0, "dense_back": 8.0, "sent": 3.0, "kept": 3.0, "cross_back": 13.0, "self_back": 8.0, "frames_sent": 5.0,
        "cross_sent": 6.0, "cross_kept": 4.5, "self_sent": 5.0, "self_kept": 4.0, "step": 1.0, "tokens_end": 5.0, "frames_kept": 5.0}
SCALE = 5e9
PINNED = ("h", "t", "r")


def shaped(shape, dtype=F32):
    return jax.ShapeDtypeStruct(tuple(shape), dtype)


def dg(a, b, ca, cb):
    return lax.dot_general(a, b, (((ca,), (cb,)), ((), ())), preferred_element_type=F32)


def nn(a, b):
    return dg(a, b, 1, 0)


def nt(a, b):
    return dg(a, b, 1, 1)


def tn(a, b):
    return dg(a, b, 0, 0)


class Feed:
    def __init__(self, source, target, sem):
        self.copy = pltpu.make_async_copy(source, target, sem)
        self.copy.start()
        self.target = target
        self.pending = True

    def ready(self):
        if self.pending:
            self.copy.wait()
            self.pending = False
        return self.target


class Drain:
    def __init__(self, source, target, sem):
        self.ref = source
        self.copy = pltpu.make_async_copy(source, target, sem)
        self.pending = True

    def flush(self):
        if self.pending:
            self.copy.start()
            self.pending = False


def use(*inputs):
    made = [i.ready() if isinstance(i, Feed) else i for i in inputs]
    return made if len(made) > 1 else made[0]


def flush(*outputs):
    for o in outputs:
        if isinstance(o, Drain):
            o.flush()


def into(*outputs):
    made = [o.ref if isinstance(o, Drain) else o for o in outputs]
    return made if len(made) > 1 else made[0]


class Chain:
    def __init__(self, seed):
        self.link = seed

    def tie(self, value):
        return lax.optimization_barrier((value, self.link))[0]

    def __call__(self, kernel, outs, args, flops, name, scratch=()):
        place = {
            "v": pl.BlockSpec(memory_space=pltpu.VMEM),
            "h": pl.BlockSpec(memory_space=pltpu.HBM),
            "s": pl.BlockSpec(memory_space=pltpu.SMEM),
        }
        args = [(self.link, "t")] + list(args)
        outs = [(shaped((8, LANES)), "t")] + list(outs)
        held = []
        for item, kind in args[1:] + outs[1:]:
            if kind == "h":
                held.append(pltpu.VMEM(item.shape, item.dtype))
        n_in, n_out = len(args), len(outs)

        def body(*refs):
            ins, results = refs[1:n_in], refs[n_in + 1 : n_in + n_out]
            rest = refs[n_in + n_out :]
            own, bufs, sems = rest[: len(scratch)], list(rest[len(scratch) : -1]), rest[-1]
            at = 0
            feeds, drains = [], []
            for ref, (_, kind) in zip(ins, args[1:]):
                if kind == "h":
                    feeds.append(Feed(ref, bufs[at], sems.at[at]))
                    at += 1
                else:
                    feeds.append(ref)
            for ref, (_, kind) in zip(results, outs[1:]):
                if kind == "h":
                    drains.append(Drain(bufs[at], ref, sems.at[at]))
                    at += 1
                else:
                    drains.append(ref)
            kernel(feeds, drains, own)
            use(*feeds)
            flush(*drains)
            for d in drains:
                if isinstance(d, Drain):
                    d.copy.wait()

        moved = 0
        for item, kind in args + outs:
            size = jnp.dtype(item.dtype).itemsize
            for d in item.shape:
                size *= d
            moved += size
        place["t"] = place["r"] = place["h"]
        made = pl.pallas_call(
            body,
            out_shape=tuple(pltpu.HBM(o.shape, o.dtype) if k in PINNED else o for o, k in outs),
            in_specs=[place[k] for _, k in args],
            out_specs=tuple(place[k] for _, k in outs),
            scratch_shapes=list(scratch) + held + [pltpu.SemaphoreType.DMA((max(1, len(held)),))],
            compiler_params=pltpu.CompilerParams(vmem_limit_bytes=28 * 1024 * 1024),
            cost_estimate=pl.CostEstimate(flops=int(COST.get(name.split("_", 1)[-1] if name.split("_")[0] in ("second", "first") else name, 3.0) * SCALE), transcendentals=0, bytes_accessed=1),
            name=name,
        )(*[pltpu.with_memory_space_constraint(a, pltpu.HBM) if k in PINNED else a for a, k in args])
        self.link = made[0]
        return made[1:]


def standard(stream):
    centred = stream - jnp.mean(stream, axis=1, keepdims=True)
    spread = jnp.mean(centred * centred, axis=1, keepdims=True)
    scale = lax.rsqrt(spread + 1e-05)
    return centred * scale, scale


def norm_back(grad, unit, scale, gain):
    lifted = grad * gain
    mean_plain = jnp.mean(lifted, axis=1, keepdims=True)
    mean_cross = jnp.mean(lifted * unit, axis=1, keepdims=True)
    return scale * (lifted - mean_plain - unit * mean_cross)


def column_sums(values):
    return jnp.sum(values, axis=0, keepdims=True)


def head_lanes(which):
    lane = lax.broadcasted_iota(jnp.int32, (1, LANES), 1)
    return (lane < HEAD_DIM) if which == 0 else (lane >= HEAD_DIM)


def only(mask, values):
    return jnp.where(mask, values, jnp.zeros_like(values))


def pair_slice(pair):
    return pl.ds(pl.multiple_of(pair * LANES, LANES), LANES)


def attend_rows(q_ref, k_ref, v_ref, rows, keys, bias, mixed_ref, send_ref, out_ref, lse_ref):
    lane = lax.broadcasted_iota(jnp.int32, (1, LANES), 1)
    count = rows.stop - rows.start

    def body(pair, lse):
        at = pair_slice(pair)
        k_pair, v_pair, q_pair = k_ref[0:keys, at], v_ref[0:keys, at], q_ref[rows, at]
        result = None
        for which in range(2):
            mask = head_lanes(which)
            scores = nt(only(mask, q_pair), k_pair) + bias
            top = jnp.max(scores, axis=1, keepdims=True)
            raised = jnp.exp(scores - top)
            total = jnp.sum(raised, axis=1, keepdims=True)
            value = nn(raised.astype(BF), v_pair) * (1.0 / total)
            result = value if which == 0 else jnp.where(mask, value, result)
            lse = jnp.where(lane == 2 * pair + which, top + jnp.log(total), lse)
        out_ref[:, at] = result
        rounded = result.astype(BF)
        mixed_ref[:, at] = rounded
        send_ref[:, at] = rounded.astype(F32)
        return lse

    lse = lax.fori_loop(0, q_ref.shape[1] // LANES, body, jnp.zeros((count, LANES), F32))
    lse_ref[...] = lse.T[0 : lse_ref.shape[0]]


def attend_back(q_ref, g_ref, o_ref, lse_ref, k_ref, v_ref, rows, keys, bias, dq_ref, emit):
    def body(pair, carry):
        at = pair_slice(pair)
        k_pair, v_pair = k_ref[0:keys, at], v_ref[0:keys, at]
        q_pair, g_pair = q_ref[rows, at], g_ref[:, at]
        product = (g_pair.astype(F32) * o_ref[:, at]).T
        k_turned = k_pair.T
        parts, grad_k, grad_v = [], None, None
        for which in range(2):
            mask = head_lanes(which)
            q_head, g_head = only(mask, q_pair), only(mask, g_pair)
            inner = column_sums(product[which * HEAD_DIM : (which + 1) * HEAD_DIM])
            scores = nt(k_pair, q_head) + bias
            probs = jnp.exp(scores - lse_ref[pl.ds(2 * pair + which, 1), :])
            grad_probs = nt(v_pair, g_head)
            grad_scores = (probs * (grad_probs - inner)).astype(BF)
            here_v = nn(probs.astype(BF), g_head)
            here_k = nn(grad_scores, q_head)
            grad_v = here_v if which == 0 else grad_v + here_v
            grad_k = here_k if which == 0 else grad_k + here_k
            parts.append(nn(k_turned[which * HEAD_DIM : (which + 1) * HEAD_DIM], grad_scores))
        emit(pair, at, grad_k, grad_v)
        dq_ref[:, at] = jnp.concatenate(parts, axis=0).T
        return carry

    lax.fori_loop(0, q_ref.shape[1] // LANES, body, 0)


def causal_bias(rows, keys, length, turned):
    count = rows.stop - rows.start
    shape = (keys, count) if turned else (count, keys)
    query = lax.broadcasted_iota(jnp.int32, shape, 1 if turned else 0) + rows.start
    key = lax.broadcasted_iota(jnp.int32, shape, 0 if turned else 1)
    return jnp.where((key <= query) & (key < length), 0.0, NEG).astype(F32)


def tail_bias(keys, real, turned):
    shape = (keys, 1) if turned else (1, keys)
    key = lax.broadcasted_iota(jnp.int32, shape, 0 if turned else 1)
    return jnp.where(key < real, 0.0, NEG).astype(F32)


def self_start(rows, ins, outs, scratch):
    tok, gains, shifts, vb, w, length = ins
    x_lo, x_hi, q_o, k_o, v_o, mixed, send, out, lse = outs
    low_ref, high_ref, q_ref, k_ref, v_ref = into(x_lo, x_hi, q_o, k_o, v_o)
    tok, gains, shifts = use(tok, gains, shifts)
    unit, _ = standard(tok[...].astype(F32))
    x = (unit * gains[0:1] + shifts[0:1]).astype(BF)
    low_ref[...] = x[: rows.start]
    high_ref[...] = x[rows.start :]
    vb, w = use(vb, w)
    q_ref[...] = ((nn(x, w[0]) + vb[0:1]) * 0.125).astype(BF)
    k_ref[...] = nn(x, w[1]).astype(BF)
    v_ref[...] = (nn(x, w[2]) + vb[1:2]).astype(BF)
    flush(x_lo, x_hi, q_o, k_o, v_o)
    bias = causal_bias(rows, rows.stop, length[0], False)
    attend_rows(q_ref, k_ref, v_ref, rows, rows.stop, bias, *into(mixed, send, out, lse))


def self_next(rows, ins, outs, scratch):
    q_ref, k_ref, v_ref, length = use(*ins)
    bias = causal_bias(rows, rows.stop, length[0], False)
    attend_rows(q_ref, k_ref, v_ref, rows, rows.stop, bias, *into(*outs))


def frames_start(ins, outs, scratch):
    frames, w, vb, order = ins
    k_o, v_o, t_o = outs
    k_ref, v_ref, t_ref = into(k_o, v_o, t_o)
    real, padded = frames.target.shape[0], k_ref.shape[0]
    low = real // 16 * 16
    for ref in (k_ref, v_ref, t_ref):
        if padded > real:
            ref[low:padded] = jnp.zeros((padded - low, ref.shape[1]), BF)
    frames, w, vb = use(frames, w, vb)
    k_ref[0:real] = nn(frames[...], w[0]).astype(BF)
    flush(k_o)
    v_ref[0:real] = (nn(frames[...], w[1]) + vb[1:2]).astype(BF)
    flush(v_o)
    t_ref[0:real] = nn(frames[...], use(order)[...]).astype(BF)


def assemble(ins, outs, scratch):
    spot, pieces = ins[0], ins[1:]
    out = into(outs[0])
    block = out.shape[0] // len(pieces)
    for j, piece in enumerate(pieces):
        source = use(piece)
        at = pl.multiple_of(((spot[0] & (len(pieces) - 1)) ^ j) * block, 16)
        out[pl.ds(at, block), :] = source[...].astype(BF)


def cross_start(rows, real, ins, outs, scratch):
    mine, other, wo, wo_other, tok, ob, gains, shifts, vb, wq, k_in, v_in = ins
    s_o, x_o, q_o, mixed, send, out, lse = outs
    s_ref, x_ref, q_ref = into(s_o, x_o, q_o)
    mine, wo, wo_other, tok, ob, gains, shifts = use(mine, wo, wo_other, tok, ob, gains, shifts)
    joined = nn(mine[...], wo[...]) + nn(use(other)[...].astype(BF), wo_other[...])
    stream = tok[rows].astype(F32) + joined + ob[0:1]
    s_ref[...] = stream
    flush(s_o)
    unit, _ = standard(stream)
    x = (unit * gains[1:2] + shifts[1:2]).astype(BF)
    x_ref[...] = x
    vb, wq = use(vb, wq)
    q_ref[...] = ((nn(x, wq[...]) + vb[0:1]) * 0.125).astype(BF)
    flush(x_o, q_o)
    k_ref, v_ref = use(k_in, v_in)
    keys = k_ref.shape[0]
    attend_rows(q_ref, k_ref, v_ref, slice(0, x.shape[0]), keys, tail_bias(keys, real, False), *into(mixed, send, out, lse))


def dense_start(ins, outs, scratch):
    mine, other, wo, wo_other, s_in, ob, gains, shifts, fb, w1, w2 = ins
    s_o, x_o, a_o, d_o, part = outs
    s_ref, x_ref, active, slope, part = into(s_o, x_o, a_o, d_o, part)
    mine, wo, wo_other, s_in, ob, gains, shifts = use(mine, wo, wo_other, s_in, ob, gains, shifts)
    joined = nn(mine[...], wo[...]) + nn(use(other)[...].astype(BF), wo_other[...])
    stream = s_in[...] + joined + ob[1:2]
    s_ref[...] = stream
    unit, _ = standard(stream)
    x_ref[...] = (unit * gains[2:3] + shifts[2:3]).astype(BF)
    flush(s_o, x_o)
    fb, w1, w2 = use(fb, w1, w2)
    wide = 3 * LANES

    def body(step, carry):
        at = pl.ds(pl.multiple_of(step * wide, wide), wide)
        hidden = nn(x_ref[...], w1[:, at]) + fb[:, at]
        below = 0.5 + 0.5 * lax.erf(hidden * 0.7071067811865476)
        slope[:, at] = below + hidden * (0.3989422804014327 * jnp.exp(-0.5 * hidden * hidden))
        value = (hidden * below).astype(BF)
        active[:, at] = value
        part[...] += nn(value, w2[at, :])
        return carry

    part[...] = jnp.zeros_like(part)
    lax.fori_loop(0, w1.shape[1] // wide, body, 0)


def dense_back(rows, ins, outs, scratch):
    mine, other, s_in, ob, gains, shifts, cot, length, w2, slope, w1 = ins
    y_o, g_o, low_o, hid_o, part, sums, hid_sums = outs
    out_ref, g_ref, low_ref, hid_ref, part, sums, hid_sums = into(*outs)
    mine, other, s_in, ob, gains, shifts = use(mine, other, s_in, ob, gains, shifts)
    stream = s_in[...] + (mine[...] + other[...]) + ob[2:3]
    unit, scale = standard(stream)
    row = lax.broadcasted_iota(jnp.int32, (stream.shape[0], 1), 0) + rows.start
    valid = (row < length[0]).astype(F32)
    out_ref[...] = ((unit * gains[3:4] + shifts[3:4]) * valid).astype(BF)
    incoming = use(cot)[rows].astype(F32) * valid
    grad = norm_back(incoming, unit, scale, gains[3:4])
    g_ref[...] = grad
    low_ref[...] = grad.astype(BF)
    flush(y_o, g_o, low_o)
    sums[0:1] = column_sums(incoming * unit)
    sums[1:2] = column_sums(incoming)
    sums[2:3] = column_sums(grad)
    w2, slope, w1 = use(w2, slope, w1)
    wide = 3 * LANES

    def body(step, carry):
        at = pl.ds(pl.multiple_of(step * wide, wide), wide)
        low = (slope[:, at] * nt(low_ref[...], w2[at, :])).astype(BF)
        hid_ref[:, at] = low
        hid_sums[0:1, at] = column_sums(low.astype(F32))
        part[...] += nt(low, w1[:, at])
        return carry

    part[...] = jnp.zeros_like(part)
    lax.fori_loop(0, w1.shape[1] // wide, body, 0)


def back_head(ins, outs, level):
    incoming, s_in, g_in, gains, wo = ins
    g_o, low_o, sums, gm = outs
    g_ref, low_ref, sums = into(g_o, low_o, sums)
    s_in, g_in, gains = use(s_in, g_in, gains)
    unit, scale = standard(s_in[...])
    grad = g_in[...] + norm_back(incoming, unit, scale, gains[level : level + 1])
    g_ref[...] = grad
    low = grad.astype(BF)
    low_ref[...] = low
    flush(g_o, low_o)
    sums[0:1] = column_sums(incoming * unit)
    sums[1:2] = column_sums(incoming)
    sums[2:3] = column_sums(grad)
    gm[...] = nt(low, use(wo)[...]).astype(BF)


def cross_back(first, real, ins, outs, scratch):
    mine, other, s_in, g_in, gains, wo, q_in, out_in, lse, k_in, v_in = ins[:11]
    g_o, low_o, lq_o, part, sums, dk_o, dv_o = outs
    gm, dq = scratch[:2]
    back_head((use(mine)[...] + use(other)[...], s_in, g_in, gains, wo), (g_o, low_o, sums, gm), 2)
    lq_ref, part, sums = into(lq_o, part, sums)
    q_ref, out_in, lse, k_ref, v_ref = use(q_in, out_in, lse, k_in, v_in)
    keys, width = k_ref.shape
    before = [use(i) for i in ins[11:]]
    if first:
        held_k, held_v, sems = scratch[2:]

        def moves(pair, at):
            return (
                pltpu.make_async_copy(held_k.at[:, at], dk_o.at[:, at], sems.at[0, pair]),
                pltpu.make_async_copy(held_v.at[:, at], dv_o.at[:, at], sems.at[1, pair]),
            )
    else:
        dk, dv = into(dk_o, dv_o)

    def emit(pair, at, grad_k, grad_v):
        if first:
            held_k[:, at] = grad_k
            held_v[:, at] = grad_v
            for move in moves(pair, at):
                move.start()
        else:
            dk[:, at] = (grad_k + before[0][:, at]).astype(BF)
            dv[:, at] = (grad_v + before[1][:, at]).astype(BF)

    attend_back(q_ref, gm, out_in, lse, k_ref, v_ref, slice(0, gm.shape[0]), keys, tail_bias(keys, real, True), dq, emit)
    low_q = (dq[...].astype(BF).astype(F32) * 0.125).astype(BF)
    lq_ref[...] = low_q
    part[...] = low_q.astype(F32)
    sums[3:4, 0:width] = column_sums(low_q.astype(F32))
    if first:
        for pair in range(width // LANES):
            for move in moves(pair, slice(pair * LANES, (pair + 1) * LANES)):
                move.wait()
    else:
        flush(dk_o, dv_o, lq_o)
        sums[3:4, width : 2 * width] = column_sums(dv[0:real].astype(F32))


def frames_sent(ins, outs, scratch):
    which, lk, lv, w = use(*ins)
    out = into(outs[0])
    real, width = out.shape
    at = pl.ds(pl.multiple_of((1 - which[0]) * width, width), width)
    out[...] = nt(lk[0:real], w[0, at, :]) + nt(lv[0:real], w[1, at, :])


def frames_kept(ins, outs, scratch):
    which, lk, lv, w, other = use(*ins)
    held, sem = scratch
    real, width = other.shape
    at = pl.ds(pl.multiple_of(which[0] * width, width), width)
    held[...] = nt(lk[0:real], w[0, at, :]) + nt(lv[0:real], w[1, at, :]) + other[...]
    copy = pltpu.make_async_copy(held, outs[0].at[:, 0, :], sem)
    copy.start()
    copy.wait()


def self_back(rows, first, keep, ins, outs, scratch):
    mine, other, wq, wq_other, s_in, g_in, gains, wo, q_in, out_in, lse, k_in, v_in, w, length = ins[:15]
    g_o, low_o, l3_o, part, sums = outs[:5]
    gm, dq = scratch
    mine, other, wq, wq_other = use(mine, other, wq, wq_other)
    incoming = nt(mine[...], wq[...]) + nt(other[...].astype(BF), wq_other[...])
    back_head((incoming, s_in, g_in, gains, wo), (g_o, low_o, sums, gm), 1)
    l3_ref, part, sums = into(l3_o, part, sums)
    q_ref, out_in, lse, k_ref, v_ref, w = use(q_in, out_in, lse, k_in, v_in, w)
    width = k_ref.shape[1]
    before = [use(i) for i in ins[15:]]

    def emit(pair, at, grad_k, grad_v):
        for slot, grad in ((1, grad_k), (2, grad_v)):
            if first:
                into(outs[4 + slot])[:, at] = grad[:keep]
                l3_ref[slot, :, at] = grad[keep:].astype(BF)
            else:
                l3_ref[slot, :, at] = (grad + before[slot - 1][:, at]).astype(BF)

    bias = causal_bias(rows, rows.stop, length[0], True)
    attend_back(q_ref, gm, out_in, lse, k_ref, v_ref, rows, rows.stop, bias, dq, emit)
    l3_ref[0] = (dq[...].astype(BF).astype(F32) * 0.125).astype(BF)
    flush(l3_o)
    part[...] = nt(l3_ref[0], w[0]) + nt(l3_ref[1], w[1]) + nt(l3_ref[2], w[2])
    sums[3:4, 0:width] = column_sums(l3_ref[0].astype(F32))
    sums[3:4, width : 2 * width] = column_sums(l3_ref[2].astype(F32))


def tokens_end(cut, ins, outs, scratch):
    tok, gains, g_low, g_high, mine_low, other_low, mine_high, other_high = use(*ins)
    out, sums = into(*outs)
    total = None
    for rows, g, mine, other in (
        (slice(0, cut), g_low, mine_low, other_low),
        (slice(cut, tok.shape[0]), g_high, mine_high, other_high),
    ):
        unit, scale = standard(tok[rows].astype(F32))
        incoming = mine[...] + other[...]
        out[rows] = g[...] + norm_back(incoming, unit, scale, gains[0:1])
        here = (column_sums(incoming * unit), column_sums(incoming))
        total = here if total is None else (total[0] + here[0], total[1] + here[1])
    sums[0:1] = total[0]
    sums[1:2] = total[1]


def grads_sent(layout, ins, outs, scratch):
    order, at = ins[0], 1
    out, turned = into(outs[0]), list(outs[1:])
    half, col = out.shape[0], 0
    for parts, ordered, blocks in layout:
        lefts = ins[at : at + parts]
        at += parts
        if ordered:
            lefts = use(*lefts) if parts > 1 else [use(*lefts)]
        else:
            made = []
            for left in lefts:
                target = turned.pop(0)
                ref = into(target)
                left, order = use(left, order)
                ref[...] = nn(left[...], order[...]).astype(BF)
                flush(target)
                made.append(ref)
            lefts = made
        for block in blocks:
            total, width = None, 0
            for part in range(parts):
                right = use(ins[at + part])
                value = right[block] if len(right.shape) == 3 else right[...]
                width = value.shape[-1]
                term = tn(lefts[part][:, half:], value)
                total = term if total is None else total + term
            out[:, col : col + width] = total
            col += width
        at += parts


def grads_kept(layout, ins, outs, scratch):
    other, at, col = use(ins[0]), 1, 0
    sent, kept = into(*outs)
    half, low = other.shape[0], kept.shape[0]
    for parts, ordered, blocks in layout:
        lefts = [use(i) for i in ins[at : at + parts]]
        at += parts
        for block in blocks:
            total = None
            for part in range(parts):
                right = use(ins[at + part])
                value = right[block] if len(right.shape) == 3 else right[...]
                width = value.shape[-1]
                term = tn(lefts[part][:, :half], value)
                total = term if total is None else total + term
            total = total + other[:, col : col + width]
            sent[:, col : col + width] = total[low:]
            kept[:, col : col + width] = total[:low]
            col += width
        at += parts


def halve(ins, outs, scratch):
    kept, other = use(*ins)
    sent, out = into(*outs)
    low = out.shape[0]
    out[...] = kept[0:low] + other[0:low]
    sent[...] = kept[low:] + other[low:]


def swap_mp(v):
    return lax.ppermute(v, "mp", [(0, 1), (1, 0)])


def swap_dp(v, bit, dp_size):
    return lax.ppermute(v, "dp", [(i, i ^ bit) for i in range(dp_size)])


def relative_order(width, bits):
    shard = width // (1 << len(bits))
    me = lax.axis_index("dp")
    place = jnp.arange(width, dtype=jnp.int32)
    block = place // shard
    owner = jnp.zeros_like(block)
    for step, bit in enumerate(bits):
        owner = owner + ((block >> (len(bits) - 1 - step)) & 1) * bit
    source = (owner ^ me) * shard + place % shard
    rows = jnp.arange(width, dtype=jnp.int32)
    return (rows[:, None] == source[None, :]).astype(BF)


class Halving:
    def __init__(self, chain, order, bits, groups, dp_size, name):
        self.chain, self.groups, self.dp_size, self.name = chain, groups, dp_size, name
        self.bits = list(bits)
        self.layout = tuple((len(lhs), ordered, blocks) for lhs, ordered, rhs, blocks in groups)
        self.model = order.shape[0]
        self.columns = sum(rhs[0].shape[-1] * len(blocks) for lhs, ordered, rhs, blocks in groups)
        args = [(order, "h")]
        outs = [(shaped((self.model // 2, self.columns)), "v")]
        for lhs, ordered, rhs, blocks in groups:
            args += [(p, "h") for p in lhs] + [(p, "h") for p in rhs]
            if not ordered:
                outs += [(shaped(p.shape, BF), "h") for p in lhs]
        made = chain(partial(grads_sent, self.layout), outs, args, 0, name + "_sent")
        self.turned = list(made[1:])
        self.swap(made[0])

    def swap(self, sent):
        self.other = swap_dp(sent, self.bits.pop(0), self.dp_size)

    def keep(self):
        args = [(self.other, "v")]
        turned = list(self.turned)
        for lhs, ordered, rhs, blocks in self.groups:
            for p in lhs:
                args.append((p if ordered else turned.pop(0), "h"))
            args += [(p, "h") for p in rhs]
        half = shaped((self.model // 4, self.columns))
        sent, self.kept = self.chain(
            partial(grads_kept, self.layout), [(half, "v"), (half, "v")], args, 0, self.name + "_kept"
        )
        self.swap(sent)

    def step(self):
        half = shaped((self.kept.shape[0] // 2, self.columns))
        sent, self.kept = self.chain(
            halve, [(half, "v"), (half, "v")], [(self.kept, "v"), (self.other, "v")], 0, self.name + "_step"
        )
        self.swap(sent)

    def end(self):
        while self.bits:
            self.step()
        return self.kept + self.other


def on_device(
    dp_size,
    tokens,
    frames,
    lengths,
    out_cot,
    self_query_key_value,
    self_qv_bias,
    self_output_weight,
    cross_query_weight,
    cross_kv,
    cross_bias,
    cross_output_weight,
    first_dense_weight,
    first_dense_bias,
    second_dense_weight,
    out_biases,
    norm_gains,
    norm_biases,
):
    _, slot, model = tokens.shape
    tok, frames, cot = tokens[0], frames[0], out_cot[0]
    real = frames.shape[0]
    padded = -(-real // 256) * 256
    own = self_output_weight.shape[0]
    ff = second_dense_weight.shape[0]
    cut = slot // 2 // 64 * 64
    low_rows, high_rows = slice(0, cut), slice(cut, slot)
    w3 = self_query_key_value.transpose(1, 0, 2)
    w2kv = cross_kv.transpose(1, 0, 2)
    fb = first_dense_bias[None]
    gains, shifts, ob = norm_gains, norm_biases, out_biases
    bits = [1 << i for i in range(dp_size.bit_length() - 1)]
    turned_bits = bits[:1] + bits[2:] + bits[1:2]
    order, order_turned = relative_order(model, bits), relative_order(model, turned_bits)
    chain = Chain(norm_gains)
    spot = (lax.axis_index("dp") & 3).astype(jnp.int32)
    spots = spot.reshape(1)

    def count(rows):
        return rows.stop - rows.start

    def sized(rows, width, dtype=F32):
        return shaped((count(rows), width), dtype)

    def attended(rows):
        return [(sized(rows, own, BF), "h"), (sized(rows, own), "v"), (sized(rows, own), "h"), (shaped((8, count(rows))), "h")]

    def fetched(weight, parts):
        block = weight.shape[0] // parts
        at = (spot & (parts - 1)) * block
        return swap_mp(chain.tie(lax.dynamic_slice_in_dim(weight, at, block, 0).astype(F32)))

    def passed(piece, bit):
        return swap_dp(chain.tie(piece), bit, dp_size)

    def placed(pieces, name):
        rows, columns = pieces[0].shape
        (full,) = chain(
            assemble,
            [(shaped((rows * len(pieces), columns), BF), "h")],
            [(spots, "s")] + [(p, "v") for p in pieces],
            0,
            name,
        )
        return full

    x1_l, x1_h, q1, k1, v1, mix1_h, send1_h, out1_h, lse1_h = chain(
        partial(self_start, high_rows),
        [(sized(low_rows, model, BF), "h"), (sized(high_rows, model, BF), "h")] + [(shaped((slot, own), BF), "h")] * 3 + attended(high_rows),
        [(tok, "h"), (gains, "h"), (shifts, "h"), (self_qv_bias, "h"), (w3, "h"), (lengths, "s")],
        2 * slot * model * own * 3 + 8 * count(high_rows) * slot * own,
        "self_start",
    )
    other1_h = swap_mp(send1_h)
    wo1_0 = fetched(self_output_weight, 4)
    mix1_l, send1_l, out1_l, lse1_l = chain(
        partial(self_next, low_rows),
        attended(low_rows),
        [(q1, "h"), (k1, "h"), (v1, "h"), (lengths, "s")],
        8 * count(low_rows) * cut * own,
        "self_next",
    )
    other1_l = swap_mp(send1_l)
    wo2_0 = fetched(cross_output_weight, 4)
    wo1_2 = passed(wo1_0, 2)
    k2, v2, turned_frames = chain(
        frames_start,
        [(shaped((padded, own), BF), "h")] * 2 + [(shaped((padded, model), BF), "h")],
        [(frames, "h"), (w2kv, "h"), (cross_bias, "h"), (order, "h")],
        4 * real * model * own + 2 * real * model * model,
        "frames_start",
    )
    wo1_1, wo1_3 = passed(wo1_0, 1), passed(wo1_2, 1)
    wq_0 = fetched(cross_query_weight, 2)
    wo2_2 = passed(wo2_0, 2)
    wo1_other = placed([wo1_0, wo1_1, wo1_2, wo1_3], "place_self")

    def cross(rows, mine, other):
        return chain(
            partial(cross_start, rows, real),
            [(sized(rows, model), "h"), (sized(rows, model, BF), "h"), (sized(rows, own, BF), "h")] + attended(rows),
            [(mine, "h"), (other, "v"), (self_output_weight, "h"), (wo1_other, "h"), (tok, "h"), (ob, "h"), (gains, "h"),
             (shifts, "h"), (cross_bias, "h"), (cross_query_weight, "h"), (k2, "h"), (v2, "h")],
            6 * count(rows) * model * own + 8 * count(rows) * padded * own,
            "cross_start",
        )

    s1_h, x2_h, q2_h, mix2_h, send2_h, out2_h, lse2_h = cross(high_rows, mix1_h, other1_h)
    other2_h = swap_mp(send2_h)
    wo2_1, wo2_3 = passed(wo2_0, 1), passed(wo2_2, 1)
    wq_1 = passed(wq_0, 1)
    s1_l, x2_l, q2_l, mix2_l, send2_l, out2_l, lse2_l = cross(low_rows, mix1_l, other1_l)
    other2_l = swap_mp(send2_l)
    wo2_other = placed([wo2_0, wo2_1, wo2_2, wo2_3], "place_cross")
    wq_other = placed([wq_0, wq_1], "place_query")

    def dense(rows, s1, mine, other):
        return chain(
            dense_start,
            [(sized(rows, model), "h"), (sized(rows, model, BF), "h"), (sized(rows, ff, BF), "h"), (sized(rows, ff), "h"),
             (sized(rows, model), "v")],
            [(mine, "h"), (other, "v"), (cross_output_weight, "h"), (wo2_other, "h"), (s1, "h"), (ob, "h"), (gains, "h"),
             (shifts, "h"), (fb, "h"), (first_dense_weight, "h"), (second_dense_weight, "h")],
            8 * count(rows) * model * ff,
            "dense_start",
        )

    s2_h, x3_h, act_h, slope_h, part3_h = dense(high_rows, s1_h, mix2_h, other2_h)
    other3_h = swap_mp(part3_h)
    s2_l, x3_l, act_l, slope_l, part3_l = dense(low_rows, s1_l, mix2_l, other2_l)
    other3_l = swap_mp(part3_l)

    def dense_b(rows, s2, mine, other, slope):
        return chain(
            partial(dense_back, rows),
            [(sized(rows, model, BF), "h"), (sized(rows, model), "h"), (sized(rows, model, BF), "h"),
             (sized(rows, ff, BF), "h"), (sized(rows, model), "v"), (shaped((8, model)), "v"), (shaped((8, ff)), "v")],
            [(mine, "v"), (other, "v"), (s2, "h"), (ob, "h"), (gains, "h"), (shifts, "h"), (cot, "h"), (lengths, "s"),
             (second_dense_weight, "h"), (slope, "h"), (first_dense_weight, "h")],
            6 * count(rows) * model * ff,
            "dense_back",
        )

    y_h, g3_h, low3_h, hid_h, part4_h, sum3_h, hsum_h = dense_b(high_rows, s2_h, part3_h, other3_h, slope_h)
    other4_h = swap_mp(part4_h)
    y_l, g3_l, low3_l, hid_l, part4_l, sum3_l, hsum_l = dense_b(low_rows, s2_l, part3_l, other3_l, slope_l)
    other4_l = swap_mp(part4_l)

    second = Halving(chain, order, bits, [((low3_h, low3_l), False, (act_h, act_l), (0,))], dp_size, "second")
    first = Halving(chain, order_turned, turned_bits, [((x3_h, x3_l), False, (hid_h, hid_l), (0,))], dp_size, "first")
    second.keep()
    first.keep()

    def cross_b(rows, early, s2, g3, mine, other, q2, out2, lse2, before):
        wide = [(shaped((padded, own)), "r")] * 2 if early else [(shaped((padded, own), BF), "h")] * 2
        scratch = [pltpu.VMEM((count(rows), own), BF), pltpu.VMEM((count(rows), own), F32)]
        if early:
            scratch += [pltpu.VMEM((padded, own), F32)] * 2 + [pltpu.SemaphoreType.DMA((2, own // LANES))]
        return chain(
            partial(cross_back, early, real),
            [(sized(rows, model), "h"), (sized(rows, model, BF), "h"), (sized(rows, own, BF), "h"), (sized(rows, own), "v"),
             (shaped((8, model)), "v")] + wide,
            [(mine, "v"), (other, "v"), (s2, "h"), (g3, "h"), (gains, "h"), (cross_output_weight, "h"), (q2, "h"), (out2, "h"),
             (lse2, "h"), (k2, "h"), (v2, "h")] + before,
            4 * count(rows) * model * own + 20 * count(rows) * padded * own,
            "cross_back",
            scratch=scratch,
        )

    g2_h, low2_h, lq2_h, part5_h, sum2_h, dk_h, dv_h = cross_b(
        high_rows, True, s2_h, g3_h, part4_h, other4_h, q2_h, out2_h, lse2_h, []
    )
    other5_h = swap_mp(part5_h)
    g2_l, low2_l, lq2_l, part5_l, sum2_l, lk2, lv2 = cross_b(
        low_rows, False, s2_l, g3_l, part4_l, other4_l, q2_l, out2_l, lse2_l, [(dk_h, "h"), (dv_h, "h")]
    )
    other5_l = swap_mp(part5_l)
    second.step()
    first.step()
    which = lax.axis_index("mp").astype(jnp.int32).reshape(1)
    half_width = model // 2
    (frames_part,) = chain(
        frames_sent, [(shaped((real, half_width)), "v")], [(which, "s"), (lk2, "h"), (lv2, "h"), (w2kv, "h")],
        4 * real * own * half_width, "frames_sent",
    )
    frames_other = swap_mp(frames_part)
    crosses = Halving(
        chain,
        order,
        bits,
        [
            ((low2_h, low2_l), False, (mix2_h, mix2_l), (0,)),
            ((x2_h, x2_l), False, (lq2_h, lq2_l), (0,)),
            ((turned_frames,), True, (lk2,), (0,)),
            ((turned_frames,), True, (lv2,), (0,)),
        ],
        dp_size,
        "cross",
    )

    def self_b(rows, early, s1, g2, mine, other, out1, lse1, before):
        outs = [(sized(rows, model), "h"), (sized(rows, model, BF), "h"), (shaped((3, count(rows), own), BF), "h"),
                (sized(rows, model), "v"), (shaped((8, model)), "v")]
        if early:
            outs += [(shaped((cut, own)), "v")] * 2
        return chain(
            partial(self_back, rows, early, cut),
            outs,
            [(mine, "h"), (other, "v"), (cross_query_weight, "h"), (wq_other, "h"), (s1, "h"), (g2, "h"), (gains, "h"), (self_output_weight, "h"), (q1, "h"), (out1, "h"),
             (lse1, "h"), (k1, "h"), (v1, "h"), (w3, "h"), (lengths, "s")] + before,
            8 * count(rows) * model * own + 20 * count(rows) * rows.stop * own,
            "self_back",
            scratch=[pltpu.VMEM((count(rows), own), BF), pltpu.VMEM((count(rows), own), F32)],
        )

    g1_h, low1_h, l3_h, part6_h, sum1_h, dk1, dv1 = self_b(
        high_rows, True, s1_h, g2_h, lq2_h, other5_h, out1_h, lse1_h, []
    )
    other6_h = swap_mp(part6_h)
    crosses.keep()
    g1_l, low1_l, l3_l, part6_l, sum1_l = self_b(
        low_rows, False, s1_l, g2_l, lq2_l, other5_l, out1_l, lse1_l, [(dk1, "v"), (dv1, "v")]
    )
    other6_l = swap_mp(part6_l)
    lefts = ((x1_h, x1_l), False)
    selves = Halving(
        chain, order, bits, [((low1_h, low1_l), False, (mix1_h, mix1_l), (0,)), lefts + ((l3_h, l3_l), (0,))], dp_size, "self"
    )
    pairs = Halving(chain, order_turned, turned_bits, [lefts + ((l3_h, l3_l), (1, 2))], dp_size, "pair")
    second.step()
    first.step()
    selves.keep()
    pairs.keep()
    tokens_grad, sum0 = chain(
        partial(tokens_end, cut),
        [(shaped((slot, model)), "h"), (shaped((8, model)), "v")],
        [(tok, "h"), (gains, "h"), (g1_l, "h"), (g1_h, "h"), (part6_l, "v"), (other6_l, "v"), (part6_h, "v"), (other6_h, "v")],
        40 * slot * model,
        "tokens_end",
    )
    crosses.step()
    selves.step()
    pairs.step()
    crosses.step()
    selves.step()
    pairs.step()
    (frames_grad,) = chain(
        frames_kept, [(shaped((real, 1, half_width)), "r")],
        [(which, "s"), (lk2, "h"), (lv2, "h"), (w2kv, "h"), (frames_other, "v")],
        4 * real * own * half_width, "frames_kept",
        scratch=[pltpu.VMEM((real, half_width), F32), pltpu.SemaphoreType.DMA],
    )
    second_turned, first_grad = second.end(), first.end()
    cross_all, self_all, pair_all = crosses.end(), selves.end(), pairs.end()
    sum1, sum2, sum3 = sum1_h + sum1_l, sum2_h + sum2_l, sum3_h + sum3_l
    cross_row = jnp.concatenate([sum2[3:4, :own], sum2_l[3:4, own:]], axis=1)
    total = jnp.concatenate(
        [
            sum0[0:1], sum1[0:1], sum2[0:1], sum3[0:1],
            sum0[1:2], sum1[1:2], sum2[1:2], sum3[1:2],
            sum1[2:3], sum2[2:3], sum3[2:3],
            sum1[3:4], cross_row,
            (hsum_h + hsum_l)[0:1].reshape(ff // model, model),
        ],
        axis=0,
    )
    bit = 1
    while bit < dp_size:
        total = total + swap_dp(total, bit, dp_size)
        bit *= 2
    shard = model // dp_size
    return (
        jnp.concatenate([y_l, y_h], axis=0)[None],
        tokens_grad[None],
        frames_grad.transpose(1, 0, 2),
        jnp.stack([self_all[:, own:], pair_all[:, :own], pair_all[:, own:]], axis=1),
        total[11].reshape(2, own),
        self_all[:, :own].T,
        cross_all[:, own : 2 * own],
        cross_all[:, 2 * own :].reshape(shard, 2, own),
        total[12].reshape(2, own),
        cross_all[:, :own].T,
        first_grad,
        total[13:].reshape(ff),
        second_turned.T,
        total[8:11],
        total[0:4],
        total[4:8],
    )


def solution(mesh):
    in_specs = (
        P("dp", None, None),
        P("dp", None, None),
        P("dp"),
        P("dp", None, None),
        P(None, None, "mp"),
        P(None, "mp"),
        P("mp", None),
        P(None, "mp"),
        P(None, None, "mp"),
        P(None, "mp"),
        P("mp", None),
        P(None, "mp"),
        P("mp"),
        P("mp", None),
        P(),
        P(),
        P(),
    )
    out_specs = (
        P("dp", None, None),
        P("dp", None, None),
        P("dp", None, "mp"),
        P("dp", None, "mp"),
        P(None, "mp"),
        P("mp", "dp"),
        P("dp", "mp"),
        P("dp", None, "mp"),
        P(None, "mp"),
        P("mp", "dp"),
        P("dp", "mp"),
        P("mp"),
        P("mp", "dp"),
        P(),
        P(),
        P(),
    )
    return jax.shard_map(
        partial(on_device, mesh.shape["dp"]),
        mesh=mesh,
        in_specs=in_specs,
        out_specs=out_specs,
        check_vma=False,
    )
```

```python
from functools import partial

import jax
import jax.numpy as jnp
from jax import lax
from jax.experimental import pallas as pl
from jax.experimental.pallas import tpu as pltpu
from jax.sharding import PartitionSpec as P

F32 = jnp.float32
BF = jnp.bfloat16
HEAD_DIM = 64
LANES = 128
NEG = -1e30
COST = {"self_start": 6.0, "self_next": 4.0, "turn": 2.5, "frames_start": 9.0, "cross_start": 8.0, "dense_start": 7.0, "dense_back": 7.0, "dense_sent": 8.0,
        "dense_kept": 6.0, "cross_back": 12.0, "self_back": 8.0, "frames_sent": 4.0, "cross_sent": 6.0, "cross_kept": 5.0,
        "self_sent": 7.0, "self_kept": 4.0, "tokens_end": 5.0, "frames_kept": 6.0, "small_end": 1.0, "pause": 8.0}
SCALE = 1.5e10
PIECES = 4
BACK_BLOCKS = 2
BYTES = 6.4e-3
PINNED = ("h", "t", "r")


def shaped(shape, dtype=F32):
    return jax.ShapeDtypeStruct(tuple(shape), dtype)


def dg(a, b, ca, cb):
    return lax.dot_general(a, b, (((ca,), (cb,)), ((), ())), preferred_element_type=F32)


def nn(a, b):
    return dg(a, b, 1, 0)


def nt(a, b):
    return dg(a, b, 1, 1)


def tn(a, b):
    return dg(a, b, 0, 0)


class Feed:
    def __init__(self, source, target, sem):
        self.copy = pltpu.make_async_copy(source, target, sem)
        self.copy.start()
        self.target = target
        self.pending = True

    def ready(self):
        if self.pending:
            self.copy.wait()
            self.pending = False
        return self.target


class Drain:
    def __init__(self, source, target, sem):
        self.ref = source
        self.copy = pltpu.make_async_copy(source, target, sem)
        self.pending = True

    def flush(self):
        if self.pending:
            self.copy.start()
            self.pending = False


def use(*inputs):
    made = [i.ready() if isinstance(i, Feed) else i for i in inputs]
    return made if len(made) > 1 else made[0]


def flush(*outputs):
    for o in outputs:
        if isinstance(o, Drain):
            o.flush()


def into(*outputs):
    made = [o.ref if isinstance(o, Drain) else o for o in outputs]
    return made if len(made) > 1 else made[0]


class Pending:
    def __init__(self, make):
        self.make, self.value = make, None


class Chain:
    def __init__(self, seed):
        self.link = seed
        self.pending = []

    def pause(self, *after):
        self(lambda ins, outs, scratch: None, [], [], 0, "pause", after=after)

    def later(self, make):
        self.pending.append(Pending(make))
        return self.pending[-1]

    def settle(self):
        for item in reversed(self.pending):
            item.value = item.make()
        self.pending = []

    def swap_mp(self, v):
        return self.later(lambda: swap_mp(v))

    def swap_dp(self, v, bit, dp_size):
        return self.later(lambda: swap_dp(v, bit, dp_size))

    def tie(self, value):
        return lax.optimization_barrier((value, self.link))[0]

    def __call__(self, kernel, outs, args, flops, name, scratch=(), after=()):
        place = {
            "v": pl.BlockSpec(memory_space=pltpu.VMEM),
            "h": pl.BlockSpec(memory_space=pltpu.HBM),
            "s": pl.BlockSpec(memory_space=pltpu.SMEM),
        }
        args = [(self.link, "t")] + [(a, "t") for a in after] + list(args)
        first = 1 + len(after)
        if any(isinstance(a, Pending) and a.value is None for a, _ in args):
            self.settle()
        args = [(a.value if isinstance(a, Pending) else a, k) for a, k in args]
        outs = [(shaped((8, LANES)), "t")] + list(outs)
        held = []
        for item, kind in args[first:] + outs[1:]:
            if kind == "h":
                held.append(pltpu.VMEM(item.shape, item.dtype))
        n_in, n_out = len(args), len(outs)

        def body(*refs):
            ins, results = refs[first:n_in], refs[n_in + 1 : n_in + n_out]
            rest = refs[n_in + n_out :]
            own, bufs, sems = rest[: len(scratch)], list(rest[len(scratch) : -1]), rest[-1]
            at = 0
            feeds, drains = [], []
            for ref, (_, kind) in zip(ins, args[first:]):
                if kind == "h":
                    feeds.append(Feed(ref, bufs[at], sems.at[at]))
                    at += 1
                else:
                    feeds.append(ref)
            for ref, (_, kind) in zip(results, outs[1:]):
                if kind == "h":
                    drains.append(Drain(bufs[at], ref, sems.at[at]))
                    at += 1
                else:
                    drains.append(ref)
            kernel(feeds, drains, own)
            for feed in feeds:
                use(feed)
            flush(*drains)
            for d in drains:
                if isinstance(d, Drain):
                    d.copy.wait()

        moved = 0
        for item, kind in args + outs:
            size = jnp.dtype(item.dtype).itemsize
            for d in item.shape:
                size *= d
            moved += size
        place["t"] = place["r"] = place["h"]
        made = pl.pallas_call(
            body,
            out_shape=tuple(pltpu.HBM(o.shape, o.dtype) if k in PINNED else o for o, k in outs),
            in_specs=[place[k] for _, k in args],
            out_specs=tuple(place[k] for _, k in outs),
            scratch_shapes=list(scratch) + held + [pltpu.SemaphoreType.DMA((max(1, len(held)),))],
            compiler_params=pltpu.CompilerParams(vmem_limit_bytes=28 * 1024 * 1024),
            cost_estimate=pl.CostEstimate(flops=int(COST.get(name, 1.0) * SCALE), transcendentals=0, bytes_accessed=int(COST.get(name, 1.0) * SCALE * BYTES)),
            name=name,
        )(*[pltpu.with_memory_space_constraint(a, pltpu.HBM) if k in PINNED else a for a, k in args])
        self.link = made[0]
        return made[1:]


def standard(stream):
    centred = stream - jnp.mean(stream, axis=1, keepdims=True)
    spread = jnp.mean(centred * centred, axis=1, keepdims=True)
    scale = lax.rsqrt(spread + 1e-05)
    return centred * scale, scale


def norm_back(grad, unit, scale, gain):
    lifted = grad * gain
    mean_plain = jnp.mean(lifted, axis=1, keepdims=True)
    mean_cross = jnp.mean(lifted * unit, axis=1, keepdims=True)
    return scale * (lifted - mean_plain - unit * mean_cross)


def column_sums(values):
    return jnp.sum(values, axis=0, keepdims=True)


def head_lanes(which):
    lane = lax.broadcasted_iota(jnp.int32, (1, LANES), 1)
    return (lane < HEAD_DIM) if which == 0 else (lane >= HEAD_DIM)


def only(mask, values):
    return jnp.where(mask, values, jnp.zeros_like(values))


def pair_slice(pair):
    return pl.ds(pl.multiple_of(pair * LANES, LANES), LANES)


def attend_rows(q_ref, k_ref, v_ref, rows, keys, bias, mixed_ref, out_ref, lse_ref):
    lane = lax.broadcasted_iota(jnp.int32, (1, LANES), 1)
    count = rows.stop - rows.start

    def body(pair, lse):
        at = pair_slice(pair)
        k_pair, v_pair, q_pair = k_ref[0:keys, at], v_ref[0:keys, at], q_ref[rows, at]
        result = None
        for which in range(2):
            mask = head_lanes(which)
            scores = nt(only(mask, q_pair), k_pair) + bias
            top = jnp.max(scores, axis=1, keepdims=True)
            raised = jnp.exp(scores - top)
            total = jnp.sum(raised, axis=1, keepdims=True)
            value = nn(raised.astype(BF), v_pair) * (1.0 / total)
            result = value if which == 0 else jnp.where(mask, value, result)
            lse = jnp.where(lane == 2 * pair + which, top + jnp.log(total), lse)
        out_ref[:, at] = result
        mixed_ref[:, at] = result.astype(BF)
        return lse

    lse = lax.fori_loop(0, q_ref.shape[1] // LANES, body, jnp.zeros((count, LANES), F32))
    lse_ref[...] = lse.T[0 : lse_ref.shape[0]]


def attend_back(q_ref, g_ref, o_ref, lse_ref, k_ref, v_ref, rows, keys, bias, dq_ref, emit, block=None):
    block = keys if block is None else block
    blocks = keys // block

    def body(step, carry):
        pair, part = (step, 0) if blocks == 1 else (step // blocks, step % blocks)
        at = pair_slice(pair)
        here = pl.ds(0, keys) if blocks == 1 else pl.ds(pl.multiple_of(part * block, block), block)
        k_pair, v_pair = k_ref[here, at], v_ref[here, at]
        q_pair, g_pair = q_ref[rows, at], g_ref[:, at]
        product = (g_pair.astype(F32) * o_ref[:, at]).T
        k_turned = k_pair.T
        parts, grad_k, grad_v = [], None, None
        for which in range(2):
            mask = head_lanes(which)
            q_head, g_head = only(mask, q_pair), only(mask, g_pair)
            inner = column_sums(product[which * HEAD_DIM : (which + 1) * HEAD_DIM])
            scores = nt(k_pair, q_head) + bias(part * block)
            probs = jnp.exp(scores - lse_ref[pl.ds(2 * pair + which, 1), :])
            grad_probs = nt(v_pair, g_head)
            grad_scores = (probs * (grad_probs - inner)).astype(BF)
            here_v = nn(probs.astype(BF), g_head)
            here_k = nn(grad_scores, q_head)
            grad_v = here_v if which == 0 else grad_v + here_v
            grad_k = here_k if which == 0 else grad_k + here_k
            parts.append(nn(k_turned[which * HEAD_DIM : (which + 1) * HEAD_DIM], grad_scores))
        emit(pair, part, at, here, grad_k, grad_v)
        grad_q = jnp.concatenate(parts, axis=0).T
        if blocks == 1:
            dq_ref[:, at] = grad_q
        else:
            dq_ref[:, at] += grad_q
        return carry

    if blocks > 1:
        dq_ref[...] = jnp.zeros_like(dq_ref)
    lax.fori_loop(0, q_ref.shape[1] // LANES * blocks, body, 0)


def causal_bias(rows, keys, length, turned):
    count = rows.stop - rows.start
    shape = (keys, count) if turned else (count, keys)
    query = lax.broadcasted_iota(jnp.int32, shape, 1 if turned else 0) + rows.start
    key = lax.broadcasted_iota(jnp.int32, shape, 0 if turned else 1)
    return jnp.where((key <= query) & (key < length), 0.0, NEG).astype(F32)


def tail_bias(keys, real, turned, start=0):
    shape = (keys, 1) if turned else (1, keys)
    key = lax.broadcasted_iota(jnp.int32, shape, 0 if turned else 1) + start
    return jnp.where(key < real, 0.0, NEG).astype(F32)


def self_start(cut, ins, outs, scratch):
    tok, gains, shifts, vb, w, length, wo = ins
    x_lo, x_hi, q_o, k_o, v_o = outs[:5]
    rows = slice(cut, tok.target.shape[0])
    low_ref, high_ref, q_ref, k_ref, v_ref = into(*outs[:5])
    tok, gains, shifts = use(tok, gains, shifts)
    unit, _ = standard(tok[...].astype(F32))
    x = (unit * gains[0:1] + shifts[0:1]).astype(BF)
    low_ref[...] = x[:cut]
    high_ref[...] = x[cut:]
    vb, w = use(vb, w)
    q_ref[...] = ((nn(x, w[0]) + vb[0:1]) * 0.125).astype(BF)
    k_ref[...] = nn(x, w[1]).astype(BF)
    v_ref[...] = (nn(x, w[2]) + vb[1:2]).astype(BF)
    flush(x_lo, x_hi, q_o, k_o, v_o)
    self_rows(rows, q_ref, k_ref, v_ref, length, wo, outs[5:])


def self_next(rows, ins, outs, scratch):
    q_ref, k_ref, v_ref, length, wo = ins
    self_rows(rows, *use(q_ref, k_ref, v_ref), length, wo, outs)


def self_rows(rows, q_ref, k_ref, v_ref, length, wo, outs):
    bias = causal_bias(rows, rows.stop, length[0], False)
    mixed, out, lse, part = into(*outs)
    attend_rows(q_ref, k_ref, v_ref, rows, rows.stop, bias, mixed, out, lse)
    flush(*outs[:3])
    part[...] = nn(mixed[...], use(wo)[...])


def turn(plan, ins, outs, scratch):
    orders = ins[: 1 + max(place for place, _ in plan)]
    parts = ins[len(orders) :]
    for (place, part), out in zip(plan, outs):
        into(out)[...] = nt(use(orders[place])[...], use(parts[part])[...]).astype(BF)
        flush(out)


def frames_start(ins, outs, scratch):
    frames, w, vb, sources = ins
    k_o, v_o, t_o, order_o, other_o = outs
    k_ref, v_ref, t_ref, order, other = into(*outs)
    sources = use(sources)
    column = lax.broadcasted_iota(jnp.int32, order.shape, 1)
    order[...] = jnp.where(column == sources[:, 0:1], 1.0, 0.0).astype(BF)
    other[...] = jnp.where(column == sources[:, 1:2], 1.0, 0.0).astype(BF)
    flush(order_o, other_o)
    real, padded = frames.target.shape[0], k_ref.shape[0]
    low = real // 16 * 16
    if padded > real:
        for ref in (k_ref, v_ref):
            ref[low:padded] = jnp.zeros((padded - low, ref.shape[1]), BF)
        edge = real // LANES * LANES
        t_ref[:, edge:padded] = jnp.zeros((t_ref.shape[0], padded - edge), BF)
    frames, w, vb = use(frames, w, vb)
    k_ref[0:real] = nn(frames[...], w[0]).astype(BF)
    flush(k_o)
    v_ref[0:real] = (nn(frames[...], w[1]) + vb[1:2]).astype(BF)
    flush(v_o)
    t_ref[:, 0:real] = nt(order[...], frames[...]).astype(BF)


def assemble(out, spot, pieces):
    block = out.shape[0] // len(pieces)
    for j, piece in enumerate(pieces):
        at = pl.multiple_of(((spot[0] & (len(pieces) - 1)) ^ j) * block, 16)
        out[pl.ds(at, block), :] = use(piece)[...].astype(BF)


def cross_start(rows, real, ins, outs, scratch):
    mine, other, tok, ob, gains, shifts, vb, wq, k_in, v_in, wo = ins
    s_o, x_o, q_o, m_o, out_o, lse_o, part = outs
    mixed, out, lse, part = into(m_o, out_o, lse_o, part)
    s_ref, x_ref, q_ref = into(s_o, x_o, q_o)
    mine, other, tok, ob, gains, shifts = use(mine, other, tok, ob, gains, shifts)
    stream = tok[rows].astype(F32) + (mine[...] + other[...]) + ob[0:1]
    s_ref[...] = stream
    flush(s_o)
    unit, _ = standard(stream)
    x = (unit * gains[1:2] + shifts[1:2]).astype(BF)
    x_ref[...] = x
    vb, wq = use(vb, wq)
    q_ref[...] = ((nn(x, wq[...]) + vb[0:1]) * 0.125).astype(BF)
    flush(x_o, q_o)
    k_ref, v_ref = use(k_in, v_in)
    keys = k_ref.shape[0]
    attend_rows(q_ref, k_ref, v_ref, slice(0, x.shape[0]), keys, tail_bias(keys, real, False), mixed, out, lse)
    flush(m_o, out_o, lse_o)
    part[...] = nn(mixed[...], use(wo)[...])


def dense_start(ins, outs, scratch):
    mine, other, s_in, ob, gains, shifts, fb, w1, w2 = ins
    s_o, x_o, a_o, d_o, part = outs
    s_ref, x_ref, active, slope, part = into(s_o, x_o, a_o, d_o, part)
    mine, other, s_in, ob, gains, shifts = use(mine, other, s_in, ob, gains, shifts)
    stream = s_in[...] + (mine[...] + other[...]) + ob[1:2]
    s_ref[...] = stream
    unit, _ = standard(stream)
    x_ref[...] = (unit * gains[2:3] + shifts[2:3]).astype(BF)
    flush(s_o, x_o)
    fb, w1, w2 = use(fb, w1, w2)
    wide = 3 * LANES

    def body(step, carry):
        at = pl.ds(pl.multiple_of(step * wide, wide), wide)
        hidden = nn(x_ref[...], w1[:, at]) + fb[:, at]
        below = 0.5 + 0.5 * lax.erf(hidden * 0.7071067811865476)
        slope[:, at] = below + hidden * (0.3989422804014327 * jnp.exp(-0.5 * hidden * hidden))
        value = (hidden * below).astype(BF)
        active[:, at] = value
        part[...] += nn(value, w2[at, :])
        return carry

    part[...] = jnp.zeros_like(part)
    lax.fori_loop(0, w1.shape[1] // wide, body, 0)


def dense_back(rows, ins, outs, scratch):
    mine, other, s_in, ob, gains, shifts, cot, length, w2, slope, w1 = ins
    y_o, g_o, low_o, hid_o, part, sums, hid_sums = outs
    out_ref, g_ref, low_ref, hid_ref, part, sums, hid_sums = into(*outs)
    mine, other, s_in, ob, gains, shifts = use(mine, other, s_in, ob, gains, shifts)
    stream = s_in[...] + (mine[...] + other[...]) + ob[2:3]
    unit, scale = standard(stream)
    row = lax.broadcasted_iota(jnp.int32, (stream.shape[0], 1), 0) + rows.start
    valid = (row < length[0]).astype(F32)
    out_ref[...] = ((unit * gains[3:4] + shifts[3:4]) * valid).astype(BF)
    incoming = use(cot)[rows].astype(F32) * valid
    grad = norm_back(incoming, unit, scale, gains[3:4])
    g_ref[...] = grad
    low_ref[...] = grad.astype(BF)
    flush(y_o, g_o, low_o)
    sums[0:1] = column_sums(incoming * unit)
    sums[1:2] = column_sums(incoming)
    sums[2:3] = column_sums(grad)
    w2, slope, w1 = use(w2, slope, w1)
    wide = 3 * LANES

    def body(step, carry):
        at = pl.ds(pl.multiple_of(step * wide, wide), wide)
        low = (slope[:, at] * nt(low_ref[...], w2[at, :])).astype(BF)
        hid_ref[:, at] = low
        hid_sums[0:1, at] = column_sums(low.astype(F32))
        part[...] += nt(low, w1[:, at])
        return carry

    part[...] = jnp.zeros_like(part)
    lax.fori_loop(0, w1.shape[1] // wide, body, 0)


def back_head(ins, outs, level):
    incoming, s_in, g_in, gains, wo = ins
    g_o, low_o, sums, gm = outs
    g_ref, low_ref, sums = into(g_o, low_o, sums)
    s_in, g_in, gains = use(s_in, g_in, gains)
    unit, scale = standard(s_in[...])
    grad = g_in[...] + norm_back(incoming, unit, scale, gains[level : level + 1])
    g_ref[...] = grad
    low = grad.astype(BF)
    low_ref[...] = low
    flush(g_o, low_o)
    sums[0:1] = column_sums(incoming * unit)
    sums[1:2] = column_sums(incoming)
    sums[2:3] = column_sums(grad)
    gm[...] = nt(low, use(wo)[...]).astype(BF)


def cross_back(first, real, ins, outs, scratch):
    mine, other, s_in, g_in, gains, wo, q_in, out_in, lse, k_in, v_in = ins[:11]
    g_o, low_o, lq_o, part, sums, dk_o, dv_o = outs
    gm, dq = scratch[:2]
    back_head((use(mine)[...] + use(other)[...], s_in, g_in, gains, wo), (g_o, low_o, sums, gm), 2)
    lq_ref, part, sums = into(lq_o, part, sums)
    q_ref, out_in, lse, k_ref, v_ref = use(q_in, out_in, lse, k_in, v_in)
    keys, width = k_ref.shape
    before = [use(i) for i in ins[11:]]
    block = keys // BACK_BLOCKS
    if first:
        held_k, held_v, sems = scratch[2:]

        def moves(pair, part):
            here = pl.ds(part * block, block)
            return (
                pltpu.make_async_copy(held_k.at[pair, here], dk_o.at[pair, here], sems.at[0, pair, part]),
                pltpu.make_async_copy(held_v.at[pair, here], dv_o.at[pair, here], sems.at[1, pair, part]),
            )
    else:
        dk, dv = into(dk_o, dv_o)

    def emit(pair, part, at, here, grad_k, grad_v):
        if first:
            held_k[pair, here] = grad_k
            held_v[pair, here] = grad_v
            for move in moves(pair, part):
                move.start()
        else:
            dk[here, at] = (grad_k + before[0][pair, here]).astype(BF)
            dv[here, at] = (grad_v + before[1][pair, here]).astype(BF)

    attend_back(q_ref, gm, out_in, lse, k_ref, v_ref, slice(0, gm.shape[0]), keys, lambda start: tail_bias(block, real, True, start), dq, emit, block)
    low_q = (dq[...].astype(BF).astype(F32) * 0.125).astype(BF)
    lq_ref[...] = low_q
    part[...] = low_q.astype(F32)
    sums[3:4, 0:width] = column_sums(low_q.astype(F32))
    if first:
        for pair in range(width // LANES):
            for part in range(BACK_BLOCKS):
                for move in moves(pair, part):
                    move.wait()
    else:
        flush(dk_o, dv_o, lq_o)
        sums[3:4, width : 2 * width] = column_sums(dv[0:real].astype(F32))


def frames_sent(ins, outs, scratch):
    which, lk, lv, w = use(*ins)
    start, width = 0, outs[0].ref.shape[1]
    at = pl.ds(pl.multiple_of((1 - which[0]) * width, width), width)
    for drain in outs:
        out = into(drain)
        rows = slice(start, start + out.shape[0])
        out[...] = nt(lk[rows], w[0, at, :]) + nt(lv[rows], w[1, at, :])
        flush(drain)
        start = rows.stop


def frames_kept(ins, outs, scratch):
    which, lk, lv, w = use(*ins[:4])
    held, sem = scratch
    start, width = 0, held.shape[1]
    at = pl.ds(pl.multiple_of(which[0] * width, width), width)
    for other in ins[4:]:
        other = use(other)
        rows = slice(start, start + other.shape[0])
        held[rows] = nt(lk[rows], w[0, at, :]) + nt(lv[rows], w[1, at, :]) + other[...]
        start = rows.stop
    copy = pltpu.make_async_copy(held, outs[0].at[:, 0, :], sem)
    copy.start()
    copy.wait()


def self_back(rows, first, keep, ins, outs, scratch):
    spot, mine, other, wq = ins[:4]
    pieces, (s_in, g_in, gains, wo, q_in, out_in, lse, k_in, v_in, w, length) = ins[4:6], ins[6:17]
    g_o, low_o, l3_o, part, sums = outs[:5]
    gm, dq, wq_other = scratch
    assemble(wq_other, spot, pieces)
    mine, other, wq = use(mine, other, wq)
    incoming = nt(mine[...], wq[...]) + nt(other[...].astype(BF), wq_other[...])
    back_head((incoming, s_in, g_in, gains, wo), (g_o, low_o, sums, gm), 1)
    l3_ref, part, sums = into(l3_o, part, sums)
    q_ref, out_in, lse, k_ref, v_ref, w = use(q_in, out_in, lse, k_in, v_in, w)
    width = k_ref.shape[1]
    before = [use(i) for i in ins[17:]]

    def emit(pair, part, at, here, grad_k, grad_v):
        for slot, grad in ((1, grad_k), (2, grad_v)):
            if first:
                into(outs[4 + slot])[:, at] = grad[:keep]
                l3_ref[slot, :, at] = grad[keep:].astype(BF)
            else:
                l3_ref[slot, :, at] = (grad + before[slot - 1][:, at]).astype(BF)

    bias = causal_bias(rows, rows.stop, length[0], True)
    attend_back(q_ref, gm, out_in, lse, k_ref, v_ref, rows, rows.stop, lambda start: bias, dq, emit)
    l3_ref[0] = (dq[...].astype(BF).astype(F32) * 0.125).astype(BF)
    flush(l3_o)
    part[...] = nt(l3_ref[0], w[0]) + nt(l3_ref[1], w[1]) + nt(l3_ref[2], w[2])
    sums[3:4, 0:width] = column_sums(l3_ref[0].astype(F32))
    sums[3:4, width : 2 * width] = column_sums(l3_ref[2].astype(F32))


def tokens_end(rows, ins, outs, scratch):
    tok, gains, g, mine, other = use(*ins[:5])
    earlier = use(ins[5])
    out, sums = into(*outs[:2])
    unit, scale = standard(tok[rows].astype(F32))
    incoming = mine[...] + other[...]
    grad = g[...] + norm_back(incoming, unit, scale, gains[0:1])
    gain, shift = column_sums(incoming * unit), column_sums(incoming)
    if len(ins) == 6:
        out[...] = grad
        flush(outs[0])
        sums[0:1], sums[1:2] = gain, shift
        total = sums
    else:
        out[rows] = grad
        out[rows.stop :] = earlier[...]
        flush(outs[0])
        total = sums
        first = use(ins[6])
        total[0:1] = gain + first[0:1]
        total[4:5] = shift + first[1:2]
        more, hid_sums, (y_low, y_high) = ins[7:13], ins[13:15], ins[15:17]
        y = into(outs[2])
        y_low, y_high = use(y_low, y_high)
        y[0 : rows.stop] = y_low[...]
        y[rows.stop :] = y_high[...]
        flush(outs[2])
        for level in range(3):
            first, second = use(more[2 * level], more[2 * level + 1])
            total[1 + level : 2 + level] = first[0:1] + second[0:1]
            total[5 + level : 6 + level] = first[1:2] + second[1:2]
            total[8 + level : 9 + level] = first[2:3] + second[2:3]
            if level == 0:
                total[11:12] = first[3:4] + second[3:4]
            if level == 1:
                half = total.shape[1] // 2
                total[12:13, :half] = first[3:4, :half] + second[3:4, :half]
                total[12:13, half:] = second[3:4, half:]
        first, second = use(*hid_sums)
        model = total.shape[1]
        for piece in range(first.shape[1] // model):
            at = slice(piece * model, (piece + 1) * model)
            total[13 + piece : 14 + piece] = first[0:1, at] + second[0:1, at]


def small_end(ins, outs, scratch):
    mine, other = use(*ins)
    gain, shift, ob, svb, cvb, fb = into(*outs)
    total = mine[...] + other[...]
    half = svb.shape[1]
    gain[...] = total[0:4]
    shift[...] = total[4:8]
    ob[...] = total[8:11]
    for target, at in ((svb, 11), (cvb, 12)):
        target[0:1] = total[at : at + 1, :half]
        target[1:2] = total[at : at + 1, half:]
    fb[...] = total[13 : 13 + fb.shape[0]]


def grads_sent(plan, ins, outs, scratch):
    orders = ins[: 1 + max(place for place, _ in plan)]
    at, col = len(orders), 0
    out, turned = into(outs[0]), list(outs[1:])
    half = out.shape[0]
    for place, items in plan:
        for parts, ordered, blocks in items:
            lefts = ins[at : at + parts]
            at += parts
            made = []
            for left in lefts:
                left = use(left)
                if not ordered:
                    target = turned.pop(0)
                    ref = into(target)
                    ref[...] = nt(use(orders[place])[...], left[...]).astype(BF)
                    flush(target)
                    left = ref
                made.append(left)
            for block in blocks:
                total, width = None, 0
                for part in range(parts):
                    right = use(ins[at + part])
                    value = right[block] if len(right.shape) == 3 else right[...]
                    width = value.shape[-1]
                    term = nn(made[part][half:], value)
                    total = term if total is None else total + term
                out[:, col : col + width] = total
                col += width
            at += parts


def grads_kept(plan, ins, outs, scratch):
    other, at, col = use(ins[0]), 1, 0
    half = other.shape[0]
    for n, (place, items) in enumerate(plan):
        sent, kept = into(outs[2 * n], outs[2 * n + 1])
        low, start = kept.shape[0], col
        for parts, ordered, blocks in items:
            lefts = [use(i) for i in ins[at : at + parts]]
            at += parts
            for block in blocks:
                total = None
                for part in range(parts):
                    right = use(ins[at + part])
                    value = right[block] if len(right.shape) == 3 else right[...]
                    width = value.shape[-1]
                    term = nn(lefts[part][:half], value)
                    total = term if total is None else total + term
                total = total + other[:, col : col + width]
                sent[:, col - start : col - start + width] = total[low:]
                kept[:, col - start : col - start + width] = total[:low]
                col += width
            at += parts
        flush(outs[2 * n], outs[2 * n + 1])


def halve(ins, outs, scratch):
    kept, other = use(*ins)
    sent, out = into(*outs)
    low = out.shape[0]
    out[...] = kept[0:low] + other[0:low]
    sent[...] = kept[low:] + other[low:]


def plain_end(ins, outs, scratch):
    kept, other = use(*ins)
    outs[0][...] = kept[...] + other[...]


def cross_end(ins, outs, scratch):
    kept, other = use(*ins)
    own = outs[0].shape[1]
    out_grad, query_grad, key_value_grad = outs
    out_grad[...] = kept[:, :own] + other[:, :own]
    query_grad[...] = kept[:, own : 2 * own] + other[:, own : 2 * own]
    for n in range(2):
        at = slice((2 + n) * own, (3 + n) * own)
        key_value_grad[:, n, :] = kept[:, at] + other[:, at]


def self_end(ins, outs, scratch):
    kept, other = use(*ins)
    own = outs[0].shape[1]
    for n, out in enumerate(outs):
        at = slice(n * own, (n + 1) * own)
        out[...] = kept[:, at] + other[:, at]


def swap_mp(v):
    return lax.ppermute(v, "mp", [(0, 1), (1, 0)])


def swap_dp(v, bit, dp_size):
    return lax.ppermute(v, "dp", [(i, i ^ bit) for i in range(dp_size)])


def relative_source(width, bits):
    shard = width // (1 << len(bits))
    me = lax.axis_index("dp")
    place = jnp.arange(width, dtype=jnp.int32)
    block = place // shard
    owner = jnp.zeros_like(block)
    for step, bit in enumerate(bits):
        owner = owner + ((block >> (len(bits) - 1 - step)) & 1) * bit
    return (owner ^ me) * shard + place % shard


class Halving:
    def __init__(self, chain, orders, groups, dp_size, name):
        self.chain, self.groups, self.dp_size, self.name = chain, groups, dp_size, name
        self.plan = tuple(
            (place, tuple((len(lhs), ordered, blocks) for lhs, ordered, rhs, blocks in items)) for place, bits, items in groups
        )
        self.model = orders[0].shape[0]
        self.columns = [
            sum(rhs[0].shape[-1] * len(blocks) for lhs, ordered, rhs, blocks in items) for place, bits, items in groups
        ]
        orders = orders[: 1 + max(place for place, bits, items in groups)]
        args = [(order, "h") for order in orders]
        outs = [(shaped((self.model // 2, sum(self.columns))), "v")]
        for place, bits, items in groups:
            for lhs, ordered, rhs, blocks in items:
                args += [(p, "h") for p in lhs] + [(p, "h") for p in rhs]
                if not ordered:
                    outs += [(shaped(p.shape[::-1], BF), "h") for p in lhs]
        made = chain(partial(grads_sent, self.plan), outs, args, 0, name + "_sent")
        self.turned = list(made[1:])
        self.first = chain.swap_dp(made[0], groups[0][1][0], dp_size)
        self.bits = [list(bits[1:]) for place, bits, items in groups]
        self.kept, self.other = [None] * len(groups), [None] * len(groups)

    def swap(self, n, sent):
        self.other[n] = self.chain.swap_dp(sent, self.bits[n].pop(0), self.dp_size)

    def keep(self, after=()):
        args, outs = [(self.first, "v")], []
        turned = list(self.turned)
        for columns, (place, bits, items) in zip(self.columns, self.groups):
            for lhs, ordered, rhs, blocks in items:
                for p in lhs:
                    args.append((p if ordered else turned.pop(0), "h"))
                args += [(p, "h") for p in rhs]
            outs += [(shaped((self.model // 4, columns)), "v")] * 2
        made = self.chain(partial(grads_kept, self.plan), outs, args, 0, self.name + "_kept", after=after)
        for n in range(len(self.groups)):
            self.kept[n] = made[2 * n + 1]
            self.swap(n, made[2 * n])

    def step(self, n, after=()):
        half = shaped((self.kept[n].shape[0] // 2, self.columns[n]))
        sent, self.kept[n] = self.chain(
            halve, [(half, "v"), (half, "v")], [(self.kept[n], "v"), (self.other[n], "v")], 0, self.name + str(n) + "_step",
            after=after,
        )
        self.swap(n, sent)

    def end(self, n, finish, outs):
        while self.bits[n]:
            self.step(n)
        return self.chain(
            finish, [(o, "v") for o in outs], [(self.kept[n], "v"), (self.other[n], "v")], 0, self.name + str(n) + "_end"
        )


def on_device(
    dp_size,
    tokens,
    frames,
    lengths,
    out_cot,
    self_query_key_value,
    self_qv_bias,
    self_output_weight,
    cross_query_weight,
    cross_kv,
    cross_bias,
    cross_output_weight,
    first_dense_weight,
    first_dense_bias,
    second_dense_weight,
    out_biases,
    norm_gains,
    norm_biases,
):
    _, slot, model = tokens.shape
    tok, frames, cot = tokens[0], frames[0], out_cot[0]
    real = frames.shape[0]
    padded = -(-real // 256) * 256
    own = self_output_weight.shape[0]
    ff = second_dense_weight.shape[0]
    cut = slot // 2 // 64 * 64
    low_rows, high_rows = slice(0, cut), slice(cut, slot)
    w3 = self_query_key_value.transpose(1, 0, 2)
    w2kv = cross_kv.transpose(1, 0, 2)
    fb = first_dense_bias[None]
    gains, shifts, ob = norm_gains, norm_biases, out_biases
    bits = [1 << i for i in range(dp_size.bit_length() - 1)]
    turned_bits = bits[:1] + bits[2:] + bits[1:2]
    sources = jnp.stack([relative_source(model, bits), relative_source(model, turned_bits)], axis=1)
    chain = Chain(norm_gains)
    spot = (lax.axis_index("dp") & 3).astype(jnp.int32)
    spots = spot.reshape(1)

    def count(rows):
        return rows.stop - rows.start

    def sized(rows, width, dtype=F32):
        return shaped((count(rows), width), dtype)

    def attended(rows):
        return [(sized(rows, own, BF), "h"), (sized(rows, own), "h"), (shaped((8, count(rows))), "h"), (sized(rows, model), "v")]

    def fetched(weight, parts):
        block = weight.shape[0] // parts
        at = (spot & (parts - 1)) * block
        return swap_mp(lax.dynamic_slice_in_dim(weight, at, block, 0).astype(F32))

    made = chain(
        partial(self_start, cut),
        [(sized(low_rows, model, BF), "h"), (sized(high_rows, model, BF), "h")] + [(shaped((slot, own), BF), "h")] * 3
        + attended(high_rows),
        [(tok, "h"), (gains, "h"), (shifts, "h"), (self_qv_bias, "h"), (w3, "h"), (lengths, "s"), (self_output_weight, "h")],
        0,
        "self_start",
    )
    x1_l, x1_h, q1, k1, v1, mix1_h, out1_h, lse1_h, part1_h = made
    other1_h = chain.swap_mp(part1_h)
    mix1_l, out1_l, lse1_l, part1_l = chain(
        partial(self_next, low_rows),
        attended(low_rows),
        [(q1, "h"), (k1, "h"), (v1, "h"), (lengths, "s"), (self_output_weight, "h")],
        0,
        "self_next",
    )
    other1_l = chain.swap_mp(part1_l)
    k2, v2, turned_frames, order, order_turned = chain(
        frames_start,
        [(shaped((padded, own), BF), "h")] * 2 + [(shaped((model, padded), BF), "h")] + [(shaped((model, model), BF), "h")] * 2,
        [(frames, "h"), (w2kv, "h"), (cross_bias, "h"), (sources, "h")],
        0,
        "frames_start",
    )
    orders = (order, order_turned)

    def turned(plan, parts):
        used = orders[: 1 + max(place for place, _ in plan)]
        return chain(
            partial(turn, plan),
            [(shaped((model, parts[part].shape[0]), BF), "h") for _, part in plan],
            [(o, "h") for o in used] + [(p, "h") for p in parts],
            0,
            "turn",
        )

    x1t_h, x1t_l, x1o_h, x1o_l = turned(((0, 0), (0, 1), (1, 0), (1, 1)), (x1_h, x1_l))

    def cross(rows, mine, other):
        return chain(
            partial(cross_start, rows, real),
            [(sized(rows, model), "h"), (sized(rows, model, BF), "h"), (sized(rows, own, BF), "h")] + attended(rows),
            [(mine, "v"), (other, "v"), (tok, "h"), (ob, "h"), (gains, "h"), (shifts, "h"), (cross_bias, "h"),
             (cross_query_weight, "h"), (k2, "h"), (v2, "h"), (cross_output_weight, "h")],
            0,
            "cross_start",
        )

    s1_h, x2_h, q2_h, mix2_h, out2_h, lse2_h, part2_h = cross(high_rows, part1_h, other1_h)
    other2_h = chain.swap_mp(part2_h)
    s1_l, x2_l, q2_l, mix2_l, out2_l, lse2_l, part2_l = cross(low_rows, part1_l, other1_l)
    other2_l = chain.swap_mp(part2_l)
    x2t_h, x2t_l = turned(((0, 0), (0, 1)), (x2_h, x2_l))

    def dense(rows, s1, mine, other):
        return chain(
            dense_start,
            [(sized(rows, model), "h"), (sized(rows, model, BF), "h"), (sized(rows, ff, BF), "h"), (sized(rows, ff), "h"),
             (sized(rows, model), "v")],
            [(mine, "v"), (other, "v"), (s1, "h"), (ob, "h"), (gains, "h"), (shifts, "h"), (fb, "h"),
             (first_dense_weight, "h"), (second_dense_weight, "h")],
            0,
            "dense_start",
        )

    s2_h, x3_h, act_h, slope_h, part3_h = dense(high_rows, s1_h, part2_h, other2_h)
    other3_h = chain.swap_mp(part3_h)
    s2_l, x3_l, act_l, slope_l, part3_l = dense(low_rows, s1_l, part2_l, other2_l)
    other3_l = chain.swap_mp(part3_l)
    x3o_h, x3o_l = turned(((1, 0), (1, 1)), (x3_h, x3_l))

    def dense_b(rows, s2, mine, other, slope):
        return chain(
            partial(dense_back, rows),
            [(sized(rows, model, BF), "h"), (sized(rows, model), "h"), (sized(rows, model, BF), "h"),
             (sized(rows, ff, BF), "h"), (sized(rows, model), "v"), (shaped((8, model)), "v"), (shaped((8, ff)), "v")],
            [(mine, "v"), (other, "v"), (s2, "h"), (ob, "h"), (gains, "h"), (shifts, "h"), (cot, "h"), (lengths, "s"),
             (second_dense_weight, "h"), (slope, "h"), (first_dense_weight, "h")],
            6 * count(rows) * model * ff,
            "dense_back",
        )

    y_h, g3_h, low3_h, hid_h, part4_h, sum3_h, hsum_h = dense_b(high_rows, s2_h, part3_h, other3_h, slope_h)
    other4_h = chain.swap_mp(part4_h)
    y_l, g3_l, low3_l, hid_l, part4_l, sum3_l, hsum_l = dense_b(low_rows, s2_l, part3_l, other3_l, slope_l)

    denses = Halving(
        chain,
        orders,
        [
            (0, bits, [((low3_h, low3_l), False, (act_h, act_l), (0,))]),
            (1, turned_bits, [((x3o_h, x3o_l), True, (hid_h, hid_l), (0,))]),
        ],
        dp_size,
        "dense",
    )
    other4_l = chain.swap_mp(chain.tie(part4_l))
    wq_0 = chain.later(lambda tied=chain.tie(cross_query_weight): fetched(tied, 2))
    chain.pause(other4_h)
    denses.keep()

    def cross_b(rows, early, s2, g3, mine, other, q2, out2, lse2, before, after=()):
        pairs = own // LANES
        wide = [(shaped((pairs, padded, LANES)), "r")] * 2 if early else [(shaped((padded, own), BF), "h")] * 2
        scratch = [pltpu.VMEM((count(rows), own), BF), pltpu.VMEM((count(rows), own), F32)]
        if early:
            scratch += [pltpu.VMEM((pairs, padded, LANES), F32)] * 2 + [pltpu.SemaphoreType.DMA((2, pairs, BACK_BLOCKS))]
        return chain(
            partial(cross_back, early, real),
            [(sized(rows, model), "h"), (sized(rows, model, BF), "h"), (sized(rows, own, BF), "h"), (sized(rows, own), "v"),
             (shaped((8, model)), "v")] + wide,
            [(mine, "v"), (other, "v"), (s2, "h"), (g3, "h"), (gains, "h"), (cross_output_weight, "h"), (q2, "h"), (out2, "h"),
             (lse2, "h"), (k2, "h"), (v2, "h")] + before,
            4 * count(rows) * model * own + 20 * count(rows) * padded * own,
            "cross_back",
            after=after,
            scratch=scratch,
        )

    g2_h, low2_h, lq2_h, part5_h, sum2_h, dk_h, dv_h = cross_b(
        high_rows, True, s2_h, g3_h, part4_h, other4_h, q2_h, out2_h, lse2_h, []
    )
    other5_h = chain.swap_mp(part5_h)
    wq_1 = chain.later(lambda tied=chain.link: swap_dp(lax.optimization_barrier((wq_0.value, tied))[0], 1, dp_size))
    g2_l, low2_l, lq2_l, part5_l, sum2_l, lk2, lv2 = cross_b(
        low_rows, False, s2_l, g3_l, part4_l, other4_l, q2_l, out2_l, lse2_l, [(dk_h, "h"), (dv_h, "h")], (wq_0,)
    )
    other5_l = chain.swap_mp(part5_l)
    denses.step(0)
    which = lax.axis_index("mp").astype(jnp.int32).reshape(1)
    half_width = model // 2
    cuts = [-(-real * n // (8 * PIECES)) * 8 for n in range(PIECES)] + [real]
    frames_parts = chain(
        frames_sent, [(shaped((cuts[n + 1] - cuts[n], half_width)), "h") for n in range(PIECES)],
        [(which, "s"), (lk2, "h"), (lv2, "h"), (w2kv, "h")], 0, "frames_sent",
    )
    frames_other = [chain.swap_mp(frames_parts[0])]
    crosses = Halving(
        chain,
        orders,
        [
            (
                0,
                bits,
                [
                    ((low2_h, low2_l), False, (mix2_h, mix2_l), (0,)),
                    ((x2t_h, x2t_l), True, (lq2_h, lq2_l), (0,)),
                    ((turned_frames,), True, (lk2,), (0,)),
                    ((turned_frames,), True, (lv2,), (0,)),
                ],
            )
        ],
        dp_size,
        "cross",
    )
    denses.step(1)
    crosses.keep()
    wqs = [(wq_0, "h"), (wq_1, "h")]

    def self_b(rows, early, s1, g2, mine, other, out1, lse1, before):
        outs = [(sized(rows, model), "h"), (sized(rows, model, BF), "h"), (shaped((3, count(rows), own), BF), "h"),
                (sized(rows, model), "v"), (shaped((8, model)), "v")]
        if early:
            outs += [(shaped((cut, own)), "v")] * 2
        return chain(
            partial(self_back, rows, early, cut),
            outs,
            [(spots, "s"), (mine, "h"), (other, "v"), (cross_query_weight, "h")] + wqs + [(s1, "h"), (g2, "h"), (gains, "h"), (self_output_weight, "h"), (q1, "h"), (out1, "h"),
             (lse1, "h"), (k1, "h"), (v1, "h"), (w3, "h"), (lengths, "s")] + before,
            8 * count(rows) * model * own + 20 * count(rows) * rows.stop * own,
            "self_back",
            scratch=[pltpu.VMEM((count(rows), own), BF), pltpu.VMEM((count(rows), own), F32), pltpu.VMEM((model, own), BF)],
        )

    g1_h, low1_h, l3_h, part6_h, sum1_h, dk1, dv1 = self_b(
        high_rows, True, s1_h, g2_h, lq2_h, other5_h, out1_h, lse1_h, []
    )
    other6_h = chain.swap_mp(part6_h)
    g1_l, low1_l, l3_l, part6_l, sum1_l = self_b(
        low_rows, False, s1_l, g2_l, lq2_l, other5_l, out1_l, lse1_l, [(dk1, "v"), (dv1, "v")]
    )
    other6_l = chain.swap_mp(part6_l)
    denses.step(0, (frames_other[0],))
    denses.step(1)
    selves = Halving(
        chain,
        orders,
        [
            (
                0,
                bits,
                [((low1_h, low1_l), False, (mix1_h, mix1_l), (0,)), ((x1t_h, x1t_l), True, (l3_h, l3_l), (0,))],
            ),
            (1, turned_bits, [((x1o_h, x1o_l), True, (l3_h, l3_l), (1, 2))]),
        ],
        dp_size,
        "self",
    )
    crosses.step(0)
    t_high, sum0_h = chain(
        partial(tokens_end, high_rows),
        [(sized(high_rows, model), "h"), (shaped((8, model)), "h")],
        [(tok, "h"), (gains, "h"), (g1_h, "h"), (part6_h, "v"), (other6_h, "v"), (lengths, "s")],
        0,
        "tokens_end",
    )
    frames_other.append(chain.swap_mp(chain.tie(frames_parts[1])))
    selves.keep()
    shard = model // dp_size
    (second_turned,) = denses.end(0, plain_end, [shaped((shard, ff))])
    (first_grad,) = denses.end(1, plain_end, [shaped((shard, ff))])
    tokens_grad, total, y = chain(
        partial(tokens_end, low_rows),
        [(shaped((slot, model)), "h"), (shaped((13 + ff // model, model)), "v"), (shaped((slot, model), BF), "h")],
        [(tok, "h"), (gains, "h"), (g1_l, "h"), (part6_l, "v"), (other6_l, "v"), (t_high, "h"), (sum0_h, "h"),
         (sum1_h, "h"), (sum1_l, "h"), (sum2_h, "h"), (sum2_l, "h"), (sum3_h, "h"), (sum3_l, "h"), (hsum_h, "h"),
         (hsum_l, "h"), (y_l, "h"), (y_h, "h")],
        0,
        "tokens_end",
    )
    small_bits = list(bits)

    def small_step(total, other):
        (total,) = chain(plain_end, [(shaped(total.shape), "v")], [(total, "v"), (other, "v")], 0, "small_step")
        return total, chain.swap_dp(total, small_bits.pop(0), dp_size)

    small_other = chain.swap_dp(total, small_bits.pop(0), dp_size)
    frames_other.append(chain.swap_mp(chain.tie(frames_parts[2])))
    crosses.step(0, (frames_other[1],))
    selves.step(0)
    total, small_other = small_step(total, small_other)
    selves.step(1)
    frames_other.append(chain.swap_mp(chain.tie(frames_parts[3])))
    selves.step(0, (frames_other[2],))
    total, small_other = small_step(total, small_other)
    selves.step(1)
    cross_out_grad, cross_q_grad, cross_kv_grad = crosses.end(
        0, cross_end, [shaped((shard, own)), shaped((shard, own)), shaped((shard, 2, own))]
    )
    while small_bits:
        total, small_other = small_step(total, small_other)
    (frames_grad,) = chain(
        frames_kept, [(shaped((real, 1, half_width)), "r")],
        [(which, "s"), (lk2, "h"), (lv2, "h"), (w2kv, "h")] + [(o, "h") for o in frames_other],
        0, "frames_kept",
        scratch=[pltpu.VMEM((real, half_width), F32), pltpu.SemaphoreType.DMA],
    )
    self_out_grad, q_grad = selves.end(0, self_end, [shaped((shard, own))] * 2)
    k_grad, v_grad = selves.end(1, self_end, [shaped((shard, own))] * 2)
    gains_grad, shifts_grad, ob_grad, svb_grad, cvb_grad, fb_grad = chain(
        small_end,
        [(shaped((4, model)), "v"), (shaped((4, model)), "v"), (shaped((3, model)), "v"), (shaped((2, own)), "v"),
         (shaped((2, own)), "v"), (shaped((ff // model, model)), "v")],
        [(total, "v"), (small_other, "v")],
        0,
        "small_end",
    )
    return (
        y[None],
        tokens_grad[None],
        frames_grad.transpose(1, 0, 2),
        jnp.stack([q_grad, k_grad, v_grad], axis=1),
        svb_grad,
        self_out_grad.T,
        cross_q_grad,
        cross_kv_grad,
        cvb_grad,
        cross_out_grad.T,
        first_grad,
        fb_grad.reshape(ff),
        second_turned.T,
        ob_grad,
        gains_grad,
        shifts_grad,
    )


def solution(mesh):
    in_specs = (
        P("dp", None, None),
        P("dp", None, None),
        P("dp"),
        P("dp", None, None),
        P(None, None, "mp"),
        P(None, "mp"),
        P("mp", None),
        P(None, "mp"),
        P(None, None, "mp"),
        P(None, "mp"),
        P("mp", None),
        P(None, "mp"),
        P("mp"),
        P("mp", None),
        P(),
        P(),
        P(),
    )
    out_specs = (
        P("dp", None, None),
        P("dp", None, None),
        P("dp", None, "mp"),
        P("dp", None, "mp"),
        P(None, "mp"),
        P("mp", "dp"),
        P("dp", "mp"),
        P("dp", None, "mp"),
        P(None, "mp"),
        P("mp", "dp"),
        P("dp", "mp"),
        P("mp"),
        P("mp", "dp"),
        P(),
        P(),
        P(),
    )
    return jax.shard_map(
        partial(on_device, mesh.shape["dp"]),
        mesh=mesh,
        in_specs=in_specs,
        out_specs=out_specs,
        check_vma=False,
    )
```

```python
from functools import partial

import jax
import jax.numpy as jnp
from jax import lax
from jax.experimental import pallas as pl
from jax.experimental.pallas import tpu as pltpu
from jax.sharding import PartitionSpec as P

F32 = jnp.float32
BF = jnp.bfloat16
HEAD_DIM = 64
LANES = 128
NEG = -1e30
COST = {"self_start": 2.0, "self_next": 1.3, "turn": 1.0, "frames_start": 3.0, "cross_start": 2.7, "dense_start": 2.4,
        "dense_back": 2.4, "dense_sent": 6.0, "dense_kept": 6.0, "cross_back": 20.0, "self_back": 12.0,
        "cross_sent": 6.0, "cross_kept": 5.0, "self_sent": 5.0, "self_kept": 4.0, "tokens_end": 5.0, "frames_kept": 6.0,
        "small_end": 1.0, "pause": 8.0}
SCALE = 1.5e10
PIECES = 4
BACK_BLOCKS = 2
BYTES = 6.4e-3
PINNED = ("h", "t", "r")


def shaped(shape, dtype=F32):
    return jax.ShapeDtypeStruct(tuple(shape), dtype)


def dg(a, b, ca, cb):
    return lax.dot_general(a, b, (((ca,), (cb,)), ((), ())), preferred_element_type=F32)


def nn(a, b):
    return dg(a, b, 1, 0)


def nt(a, b):
    return dg(a, b, 1, 1)


def tn(a, b):
    return dg(a, b, 0, 0)


class Feed:
    def __init__(self, source, target, sem):
        self.copy = pltpu.make_async_copy(source, target, sem)
        self.copy.start()
        self.target = target
        self.pending = True

    def ready(self):
        if self.pending:
            self.copy.wait()
            self.pending = False
        return self.target


class Drain:
    def __init__(self, source, target, sem):
        self.ref = source
        self.copy = pltpu.make_async_copy(source, target, sem)
        self.pending = True

    def flush(self):
        if self.pending:
            self.copy.start()
            self.pending = False


def use(*inputs):
    made = [i.ready() if isinstance(i, Feed) else i for i in inputs]
    return made if len(made) > 1 else made[0]


def flush(*outputs):
    for o in outputs:
        if isinstance(o, Drain):
            o.flush()


def into(*outputs):
    made = [o.ref if isinstance(o, Drain) else o for o in outputs]
    return made if len(made) > 1 else made[0]


class Pending:
    def __init__(self, make):
        self.make, self.value = make, None


class Chain:
    def __init__(self, seed):
        self.link = seed
        self.pending = []

    def pause(self, *after):
        self(lambda ins, outs, scratch: None, [], [], 0, "pause", after=after)

    def later(self, make):
        self.pending.append(Pending(make))
        return self.pending[-1]

    def settle(self):
        for item in reversed(self.pending):
            item.value = item.make()
        self.pending = []

    def swap_mp(self, v):
        return self.later(lambda: swap_mp(v))

    def swap_dp(self, v, bit, dp_size):
        return self.later(lambda: swap_dp(v, bit, dp_size))

    def tie(self, value):
        return lax.optimization_barrier((value, self.link))[0]

    def __call__(self, kernel, outs, args, flops, name, scratch=(), after=()):
        place = {
            "v": pl.BlockSpec(memory_space=pltpu.VMEM),
            "h": pl.BlockSpec(memory_space=pltpu.HBM),
            "s": pl.BlockSpec(memory_space=pltpu.SMEM),
        }
        args = [(self.link, "t")] + [(a, "t") for a in after] + list(args)
        first = 1 + len(after)
        if any(isinstance(a, Pending) and a.value is None for a, _ in args):
            self.settle()
        args = [(a.value if isinstance(a, Pending) else a, k) for a, k in args]
        outs = [(shaped((8, LANES)), "t")] + list(outs)
        held = []
        for item, kind in args[first:] + outs[1:]:
            if kind == "h":
                held.append(pltpu.VMEM(item.shape, item.dtype))
        n_in, n_out = len(args), len(outs)

        def body(*refs):
            ins, results = refs[first:n_in], refs[n_in + 1 : n_in + n_out]
            rest = refs[n_in + n_out :]
            own, bufs, sems = rest[: len(scratch)], list(rest[len(scratch) : -1]), rest[-1]
            at = 0
            feeds, drains = [], []
            for ref, (_, kind) in zip(ins, args[first:]):
                if kind == "h":
                    feeds.append(Feed(ref, bufs[at], sems.at[at]))
                    at += 1
                else:
                    feeds.append(ref)
            for ref, (_, kind) in zip(results, outs[1:]):
                if kind == "h":
                    drains.append(Drain(bufs[at], ref, sems.at[at]))
                    at += 1
                else:
                    drains.append(ref)
            kernel(feeds, drains, own)
            for feed in feeds:
                use(feed)
            flush(*drains)
            for d in drains:
                if isinstance(d, Drain):
                    d.copy.wait()

        moved = 0
        for item, kind in args + outs:
            size = jnp.dtype(item.dtype).itemsize
            for d in item.shape:
                size *= d
            moved += size
        place["t"] = place["r"] = place["h"]
        made = pl.pallas_call(
            body,
            out_shape=tuple(pltpu.HBM(o.shape, o.dtype) if k in PINNED else o for o, k in outs),
            in_specs=[place[k] for _, k in args],
            out_specs=tuple(place[k] for _, k in outs),
            scratch_shapes=list(scratch) + held + [pltpu.SemaphoreType.DMA((max(1, len(held)),))],
            compiler_params=pltpu.CompilerParams(vmem_limit_bytes=28 * 1024 * 1024),
            cost_estimate=pl.CostEstimate(flops=int(COST.get(name, 1.0) * SCALE), transcendentals=0, bytes_accessed=int(COST.get(name, 1.0) * SCALE * BYTES)),
            name=name,
        )(*[pltpu.with_memory_space_constraint(a, pltpu.HBM) if k in PINNED else a for a, k in args])
        self.link = made[0]
        return made[1:]


def standard(stream):
    centred = stream - jnp.mean(stream, axis=1, keepdims=True)
    spread = jnp.mean(centred * centred, axis=1, keepdims=True)
    scale = lax.rsqrt(spread + 1e-05)
    return centred * scale, scale


def norm_back(grad, unit, scale, gain):
    lifted = grad * gain
    mean_plain = jnp.mean(lifted, axis=1, keepdims=True)
    mean_cross = jnp.mean(lifted * unit, axis=1, keepdims=True)
    return scale * (lifted - mean_plain - unit * mean_cross)


def column_sums(values):
    return jnp.sum(values, axis=0, keepdims=True)


def head_lanes(which):
    lane = lax.broadcasted_iota(jnp.int32, (1, LANES), 1)
    return (lane < HEAD_DIM) if which == 0 else (lane >= HEAD_DIM)


def only(mask, values):
    return jnp.where(mask, values, jnp.zeros_like(values))


def pair_slice(pair):
    return pl.ds(pl.multiple_of(pair * LANES, LANES), LANES)


def attend_rows(q_ref, k_ref, v_ref, rows, keys, bias, mixed_ref, out_ref, lse_ref):
    lane = lax.broadcasted_iota(jnp.int32, (1, LANES), 1)
    count = rows.stop - rows.start

    def body(pair, lse):
        at = pair_slice(pair)
        k_pair, v_pair, q_pair = k_ref[0:keys, at], v_ref[0:keys, at], q_ref[rows, at]
        result = None
        for which in range(2):
            mask = head_lanes(which)
            scores = nt(only(mask, q_pair), k_pair) + bias
            top = jnp.max(scores, axis=1, keepdims=True)
            raised = jnp.exp(scores - top)
            total = jnp.sum(raised, axis=1, keepdims=True)
            value = nn(raised.astype(BF), v_pair) * (1.0 / total)
            result = value if which == 0 else jnp.where(mask, value, result)
            lse = jnp.where(lane == 2 * pair + which, top + jnp.log(total), lse)
        out_ref[:, at] = result
        mixed_ref[:, at] = result.astype(BF)
        return lse

    lse = lax.fori_loop(0, q_ref.shape[1] // LANES, body, jnp.zeros((count, LANES), F32))
    lse_ref[...] = lse.T[0 : lse_ref.shape[0]]


def attend_back(q_ref, g_ref, o_ref, lse_ref, k_ref, v_ref, rows, keys, bias, dq_ref, emit, block=None):
    block = keys if block is None else block
    blocks = keys // block

    def body(step, carry):
        pair, part = (step, 0) if blocks == 1 else (step // blocks, step % blocks)
        at = pair_slice(pair)
        here = pl.ds(0, keys) if blocks == 1 else pl.ds(pl.multiple_of(part * block, block), block)
        k_pair, v_pair = k_ref[here, at], v_ref[here, at]
        q_pair, g_pair = q_ref[rows, at], g_ref[:, at]
        product = (g_pair.astype(F32) * o_ref[:, at]).T
        k_turned = k_pair.T
        parts, grad_k, grad_v = [], None, None
        for which in range(2):
            mask = head_lanes(which)
            q_head, g_head = only(mask, q_pair), only(mask, g_pair)
            inner = column_sums(product[which * HEAD_DIM : (which + 1) * HEAD_DIM])
            scores = nt(k_pair, q_head) + bias(part * block)
            probs = jnp.exp(scores - lse_ref[pl.ds(2 * pair + which, 1), :])
            grad_probs = nt(v_pair, g_head)
            grad_scores = (probs * (grad_probs - inner)).astype(BF)
            here_v = nn(probs.astype(BF), g_head)
            here_k = nn(grad_scores, q_head)
            grad_v = here_v if which == 0 else grad_v + here_v
            grad_k = here_k if which == 0 else grad_k + here_k
            parts.append(nn(k_turned[which * HEAD_DIM : (which + 1) * HEAD_DIM], grad_scores))
        emit(pair, part, at, here, grad_k, grad_v)
        grad_q = jnp.concatenate(parts, axis=0).T
        if blocks == 1:
            dq_ref[:, at] = grad_q
        else:
            dq_ref[:, at] += grad_q
        return carry

    if blocks > 1:
        dq_ref[...] = jnp.zeros_like(dq_ref)
    lax.fori_loop(0, q_ref.shape[1] // LANES * blocks, body, 0)


def causal_bias(rows, keys, length, turned):
    count = rows.stop - rows.start
    shape = (keys, count) if turned else (count, keys)
    query = lax.broadcasted_iota(jnp.int32, shape, 1 if turned else 0) + rows.start
    key = lax.broadcasted_iota(jnp.int32, shape, 0 if turned else 1)
    return jnp.where((key <= query) & (key < length), 0.0, NEG).astype(F32)


def tail_bias(keys, real, turned, start=0):
    shape = (keys, 1) if turned else (1, keys)
    key = lax.broadcasted_iota(jnp.int32, shape, 0 if turned else 1) + start
    return jnp.where(key < real, 0.0, NEG).astype(F32)


def self_start(cut, ins, outs, scratch):
    tok, gains, shifts, vb, w, length, wo = ins
    x_lo, x_hi, q_o, k_o, v_o = outs[:5]
    rows = slice(cut, tok.target.shape[0])
    low_ref, high_ref, q_ref, k_ref, v_ref = into(*outs[:5])
    tok, gains, shifts = use(tok, gains, shifts)
    unit, _ = standard(tok[...].astype(F32))
    x = (unit * gains[0:1] + shifts[0:1]).astype(BF)
    low_ref[...] = x[:cut]
    high_ref[...] = x[cut:]
    vb, w = use(vb, w)
    q_ref[...] = ((nn(x, w[0]) + vb[0:1]) * 0.125).astype(BF)
    k_ref[...] = nn(x, w[1]).astype(BF)
    v_ref[...] = (nn(x, w[2]) + vb[1:2]).astype(BF)
    flush(x_lo, x_hi, q_o, k_o, v_o)
    self_rows(rows, q_ref, k_ref, v_ref, length, wo, outs[5:])


def self_next(rows, ins, outs, scratch):
    q_ref, k_ref, v_ref, length, wo = ins
    self_rows(rows, *use(q_ref, k_ref, v_ref), length, wo, outs)


def self_rows(rows, q_ref, k_ref, v_ref, length, wo, outs):
    bias = causal_bias(rows, rows.stop, length[0], False)
    mixed, out, lse, part = into(*outs)
    attend_rows(q_ref, k_ref, v_ref, rows, rows.stop, bias, mixed, out, lse)
    flush(*outs[:3])
    part[...] = nn(mixed[...], use(wo)[...])


def turn(plan, ins, outs, scratch):
    orders = ins[: 1 + max(place for place, _ in plan)]
    parts = ins[len(orders) :]
    for (place, part), out in zip(plan, outs):
        into(out)[...] = nt(use(orders[place])[...], use(parts[part])[...]).astype(BF)
        flush(out)


def frames_start(ins, outs, scratch):
    frames, w, vb, sources = ins
    k_o, v_o, t_o, order_o, other_o = outs
    k_ref, v_ref, t_ref, order, other = into(*outs)
    sources = use(sources)
    column = lax.broadcasted_iota(jnp.int32, order.shape, 1)
    order[...] = jnp.where(column == sources[:, 0:1], 1.0, 0.0).astype(BF)
    other[...] = jnp.where(column == sources[:, 1:2], 1.0, 0.0).astype(BF)
    flush(order_o, other_o)
    real, padded = frames.target.shape[0], k_ref.shape[0]
    low = real // 16 * 16
    if padded > real:
        for ref in (k_ref, v_ref):
            ref[low:padded] = jnp.zeros((padded - low, ref.shape[1]), BF)
        edge = real // LANES * LANES
        t_ref[:, edge:padded] = jnp.zeros((t_ref.shape[0], padded - edge), BF)
    frames, w, vb = use(frames, w, vb)
    k_ref[0:real] = nn(frames[...], w[0]).astype(BF)
    flush(k_o)
    v_ref[0:real] = (nn(frames[...], w[1]) + vb[1:2]).astype(BF)
    flush(v_o)
    t_ref[:, 0:real] = nt(order[...], frames[...]).astype(BF)


def assemble(out, spot, pieces):
    block = out.shape[0] // len(pieces)
    for j, piece in enumerate(pieces):
        at = pl.multiple_of(((spot[0] & (len(pieces) - 1)) ^ j) * block, 16)
        out[pl.ds(at, block), :] = use(piece)[...].astype(BF)


def cross_start(rows, real, ins, outs, scratch):
    mine, other, tok, ob, gains, shifts, vb, wq, k_in, v_in, wo = ins
    s_o, x_o, q_o, m_o, out_o, lse_o, part = outs
    mixed, out, lse, part = into(m_o, out_o, lse_o, part)
    s_ref, x_ref, q_ref = into(s_o, x_o, q_o)
    mine, other, tok, ob, gains, shifts = use(mine, other, tok, ob, gains, shifts)
    stream = tok[rows].astype(F32) + (mine[...] + other[...]) + ob[0:1]
    s_ref[...] = stream
    flush(s_o)
    unit, _ = standard(stream)
    x = (unit * gains[1:2] + shifts[1:2]).astype(BF)
    x_ref[...] = x
    vb, wq = use(vb, wq)
    q_ref[...] = ((nn(x, wq[...]) + vb[0:1]) * 0.125).astype(BF)
    flush(x_o, q_o)
    k_ref, v_ref = use(k_in, v_in)
    keys = k_ref.shape[0]
    attend_rows(q_ref, k_ref, v_ref, slice(0, x.shape[0]), keys, tail_bias(keys, real, False), mixed, out, lse)
    flush(m_o, out_o, lse_o)
    part[...] = nn(mixed[...], use(wo)[...])


def dense_start(ins, outs, scratch):
    mine, other, s_in, ob, gains, shifts, fb, w1, w2 = ins
    s_o, x_o, a_o, d_o, part = outs
    s_ref, x_ref, active, slope, part = into(s_o, x_o, a_o, d_o, part)
    mine, other, s_in, ob, gains, shifts = use(mine, other, s_in, ob, gains, shifts)
    stream = s_in[...] + (mine[...] + other[...]) + ob[1:2]
    s_ref[...] = stream
    unit, _ = standard(stream)
    x_ref[...] = (unit * gains[2:3] + shifts[2:3]).astype(BF)
    flush(s_o, x_o)
    fb, w1, w2 = use(fb, w1, w2)
    wide = 3 * LANES

    def body(step, carry):
        at = pl.ds(pl.multiple_of(step * wide, wide), wide)
        hidden = nn(x_ref[...], w1[:, at]) + fb[:, at]
        below = 0.5 + 0.5 * lax.erf(hidden * 0.7071067811865476)
        slope[:, at] = below + hidden * (0.3989422804014327 * jnp.exp(-0.5 * hidden * hidden))
        value = (hidden * below).astype(BF)
        active[:, at] = value
        part[...] += nn(value, w2[at, :])
        return carry

    part[...] = jnp.zeros_like(part)
    lax.fori_loop(0, w1.shape[1] // wide, body, 0)


def dense_back(rows, ins, outs, scratch):
    mine, other, s_in, ob, gains, shifts, cot, length, w2, slope, w1 = ins
    y_o, g_o, low_o, hid_o, part, sums, hid_sums = outs
    out_ref, g_ref, low_ref, hid_ref, part, sums, hid_sums = into(*outs)
    mine, other, s_in, ob, gains, shifts = use(mine, other, s_in, ob, gains, shifts)
    stream = s_in[...] + (mine[...] + other[...]) + ob[2:3]
    unit, scale = standard(stream)
    row = lax.broadcasted_iota(jnp.int32, (stream.shape[0], 1), 0) + rows.start
    valid = (row < length[0]).astype(F32)
    out_ref[...] = ((unit * gains[3:4] + shifts[3:4]) * valid).astype(BF)
    incoming = use(cot)[rows].astype(F32) * valid
    grad = norm_back(incoming, unit, scale, gains[3:4])
    g_ref[...] = grad
    low_ref[...] = grad.astype(BF)
    flush(y_o, g_o, low_o)
    sums[0:1] = column_sums(incoming * unit)
    sums[1:2] = column_sums(incoming)
    sums[2:3] = column_sums(grad)
    w2, slope, w1 = use(w2, slope, w1)
    wide = 3 * LANES

    def body(step, carry):
        at = pl.ds(pl.multiple_of(step * wide, wide), wide)
        low = (slope[:, at] * nt(low_ref[...], w2[at, :])).astype(BF)
        hid_ref[:, at] = low
        hid_sums[0:1, at] = column_sums(low.astype(F32))
        part[...] += nt(low, w1[:, at])
        return carry

    part[...] = jnp.zeros_like(part)
    lax.fori_loop(0, w1.shape[1] // wide, body, 0)


def back_head(incoming, ins, outs, gm, gains, wo, sums, level, more):
    s_in, g_in = ins
    g_o, low_o = outs
    g_ref, low_ref = into(g_o, low_o)
    s_in, g_in, gains = use(s_in, g_in, gains)
    unit, scale = standard(s_in[...])
    grad = g_in[...] + norm_back(incoming, unit, scale, gains[level : level + 1])
    g_ref[...] = grad
    low = grad.astype(BF)
    low_ref[...] = low
    flush(g_o, low_o)
    made = (column_sums(incoming * unit), column_sums(incoming), column_sums(grad))
    for n, value in enumerate(made):
        sums[n : n + 1] = sums[n : n + 1] + value if more else value
    gm[...] = nt(low, use(wo)[...]).astype(BF)


def gather_heads(count, q_all, o_all, lse_all, refs):
    start = 0
    for q_ref, out_in, lse in refs:
        q_ref, out_in, lse = use(q_ref, out_in, lse)
        stop = start + out_in.shape[0]
        if q_all is not None:
            q_all[start:stop] = q_ref[...]
        o_all[start:stop] = out_in[...]
        lse_all[:, start:stop] = lse[...]
        start = stop


def cross_back(cut, real, ins, outs, scratch):
    blocks = (ins[:7], ins[7:14])
    gains, wo, k_in, v_in, which, kv = ins[14:20]
    lq_outs, part, sums, dk_o, dv_o = outs[4:6], outs[6], outs[7], outs[8], outs[9]
    gm, dq, q_all, o_all, lse_all = scratch
    part, sums, dk, dv = into(part, sums, dk_o, dv_o)
    start = 0
    for n, (mine, other, s_in, g_in, q_ref, out_in, lse) in enumerate(blocks):
        incoming = use(mine)[...] + use(other)[...]
        stop = start + incoming.shape[0]
        back_head(incoming, (s_in, g_in), outs[2 * n : 2 * n + 2], gm.at[start:stop], gains, wo, sums, 2, n > 0)
        start = stop
    gather_heads(start, q_all, o_all, lse_all, [b[4:7] for b in blocks])
    k_ref, v_ref = use(k_in, v_in)
    keys, width = k_ref.shape
    block = keys // BACK_BLOCKS

    def emit(pair, n, at, here, grad_k, grad_v):
        dk[here, at] = grad_k.astype(BF)
        dv[here, at] = grad_v.astype(BF)

    attend_back(q_all, gm, o_all, lse_all, k_ref, v_ref, slice(0, start), keys,
                lambda first: tail_bias(block, real, True, first), dq, emit, block)
    flush(dk_o, dv_o)
    low_q = (dq[...].astype(BF).astype(F32) * 0.125).astype(BF)
    part[...] = low_q.astype(F32)
    high = start - cut
    for o, rows in ((lq_outs[0], slice(0, high)), (lq_outs[1], slice(high, start))):
        into(o)[...] = low_q[rows]
        flush(o)
    sums[3:4, 0:width] = column_sums(low_q.astype(F32))
    sums[3:4, width : 2 * width] = column_sums(dv[0:real].astype(F32))
    frames_sent(which, dk, dv, use(kv), outs[10:])


def frames_sent(which, lk, lv, w, outs):
    start, width = 0, outs[0].ref.shape[1]
    at = pl.ds(pl.multiple_of((1 - which[0]) * width, width), width)
    for drain in outs:
        out = into(drain)
        rows = slice(start, start + out.shape[0])
        out[...] = nt(lk[rows], w[0, at, :]) + nt(lv[rows], w[1, at, :])
        flush(drain)
        start = rows.stop


def frames_kept(ins, outs, scratch):
    which, lk, lv, w = use(*ins[:4])
    held, sem = scratch
    start, width = 0, held.shape[1]
    at = pl.ds(pl.multiple_of(which[0] * width, width), width)
    for other in ins[4:]:
        other = use(other)
        rows = slice(start, start + other.shape[0])
        held[rows] = nt(lk[rows], w[0, at, :]) + nt(lv[rows], w[1, at, :]) + other[...]
        start = rows.stop
    copy = pltpu.make_async_copy(held, outs[0].at[:, 0, :], sem)
    copy.start()
    copy.wait()


def self_back(cut, ins, outs, scratch):
    spot, mine, other, wq = ins[:4]
    pieces, (gains, wo, q_in, k_in, v_in, w, length) = ins[4:6], ins[6:13]
    blocks = (ins[13:17], ins[17:21])
    l3_outs, part_high, part_low, sums = outs[4:6], outs[6], outs[7], outs[8]
    gm, dq, wq_other, q_all, o_all, lse_all, lows = scratch
    l3_high, l3_low, part_high, part_low, sums = into(*l3_outs, part_high, part_low, sums)
    assemble(wq_other, spot, pieces)
    mine, other, wq = use(mine, other, wq)
    incoming = nt(mine[...].astype(BF), wq[...]) + nt(other[...].astype(BF), wq_other[...])
    start = 0
    for n, (s_in, g_in, out_in, lse) in enumerate(blocks):
        stop = start + out_in.target.shape[0]
        back_head(incoming[start:stop], (s_in, g_in), outs[2 * n : 2 * n + 2], gm.at[start:stop], gains, wo, sums, 1, n > 0)
        start = stop
    high = start - cut
    q_ref = use(q_in)
    q_all[0:high] = q_ref[cut:]
    q_all[high:] = q_ref[:cut]
    gather_heads(start, None, o_all, lse_all, [(b[2], b[2], b[3]) for b in blocks])
    k_ref, v_ref, w = use(k_in, v_in, w)
    width = k_ref.shape[1]
    lane = lax.broadcasted_iota(jnp.int32, (start, start), 1)
    query = jnp.where(lane < high, lane + cut, lane - high)
    key = lax.broadcasted_iota(jnp.int32, (start, start), 0)
    bias = jnp.where((key <= query) & (key < length[0]), 0.0, NEG).astype(F32)

    def emit(pair, n, at, here, grad_k, grad_v):
        lows[0, :, at] = grad_k.astype(BF)
        lows[1, :, at] = grad_v.astype(BF)

    attend_back(q_all, gm, o_all, lse_all, k_ref, v_ref, slice(0, start), start, lambda first: bias, dq, emit)
    low_q = (dq[...].astype(BF).astype(F32) * 0.125).astype(BF)
    l3_high[0], l3_low[0] = low_q[:high], low_q[high:]
    for n in range(2):
        l3_high[1 + n], l3_low[1 + n] = lows[n, cut:], lows[n, :cut]
    flush(*l3_outs)
    for l3, part in ((l3_low, part_low), (l3_high, part_high)):
        part[...] = nt(l3[0], w[0]) + nt(l3[1], w[1]) + nt(l3[2], w[2])
    sums[3:4, 0:width] = column_sums(low_q.astype(F32))
    sums[3:4, width : 2 * width] = column_sums(lows[1].astype(F32))


def tokens_end(rows, ins, outs, scratch):
    tok, gains, g, mine, other = use(*ins[:5])
    unit, scale = standard(tok[rows].astype(F32))
    incoming = mine[...] + other[...]
    grad = g[...] + norm_back(incoming, unit, scale, gains[0:1])
    gain, shift = column_sums(incoming * unit), column_sums(incoming)
    if len(ins) == 6:
        out, sums = into(*outs)
        out[...] = grad
        flush(outs[0])
        sums[0:1], sums[1:2] = gain, shift
        return
    out, total, y = into(*outs)
    earlier, first = use(*ins[5:7])
    sums, hid_sums, (y_low, y_high) = use(*ins[7:11]), use(*ins[11:13]), ins[13:15]
    out[rows] = grad
    out[rows.stop :] = earlier[...]
    flush(outs[0])
    y_low, y_high = use(y_low, y_high)
    y[0 : rows.stop] = y_low[...]
    y[rows.stop :] = y_high[...]
    flush(outs[2])
    total[0:1] = gain + first[0:1]
    total[4:5] = shift + first[1:2]
    for level, one in enumerate((sums[0][...], sums[1][...], sums[2][...] + sums[3][...])):
        total[1 + level : 2 + level] = one[0:1]
        total[5 + level : 6 + level] = one[1:2]
        total[8 + level : 9 + level] = one[2:3]
        if level < 2:
            total[11 + level : 12 + level] = one[3:4]
    model = total.shape[1]
    for piece in range(hid_sums[0].shape[1] // model):
        at = slice(piece * model, (piece + 1) * model)
        total[13 + piece : 14 + piece] = hid_sums[0][0:1, at] + hid_sums[1][0:1, at]


def small_end(ins, outs, scratch):
    mine, other = use(*ins)
    gain, shift, ob, svb, cvb, fb = into(*outs)
    total = mine[...] + other[...]
    half = svb.shape[1]
    gain[...] = total[0:4]
    shift[...] = total[4:8]
    ob[...] = total[8:11]
    for target, at in ((svb, 11), (cvb, 12)):
        target[0:1] = total[at : at + 1, :half]
        target[1:2] = total[at : at + 1, half:]
    fb[...] = total[13 : 13 + fb.shape[0]]


def grads_sent(plan, ins, outs, scratch):
    orders = ins[: 1 + max(place for place, _ in plan)]
    at, col = len(orders), 0
    out, turned = into(outs[0]), list(outs[1:])
    half = out.shape[0]
    for place, items in plan:
        for parts, ordered, blocks in items:
            lefts = ins[at : at + parts]
            at += parts
            made = []
            for left in lefts:
                left = use(left)
                if not ordered:
                    target = turned.pop(0)
                    ref = into(target)
                    ref[...] = nt(use(orders[place])[...], left[...]).astype(BF)
                    flush(target)
                    left = ref
                made.append(left)
            for block in blocks:
                total, width = None, 0
                for part in range(parts):
                    right = use(ins[at + part])
                    value = right[block] if len(right.shape) == 3 else right[...]
                    width = value.shape[-1]
                    term = nn(made[part][half:], value)
                    total = term if total is None else total + term
                out[:, col : col + width] = total
                col += width
            at += parts


def grads_kept(plan, ins, outs, scratch):
    other, at, col = use(ins[0]), 1, 0
    half = other.shape[0]
    for n, (place, items) in enumerate(plan):
        sent, kept = into(outs[2 * n], outs[2 * n + 1])
        low, start = kept.shape[0], col
        for parts, ordered, blocks in items:
            lefts = [use(i) for i in ins[at : at + parts]]
            at += parts
            for block in blocks:
                total = None
                for part in range(parts):
                    right = use(ins[at + part])
                    value = right[block] if len(right.shape) == 3 else right[...]
                    width = value.shape[-1]
                    term = nn(lefts[part][:half], value)
                    total = term if total is None else total + term
                total = total + other[:, col : col + width]
                sent[:, col - start : col - start + width] = total[low:]
                kept[:, col - start : col - start + width] = total[:low]
                col += width
            at += parts
        flush(outs[2 * n], outs[2 * n + 1])


def halve(ins, outs, scratch):
    for n in range(0, len(outs), 2):
        kept, other = use(*ins[n : n + 2])
        sent, out = into(*outs[n : n + 2])
        low = out.shape[0]
        out[...] = kept[0:low] + other[0:low]
        sent[...] = kept[low:] + other[low:]


def steps(chain, items, after=()):
    outs, args = [], []
    for h, n in items:
        half = shaped((h.kept[n].shape[0] // 2, h.columns[n]))
        outs += [(half, "v"), (half, "v")]
        args += [(h.kept[n], "v"), (h.other[n], "v")]
    made = chain(halve, outs, args, 0, "steps", after=after)
    for place, (h, n) in enumerate(items):
        h.kept[n] = made[2 * place + 1]
        h.swap(n, made[2 * place])


def ends(chain, items, shape):
    while items[0][0].bits[items[0][1]]:
        steps(chain, items)
    args = []
    for h, n in items:
        args += [(h.kept[n], "v"), (h.other[n], "v")]
    return chain(plain_end, [(shape, "v") for _ in items], args, 0, "ends")


def plain_end(ins, outs, scratch):
    for n, out in enumerate(outs):
        out[...] = use(ins[2 * n])[...] + use(ins[2 * n + 1])[...]


def cross_end(ins, outs, scratch):
    kept, other = use(*ins)
    own = outs[0].shape[1]
    out_grad, query_grad, key_value_grad = outs
    out_grad[...] = kept[:, :own] + other[:, :own]
    query_grad[...] = kept[:, own : 2 * own] + other[:, own : 2 * own]
    for n in range(2):
        at = slice((2 + n) * own, (3 + n) * own)
        key_value_grad[:, n, :] = kept[:, at] + other[:, at]


def self_end(ins, outs, scratch):
    kept, other = use(*ins)
    own = outs[0].shape[1]
    for n, out in enumerate(outs):
        at = slice(n * own, (n + 1) * own)
        out[...] = kept[:, at] + other[:, at]


def swap_mp(v):
    return lax.ppermute(v, "mp", [(0, 1), (1, 0)])


def swap_dp(v, bit, dp_size):
    return lax.ppermute(v, "dp", [(i, i ^ bit) for i in range(dp_size)])


def relative_source(width, bits):
    shard = width // (1 << len(bits))
    me = lax.axis_index("dp")
    place = jnp.arange(width, dtype=jnp.int32)
    block = place // shard
    owner = jnp.zeros_like(block)
    for step, bit in enumerate(bits):
        owner = owner + ((block >> (len(bits) - 1 - step)) & 1) * bit
    return (owner ^ me) * shard + place % shard


class Halving:
    def __init__(self, chain, orders, groups, dp_size, name):
        self.chain, self.groups, self.dp_size, self.name = chain, groups, dp_size, name
        self.plan = tuple(
            (place, tuple((len(lhs), ordered, blocks) for lhs, ordered, rhs, blocks in items)) for place, bits, items in groups
        )
        self.model = orders[0].shape[0]
        self.columns = [
            sum(rhs[0].shape[-1] * len(blocks) for lhs, ordered, rhs, blocks in items) for place, bits, items in groups
        ]
        orders = orders[: 1 + max(place for place, bits, items in groups)]
        args = [(order, "h") for order in orders]
        outs = [(shaped((self.model // 2, sum(self.columns))), "v")]
        for place, bits, items in groups:
            for lhs, ordered, rhs, blocks in items:
                args += [(p, "h") for p in lhs] + [(p, "h") for p in rhs]
                if not ordered:
                    outs += [(shaped(p.shape[::-1], BF), "h") for p in lhs]
        made = chain(partial(grads_sent, self.plan), outs, args, 0, name + "_sent")
        self.turned = list(made[1:])
        self.first = chain.swap_dp(made[0], groups[0][1][0], dp_size)
        self.bits = [list(bits[1:]) for place, bits, items in groups]
        self.kept, self.other = [None] * len(groups), [None] * len(groups)

    def swap(self, n, sent):
        self.other[n] = self.chain.swap_dp(sent, self.bits[n].pop(0), self.dp_size)

    def keep(self, after=()):
        args, outs = [(self.first, "v")], []
        turned = list(self.turned)
        for columns, (place, bits, items) in zip(self.columns, self.groups):
            for lhs, ordered, rhs, blocks in items:
                for p in lhs:
                    args.append((p if ordered else turned.pop(0), "h"))
                args += [(p, "h") for p in rhs]
            outs += [(shaped((self.model // 4, columns)), "v")] * 2
        made = self.chain(partial(grads_kept, self.plan), outs, args, 0, self.name + "_kept", after=after)
        for n in range(len(self.groups)):
            self.kept[n] = made[2 * n + 1]
            self.swap(n, made[2 * n])

    def step(self, n, after=()):
        half = shaped((self.kept[n].shape[0] // 2, self.columns[n]))
        sent, self.kept[n] = self.chain(
            halve, [(half, "v"), (half, "v")], [(self.kept[n], "v"), (self.other[n], "v")], 0, self.name + str(n) + "_step",
            after=after,
        )
        self.swap(n, sent)

    def end(self, n, finish, outs):
        while self.bits[n]:
            self.step(n)
        return self.chain(
            finish, [(o, "v") for o in outs], [(self.kept[n], "v"), (self.other[n], "v")], 0, self.name + str(n) + "_end"
        )


def on_device(
    dp_size,
    tokens,
    frames,
    lengths,
    out_cot,
    self_query_key_value,
    self_qv_bias,
    self_output_weight,
    cross_query_weight,
    cross_kv,
    cross_bias,
    cross_output_weight,
    first_dense_weight,
    first_dense_bias,
    second_dense_weight,
    out_biases,
    norm_gains,
    norm_biases,
):
    _, slot, model = tokens.shape
    tok, frames, cot = tokens[0], frames[0], out_cot[0]
    real = frames.shape[0]
    padded = -(-real // 256) * 256
    own = self_output_weight.shape[0]
    ff = second_dense_weight.shape[0]
    cut = slot // 2 // 64 * 64
    low_rows, high_rows = slice(0, cut), slice(cut, slot)
    w3 = self_query_key_value.transpose(1, 0, 2)
    w2kv = cross_kv.transpose(1, 0, 2)
    fb = first_dense_bias[None]
    gains, shifts, ob = norm_gains, norm_biases, out_biases
    bits = [1 << i for i in range(dp_size.bit_length() - 1)]
    turned_bits = bits[:1] + bits[2:] + bits[1:2]
    sources = jnp.stack([relative_source(model, bits), relative_source(model, turned_bits)], axis=1)
    chain = Chain(norm_gains)
    spot = (lax.axis_index("dp") & 3).astype(jnp.int32)
    spots = spot.reshape(1)

    def count(rows):
        return rows.stop - rows.start

    def sized(rows, width, dtype=F32):
        return shaped((count(rows), width), dtype)

    def attended(rows):
        return [(sized(rows, own, BF), "h"), (sized(rows, own), "h"), (shaped((8, count(rows))), "h"), (sized(rows, model), "v")]

    def fetched(weight, parts):
        block = weight.shape[0] // parts
        at = (spot & (parts - 1)) * block
        return swap_mp(lax.dynamic_slice_in_dim(weight, at, block, 0).astype(F32))

    made = chain(
        partial(self_start, cut),
        [(sized(low_rows, model, BF), "h"), (sized(high_rows, model, BF), "h")] + [(shaped((slot, own), BF), "h")] * 3
        + attended(high_rows),
        [(tok, "h"), (gains, "h"), (shifts, "h"), (self_qv_bias, "h"), (w3, "h"), (lengths, "s"), (self_output_weight, "h")],
        0,
        "self_start",
    )
    x1_l, x1_h, q1, k1, v1, mix1_h, out1_h, lse1_h, part1_h = made
    other1_h = chain.swap_mp(part1_h)
    mix1_l, out1_l, lse1_l, part1_l = chain(
        partial(self_next, low_rows),
        attended(low_rows),
        [(q1, "h"), (k1, "h"), (v1, "h"), (lengths, "s"), (self_output_weight, "h")],
        0,
        "self_next",
    )
    other1_l = chain.swap_mp(part1_l)
    k2, v2, turned_frames, order, order_turned = chain(
        frames_start,
        [(shaped((padded, own), BF), "h")] * 2 + [(shaped((model, padded), BF), "h")] + [(shaped((model, model), BF), "h")] * 2,
        [(frames, "h"), (w2kv, "h"), (cross_bias, "h"), (sources, "h")],
        0,
        "frames_start",
    )
    orders = (order, order_turned)

    def turned(plan, parts):
        used = orders[: 1 + max(place for place, _ in plan)]
        return chain(
            partial(turn, plan),
            [(shaped((model, parts[part].shape[0]), BF), "h") for _, part in plan],
            [(o, "h") for o in used] + [(p, "h") for p in parts],
            0,
            "turn",
        )


    def cross(rows, mine, other):
        return chain(
            partial(cross_start, rows, real),
            [(sized(rows, model), "h"), (sized(rows, model, BF), "h"), (sized(rows, own, BF), "h")] + attended(rows),
            [(mine, "v"), (other, "v"), (tok, "h"), (ob, "h"), (gains, "h"), (shifts, "h"), (cross_bias, "h"),
             (cross_query_weight, "h"), (k2, "h"), (v2, "h"), (cross_output_weight, "h")],
            0,
            "cross_start",
        )

    s1_h, x2_h, q2_h, mix2_h, out2_h, lse2_h, part2_h = cross(high_rows, part1_h, other1_h)
    other2_h = chain.swap_mp(part2_h)
    s1_l, x2_l, q2_l, mix2_l, out2_l, lse2_l, part2_l = cross(low_rows, part1_l, other1_l)
    other2_l = chain.swap_mp(part2_l)
    x1t_h, x1t_l, x2t_h, x2t_l = turned(((0, 0), (0, 1), (0, 2), (0, 3)), (x1_h, x1_l, x2_h, x2_l))

    def dense(rows, s1, mine, other):
        return chain(
            dense_start,
            [(sized(rows, model), "h"), (sized(rows, model, BF), "h"), (sized(rows, ff, BF), "h"), (sized(rows, ff), "h"),
             (sized(rows, model), "v")],
            [(mine, "v"), (other, "v"), (s1, "h"), (ob, "h"), (gains, "h"), (shifts, "h"), (fb, "h"),
             (first_dense_weight, "h"), (second_dense_weight, "h")],
            0,
            "dense_start",
        )

    s2_h, x3_h, act_h, slope_h, part3_h = dense(high_rows, s1_h, part2_h, other2_h)
    other3_h = chain.swap_mp(part3_h)
    s2_l, x3_l, act_l, slope_l, part3_l = dense(low_rows, s1_l, part2_l, other2_l)
    other3_l = chain.swap_mp(part3_l)
    x3o_h, x3o_l = turned(((1, 0), (1, 1)), (x3_h, x3_l))

    def dense_b(rows, s2, mine, other, slope):
        return chain(
            partial(dense_back, rows),
            [(sized(rows, model, BF), "h"), (sized(rows, model), "h"), (sized(rows, model, BF), "h"),
             (sized(rows, ff, BF), "h"), (sized(rows, model), "v"), (shaped((8, model)), "v"), (shaped((8, ff)), "v")],
            [(mine, "v"), (other, "v"), (s2, "h"), (ob, "h"), (gains, "h"), (shifts, "h"), (cot, "h"), (lengths, "s"),
             (second_dense_weight, "h"), (slope, "h"), (first_dense_weight, "h")],
            6 * count(rows) * model * ff,
            "dense_back",
        )

    y_h, g3_h, low3_h, hid_h, part4_h, sum3_h, hsum_h = dense_b(high_rows, s2_h, part3_h, other3_h, slope_h)
    other4_h = chain.swap_mp(part4_h)
    y_l, g3_l, low3_l, hid_l, part4_l, sum3_l, hsum_l = dense_b(low_rows, s2_l, part3_l, other3_l, slope_l)

    denses = Halving(
        chain,
        orders,
        [
            (0, bits, [((low3_h, low3_l), False, (act_h, act_l), (0,))]),
            (1, turned_bits, [((x3o_h, x3o_l), True, (hid_h, hid_l), (0,))]),
        ],
        dp_size,
        "dense",
    )
    other4_l = chain.swap_mp(chain.tie(part4_l))
    wq_0 = chain.later(lambda tied=chain.tie(cross_query_weight): fetched(tied, 2))
    chain.pause(other4_h)
    denses.keep()
    all_rows = slice(0, slot)

    def block_sizes(dtype, width):
        return [(sized(high_rows, width, dtype), "h"), (sized(low_rows, width, dtype), "h")]

    heads = [pltpu.VMEM((slot, own), BF), pltpu.VMEM((slot, own), F32)]
    joined = [pltpu.VMEM((slot, own), BF), pltpu.VMEM((slot, own), F32), pltpu.VMEM((8, slot), F32)]
    which = lax.axis_index("mp").astype(jnp.int32).reshape(1)
    half_width = model // 2
    cuts = [-(-real * n // (8 * PIECES)) * 8 for n in range(PIECES)] + [real]
    g2_h, low2_h, g2_l, low2_l, lq2_h, lq2_l, part5, sum2, lk2, lv2, *frames_parts = chain(
        partial(cross_back, cut, real),
        [(sized(high_rows, model), "h"), (sized(high_rows, model, BF), "h"), (sized(low_rows, model), "h"),
         (sized(low_rows, model, BF), "h")] + block_sizes(BF, own)
        + [(shaped((slot, own)), "v"), (shaped((8, model)), "v")] + [(shaped((padded, own), BF), "h")] * 2
        + [(shaped((cuts[n + 1] - cuts[n], half_width)), "h") for n in range(PIECES)],
        [(part4_h, "h"), (other4_h, "h"), (s2_h, "h"), (g3_h, "h"), (q2_h, "h"), (out2_h, "h"), (lse2_h, "h"),
         (part4_l, "h"), (other4_l, "h"), (s2_l, "h"), (g3_l, "h"), (q2_l, "h"), (out2_l, "h"), (lse2_l, "h"),
         (gains, "h"), (cross_output_weight, "h"), (k2, "h"), (v2, "h"), (which, "s"), (w2kv, "h")],
        0,
        "cross_back",
        scratch=heads + joined,
    )
    other5 = chain.swap_mp(part5)
    wq_1 = chain.later(lambda tied=chain.link: swap_dp(lax.optimization_barrier((wq_0.value, tied))[0], 1, dp_size))
    steps(chain, [(denses, 0), (denses, 1)], (wq_0,))
    crosses = Halving(
        chain,
        orders,
        [
            (
                0,
                bits,
                [
                    ((low2_h, low2_l), False, (mix2_h, mix2_l), (0,)),
                    ((x2t_h, x2t_l), True, (lq2_h, lq2_l), (0,)),
                    ((turned_frames,), True, (lk2,), (0,)),
                    ((turned_frames,), True, (lv2,), (0,)),
                ],
            )
        ],
        dp_size,
        "cross",
    )
    frames_other = [chain.swap_mp(chain.tie(frames_parts[0]))]
    chain.pause(other5)
    crosses.keep()
    frames_other.append(chain.swap_mp(chain.tie(frames_parts[1])))
    g1_h, low1_h, g1_l, low1_l, l3_h, l3_l, part6_h, part6_l, sum1 = chain(
        partial(self_back, cut),
        [(sized(high_rows, model), "h"), (sized(high_rows, model, BF), "h"), (sized(low_rows, model), "h"),
         (sized(low_rows, model, BF), "h"), (shaped((3, count(high_rows), own), BF), "h"),
         (shaped((3, count(low_rows), own), BF), "h"), (sized(high_rows, model), "v"), (sized(low_rows, model), "v"),
         (shaped((8, model)), "v")],
        [(spots, "s"), (part5, "h"), (other5, "h"), (cross_query_weight, "h"), (wq_0, "h"), (wq_1, "h"), (gains, "h"),
         (self_output_weight, "h"), (q1, "h"), (k1, "h"), (v1, "h"), (w3, "h"), (lengths, "s"),
         (s1_h, "h"), (g2_h, "h"), (out1_h, "h"), (lse1_h, "h"), (s1_l, "h"), (g2_l, "h"), (out1_l, "h"), (lse1_l, "h")],
        0,
        "self_back",
        scratch=heads + [pltpu.VMEM((model, own), BF)] + joined + [pltpu.VMEM((2, slot, own), BF)],
    )
    other6_h = chain.swap_mp(part6_h)
    steps(chain, [(denses, 0), (denses, 1)], (frames_other[0],))
    selves = Halving(
        chain,
        orders,
        [
            (
                0,
                bits,
                [((low1_h, low1_l), False, (mix1_h, mix1_l), (0,)), ((x1t_h, x1t_l), True, (l3_h, l3_l), (0,))],
            ),
            (0, bits, [((x1t_h, x1t_l), True, (l3_h, l3_l), (1, 2))]),
        ],
        dp_size,
        "self",
    )
    other6_l = chain.swap_mp(chain.tie(part6_l))
    shard = model // dp_size
    crosses.step(0, (frames_other[1],))
    t_high, sum0_h = chain(
        partial(tokens_end, high_rows),
        [(sized(high_rows, model), "h"), (shaped((8, model)), "h")],
        [(tok, "h"), (gains, "h"), (g1_h, "h"), (part6_h, "v"), (other6_h, "v"), (lengths, "s")],
        0,
        "tokens_end",
    )
    second_turned, first_grad = ends(chain, [(denses, 0), (denses, 1)], shaped((shard, ff)))
    selves.keep()
    tokens_grad, total, y = chain(
        partial(tokens_end, low_rows),
        [(shaped((slot, model)), "h"), (shaped((13 + ff // model, model)), "v"), (shaped((slot, model), BF), "h")],
        [(tok, "h"), (gains, "h"), (g1_l, "h"), (part6_l, "v"), (other6_l, "v"), (t_high, "h"), (sum0_h, "h"),
         (sum1, "h"), (sum2, "h"), (sum3_h, "h"), (sum3_l, "h"), (hsum_h, "h"), (hsum_l, "h"), (y_l, "h"), (y_h, "h")],
        0,
        "tokens_end",
    )
    small_bits = list(bits)

    def small_step(total, other):
        (total,) = chain(plain_end, [(shaped(total.shape), "v")], [(total, "v"), (other, "v")], 0, "small_step")
        return total, chain.swap_dp(total, small_bits.pop(0), dp_size)

    small_other = chain.swap_dp(total, small_bits.pop(0), dp_size)
    frames_other.append(chain.swap_mp(chain.tie(frames_parts[2])))
    crosses.step(0)
    selves.step(0)
    total, small_other = small_step(total, small_other)
    frames_other.append(chain.swap_mp(chain.tie(frames_parts[3])))
    selves.step(1, (frames_other[2],))
    cross_out_grad, cross_q_grad, cross_kv_grad = crosses.end(
        0, cross_end, [shaped((shard, own)), shaped((shard, own)), shaped((shard, 2, own))]
    )
    selves.step(0)
    total, small_other = small_step(total, small_other)
    selves.step(1)
    while small_bits:
        total, small_other = small_step(total, small_other)
    (frames_grad,) = chain(
        frames_kept, [(shaped((real, 1, half_width)), "r")],
        [(which, "s"), (lk2, "h"), (lv2, "h"), (w2kv, "h")] + [(o, "h") for o in frames_other],
        0, "frames_kept",
        scratch=[pltpu.VMEM((real, half_width), F32), pltpu.SemaphoreType.DMA],
    )
    self_out_grad, q_grad = selves.end(0, self_end, [shaped((shard, own))] * 2)
    k_grad, v_grad = selves.end(1, self_end, [shaped((shard, own))] * 2)
    gains_grad, shifts_grad, ob_grad, svb_grad, cvb_grad, fb_grad = chain(
        small_end,
        [(shaped((4, model)), "v"), (shaped((4, model)), "v"), (shaped((3, model)), "v"), (shaped((2, own)), "v"),
         (shaped((2, own)), "v"), (shaped((ff // model, model)), "v")],
        [(total, "v"), (small_other, "v")],
        0,
        "small_end",
    )
    return (
        y[None],
        tokens_grad[None],
        frames_grad.transpose(1, 0, 2),
        jnp.stack([q_grad, k_grad, v_grad], axis=1),
        svb_grad,
        self_out_grad.T,
        cross_q_grad,
        cross_kv_grad,
        cvb_grad,
        cross_out_grad.T,
        first_grad,
        fb_grad.reshape(ff),
        second_turned.T,
        ob_grad,
        gains_grad,
        shifts_grad,
    )


def solution(mesh):
    in_specs = (
        P("dp", None, None),
        P("dp", None, None),
        P("dp"),
        P("dp", None, None),
        P(None, None, "mp"),
        P(None, "mp"),
        P("mp", None),
        P(None, "mp"),
        P(None, None, "mp"),
        P(None, "mp"),
        P("mp", None),
        P(None, "mp"),
        P("mp"),
        P("mp", None),
        P(),
        P(),
        P(),
    )
    out_specs = (
        P("dp", None, None),
        P("dp", None, None),
        P("dp", None, "mp"),
        P("dp", None, "mp"),
        P(None, "mp"),
        P("mp", "dp"),
        P("dp", "mp"),
        P("dp", None, "mp"),
        P(None, "mp"),
        P("mp", "dp"),
        P("dp", "mp"),
        P("mp"),
        P("mp", "dp"),
        P(),
        P(),
        P(),
    )
    return jax.shard_map(
        partial(on_device, mesh.shape["dp"]),
        mesh=mesh,
        in_specs=in_specs,
        out_specs=out_specs,
        check_vma=False,
    )
```

```python
from functools import partial

import jax
import jax.numpy as jnp
from jax import lax
from jax.experimental import pallas as pl
from jax.experimental.pallas import tpu as pltpu
from jax.sharding import PartitionSpec as P

F32 = jnp.float32
BF = jnp.bfloat16
HEAD_DIM = 64
LANES = 128
NEG = -1e30
COST = {"self_start": 2.0, "self_next": 1.3, "turn": 1.0, "frames_start": 3.0, "cross_start": 2.7, "dense_start": 2.4,
        "dense_back": 2.4, "dense_sent": 6.0, "dense_kept": 6.0, "cross_back": 20.0, "self_back": 12.0,
        "cross_sent": 6.0, "cross_kept": 5.0, "self_sent": 5.0, "self_kept": 4.0, "tokens_end": 5.0, "frames_kept": 6.0,
        "small_end": 1.0, "pause": 8.0}
SCALE = 1.5e10
PIECES = 4
BACK_BLOCKS = 2
ROW_BLOCKS = 1
BYTES = 6.4e-3
PINNED = ("h", "t", "r")


def shaped(shape, dtype=F32):
    return jax.ShapeDtypeStruct(tuple(shape), dtype)


def dg(a, b, ca, cb):
    return lax.dot_general(a, b, (((ca,), (cb,)), ((), ())), preferred_element_type=F32)


def nn(a, b):
    return dg(a, b, 1, 0)


def nt(a, b):
    return dg(a, b, 1, 1)


def tn(a, b):
    return dg(a, b, 0, 0)


class Feed:
    def __init__(self, source, target, sem):
        self.copy = pltpu.make_async_copy(source, target, sem)
        self.copy.start()
        self.target = target
        self.pending = True

    def ready(self):
        if self.pending:
            self.copy.wait()
            self.pending = False
        return self.target


class Drain:
    def __init__(self, source, target, sem):
        self.ref = source
        self.copy = pltpu.make_async_copy(source, target, sem)
        self.pending = True

    def flush(self):
        if self.pending:
            self.copy.start()
            self.pending = False


def use(*inputs):
    made = [i.ready() if isinstance(i, Feed) else i for i in inputs]
    return made if len(made) > 1 else made[0]


def flush(*outputs):
    for o in outputs:
        if isinstance(o, Drain):
            o.flush()


def into(*outputs):
    made = [o.ref if isinstance(o, Drain) else o for o in outputs]
    return made if len(made) > 1 else made[0]


class Pending:
    def __init__(self, make):
        self.make, self.value = make, None


class Chain:
    def __init__(self, seed):
        self.link = seed
        self.pending = []

    def pause(self, *after):
        self(lambda ins, outs, scratch: None, [], [], 0, "pause", after=after)

    def later(self, make):
        self.pending.append(Pending(make))
        return self.pending[-1]

    def settle(self):
        for item in reversed(self.pending):
            item.value = item.make()
        self.pending = []

    def swap_mp(self, v):
        return self.later(lambda: swap_mp(v))

    def swap_dp(self, v, bit, dp_size):
        return self.later(lambda: swap_dp(v, bit, dp_size))

    def tie(self, value):
        return lax.optimization_barrier((value, self.link))[0]

    def __call__(self, kernel, outs, args, flops, name, scratch=(), after=()):
        place = {
            "v": pl.BlockSpec(memory_space=pltpu.VMEM),
            "h": pl.BlockSpec(memory_space=pltpu.HBM),
            "s": pl.BlockSpec(memory_space=pltpu.SMEM),
        }
        args = [(self.link, "t")] + [(a, "t") for a in after] + list(args)
        first = 1 + len(after)
        if any(isinstance(a, Pending) and a.value is None for a, _ in args):
            self.settle()
        args = [(a.value if isinstance(a, Pending) else a, k) for a, k in args]
        outs = [(shaped((8, LANES)), "t")] + list(outs)
        held = []
        for item, kind in args[first:] + outs[1:]:
            if kind == "h":
                held.append(pltpu.VMEM(item.shape, item.dtype))
        n_in, n_out = len(args), len(outs)

        def body(*refs):
            ins, results = refs[first:n_in], refs[n_in + 1 : n_in + n_out]
            rest = refs[n_in + n_out :]
            own, bufs, sems = rest[: len(scratch)], list(rest[len(scratch) : -1]), rest[-1]
            at = 0
            feeds, drains = [], []
            for ref, (_, kind) in zip(ins, args[first:]):
                if kind == "h":
                    feeds.append(Feed(ref, bufs[at], sems.at[at]))
                    at += 1
                else:
                    feeds.append(ref)
            for ref, (_, kind) in zip(results, outs[1:]):
                if kind == "h":
                    drains.append(Drain(bufs[at], ref, sems.at[at]))
                    at += 1
                else:
                    drains.append(ref)
            kernel(feeds, drains, own)
            for feed in feeds:
                use(feed)
            flush(*drains)
            for d in drains:
                if isinstance(d, Drain):
                    d.copy.wait()

        moved = 0
        for item, kind in args + outs:
            size = jnp.dtype(item.dtype).itemsize
            for d in item.shape:
                size *= d
            moved += size
        place["t"] = place["r"] = place["h"]
        made = pl.pallas_call(
            body,
            out_shape=tuple(pltpu.HBM(o.shape, o.dtype) if k in PINNED else o for o, k in outs),
            in_specs=[place[k] for _, k in args],
            out_specs=tuple(place[k] for _, k in outs),
            scratch_shapes=list(scratch) + held + [pltpu.SemaphoreType.DMA((max(1, len(held)),))],
            compiler_params=pltpu.CompilerParams(vmem_limit_bytes=28 * 1024 * 1024),
            cost_estimate=pl.CostEstimate(flops=int(COST.get(name, 1.0) * SCALE), transcendentals=0, bytes_accessed=int(COST.get(name, 1.0) * SCALE * BYTES)),
            name=name,
        )(*[pltpu.with_memory_space_constraint(a, pltpu.HBM) if k in PINNED else a for a, k in args])
        self.link = made[0]
        return made[1:]


def standard(stream):
    centred = stream - jnp.mean(stream, axis=1, keepdims=True)
    spread = jnp.mean(centred * centred, axis=1, keepdims=True)
    scale = lax.rsqrt(spread + 1e-05)
    return centred * scale, scale


def norm_back(grad, unit, scale, gain):
    lifted = grad * gain
    mean_plain = jnp.mean(lifted, axis=1, keepdims=True)
    mean_cross = jnp.mean(lifted * unit, axis=1, keepdims=True)
    return scale * (lifted - mean_plain - unit * mean_cross)


def column_sums(values):
    return jnp.sum(values, axis=0, keepdims=True)


def head_lanes(which):
    lane = lax.broadcasted_iota(jnp.int32, (1, LANES), 1)
    return (lane < HEAD_DIM) if which == 0 else (lane >= HEAD_DIM)


def only(mask, values):
    return jnp.where(mask, values, jnp.zeros_like(values))


def pair_slice(pair):
    return pl.ds(pl.multiple_of(pair * LANES, LANES), LANES)


def attend_rows(q_ref, k_ref, v_ref, rows, keys, bias, mixed_ref, out_ref, lse_ref, lse_all, blocks):
    lane = lax.broadcasted_iota(jnp.int32, (1, LANES), 1)
    size = (rows.stop - rows.start) // blocks

    def body(step, carry):
        pair, part = (step, 0) if blocks == 1 else (step // blocks, step % blocks)
        at = pair_slice(pair)
        here = place(part, size) if blocks > 1 else slice(0, size)
        theirs = pl.ds(pl.multiple_of(rows.start + part * size, 16), size) if blocks > 1 else rows
        k_pair, v_pair, q_pair = k_ref[0:keys, at], v_ref[0:keys, at], q_ref[theirs, at]
        result, lse = None, lse_all[here]
        for which in range(2):
            mask = head_lanes(which)
            scores = nt(only(mask, q_pair), k_pair) + bias(part * size, size)
            top = jnp.max(scores, axis=1, keepdims=True)
            raised = jnp.exp(scores - top)
            total = jnp.sum(raised, axis=1, keepdims=True)
            value = nn(raised.astype(BF), v_pair) * (1.0 / total)
            result = value if which == 0 else jnp.where(mask, value, result)
            lse = jnp.where(lane == 2 * pair + which, top + jnp.log(total), lse)
        lse_all[here] = lse
        out_ref[here, at] = result
        mixed_ref[here, at] = result.astype(BF)
        return carry

    lse_all[...] = jnp.zeros_like(lse_all)
    lax.fori_loop(0, q_ref.shape[1] // LANES * blocks, body, 0)
    lse_ref[...] = lse_all[...].T[0 : lse_ref.shape[0]]


def attend_back(q_ref, g_ref, o_ref, lse_ref, k_ref, v_ref, rows, keys, bias, dq_ref, emit, block=None):
    block = keys if block is None else block
    blocks = keys // block

    def body(step, carry):
        pair, part = (step, 0) if blocks == 1 else (step // blocks, step % blocks)
        at = pair_slice(pair)
        here = pl.ds(0, keys) if blocks == 1 else pl.ds(pl.multiple_of(part * block, block), block)
        k_pair, v_pair = k_ref[here, at], v_ref[here, at]
        q_pair, g_pair = q_ref[rows, at], g_ref[:, at]
        product = (g_pair.astype(F32) * o_ref[:, at]).T
        k_turned = k_pair.T
        parts, grad_k, grad_v = [], None, None
        for which in range(2):
            mask = head_lanes(which)
            q_head, g_head = only(mask, q_pair), only(mask, g_pair)
            inner = column_sums(product[which * HEAD_DIM : (which + 1) * HEAD_DIM])
            scores = nt(k_pair, q_head) + bias(part * block)
            probs = jnp.exp(scores - lse_ref[pl.ds(2 * pair + which, 1), :])
            grad_probs = nt(v_pair, g_head)
            grad_scores = (probs * (grad_probs - inner)).astype(BF)
            here_v = nn(probs.astype(BF), g_head)
            here_k = nn(grad_scores, q_head)
            grad_v = here_v if which == 0 else grad_v + here_v
            grad_k = here_k if which == 0 else grad_k + here_k
            parts.append(nn(k_turned[which * HEAD_DIM : (which + 1) * HEAD_DIM], grad_scores))
        emit(pair, part, at, here, grad_k, grad_v)
        grad_q = jnp.concatenate(parts, axis=0).T
        if blocks == 1:
            dq_ref[:, at] = grad_q
        else:
            dq_ref[:, at] += grad_q
        return carry

    if blocks > 1:
        dq_ref[...] = jnp.zeros_like(dq_ref)
    lax.fori_loop(0, q_ref.shape[1] // LANES * blocks, body, 0)


def causal_bias(start, count, keys, length):
    shape = (count, keys)
    query = lax.broadcasted_iota(jnp.int32, shape, 0) + start
    key = lax.broadcasted_iota(jnp.int32, shape, 1)
    return jnp.where((key <= query) & (key < length), 0.0, NEG).astype(F32)


def tail_bias(keys, real, turned, start=0):
    shape = (keys, 1) if turned else (1, keys)
    key = lax.broadcasted_iota(jnp.int32, shape, 0 if turned else 1) + start
    return jnp.where(key < real, 0.0, NEG).astype(F32)


def place(step, size):
    return pl.ds(pl.multiple_of(step * size, size), size)


def by_rows(count, work):
    size = count // 2

    def body(step, carry):
        work(place(step, size))
        return carry

    lax.fori_loop(0, count // size, body, 0)


def ordered(out, order, left):
    size = 2 * LANES

    def body(step, carry):
        out[place(step, size)] = nt(order[place(step, size)], left[...]).astype(BF)
        return carry

    lax.fori_loop(0, order.shape[0] // size, body, 0)


def self_start(cut, ins, outs, scratch):
    tok, gains, shifts, vb, w, length, wo = ins
    x_lo, x_hi, q_o, k_o, v_o = outs[:5]
    rows = slice(cut, tok.target.shape[0])
    low_ref, high_ref, q_ref, k_ref, v_ref = into(*outs[:5])
    tok, gains, shifts, vb, w = use(tok, gains, shifts, vb, w)
    x_all, size = scratch[1], tok.shape[0] // 2

    def work(here):
        unit, _ = standard(tok[here].astype(F32))
        x_all[here] = (unit * gains[0:1] + shifts[0:1]).astype(BF)

    by_rows(tok.shape[0], work)

    def body(step, carry):
        here = place(step, size)
        x = x_all[here]
        q_ref[here] = ((nn(x, w[0]) + vb[0:1]) * 0.125).astype(BF)
        k_ref[here] = nn(x, w[1]).astype(BF)
        v_ref[here] = (nn(x, w[2]) + vb[1:2]).astype(BF)
        return carry

    lax.fori_loop(0, 2, body, 0)
    low_ref[...] = x_all[:cut]
    high_ref[...] = x_all[cut:]
    flush(x_lo, x_hi, q_o, k_o, v_o)
    self_rows(rows, q_ref, k_ref, v_ref, length, wo, outs[5:], scratch)


def self_next(rows, ins, outs, scratch):
    q_ref, k_ref, v_ref, length, wo = ins
    self_rows(rows, *use(q_ref, k_ref, v_ref), length, wo, outs, scratch)


def self_rows(rows, q_ref, k_ref, v_ref, length, wo, outs, scratch):
    def bias(start, size):
        return causal_bias(rows.start + start, size, rows.stop, length[0])

    mixed, out, lse, part = into(*outs)
    attend_rows(q_ref, k_ref, v_ref, rows, rows.stop, bias, mixed, out, lse, scratch[0], 1)
    flush(*outs[:3])
    part[...] = nn(mixed[...], use(wo)[...])


def turn(plan, ins, outs, scratch):
    orders = ins[: 1 + max(which for which, _ in plan)]
    parts = ins[len(orders) :]
    for (which, part), out in zip(plan, outs):
        ordered(into(out), use(orders[which]), use(parts[part]))
        flush(out)


def frames_start(ins, outs, scratch):
    frames, w, vb, sources = ins
    k_o, v_o, t_o, order_o, other_o = outs
    k_ref, v_ref, t_ref, order, other = into(*outs)
    (frames_all,) = scratch
    sources = use(sources)
    column = lax.broadcasted_iota(jnp.int32, order.shape, 1)
    order[...] = jnp.where(column == sources[:, 0:1], 1.0, 0.0).astype(BF)
    other[...] = jnp.where(column == sources[:, 1:2], 1.0, 0.0).astype(BF)
    flush(order_o, other_o)
    real, padded = frames.target.shape[0], k_ref.shape[0]
    if padded > real:
        low = real // 16 * 16
        frames_all[low:padded] = jnp.zeros((padded - low, frames_all.shape[1]), BF)
    frames, w, vb = use(frames, w, vb)
    frames_all[0:real] = frames[...]
    size = padded // 3

    def body(step, carry):
        rows = frames_all[place(step, size)]
        k_ref[place(step, size)] = nn(rows, w[0]).astype(BF)
        v_ref[place(step, size)] = (nn(rows, w[1]) + vb[1:2]).astype(BF)
        t_ref[:, place(step, size)] = nt(order[...], rows).astype(BF)
        return carry

    lax.fori_loop(0, 3, body, 0)


def assemble(out, spot, pieces):
    block = out.shape[0] // len(pieces)
    for j, piece in enumerate(pieces):
        at = pl.multiple_of(((spot[0] & (len(pieces) - 1)) ^ j) * block, 16)
        out[pl.ds(at, block), :] = use(piece)[...].astype(BF)


def cross_start(rows, real, ins, outs, scratch):
    mine, other, tok, ob, gains, shifts, vb, wq, k_in, v_in, wo = ins
    s_o, x_o, q_o, m_o, out_o, lse_o, part = outs
    mixed, out, lse, part = into(m_o, out_o, lse_o, part)
    s_ref, x_ref, q_ref = into(s_o, x_o, q_o)
    mine, other, tok, ob, gains, shifts = use(mine, other, tok, ob, gains, shifts)
    block = tok.at[rows]

    def work(here):
        stream = block[here].astype(F32) + (mine[here] + other[here]) + ob[0:1]
        s_ref[here] = stream
        unit, _ = standard(stream)
        x_ref[here] = (unit * gains[1:2] + shifts[1:2]).astype(BF)

    by_rows(s_ref.shape[0], work)
    flush(s_o)
    vb, wq = use(vb, wq)
    q_ref[...] = ((nn(x_ref[...], wq[...]) + vb[0:1]) * 0.125).astype(BF)
    flush(x_o, q_o)
    k_ref, v_ref = use(k_in, v_in)
    keys = k_ref.shape[0]
    tail = tail_bias(keys, real, False)
    attend_rows(q_ref, k_ref, v_ref, slice(0, x_ref.shape[0]), keys, lambda start, size: tail, mixed, out, lse, scratch[0], ROW_BLOCKS)
    flush(m_o, out_o, lse_o)
    part[...] = nn(mixed[...], use(wo)[...])


def dense_start(ins, outs, scratch):
    mine, other, s_in, ob, gains, shifts, fb, w1, w2 = ins
    s_o, x_o, a_o, d_o, part = outs
    s_ref, x_ref, active, slope, part = into(s_o, x_o, a_o, d_o, part)
    mine, other, s_in, ob, gains, shifts = use(mine, other, s_in, ob, gains, shifts)
    def work(here):
        stream = s_in[here] + (mine[here] + other[here]) + ob[1:2]
        s_ref[here] = stream
        unit, _ = standard(stream)
        x_ref[here] = (unit * gains[2:3] + shifts[2:3]).astype(BF)

    by_rows(s_ref.shape[0], work)
    flush(s_o, x_o)
    fb, w1, w2 = use(fb, w1, w2)
    wide = 3 * LANES

    def body(step, carry):
        at = pl.ds(pl.multiple_of(step * wide, wide), wide)
        hidden = nn(x_ref[...], w1[:, at]) + fb[:, at]
        below = 0.5 + 0.5 * lax.erf(hidden * 0.7071067811865476)
        slope[:, at] = below + hidden * (0.3989422804014327 * jnp.exp(-0.5 * hidden * hidden))
        value = (hidden * below).astype(BF)
        active[:, at] = value
        part[...] += nn(value, w2[at, :])
        return carry

    part[...] = jnp.zeros_like(part)
    lax.fori_loop(0, w1.shape[1] // wide, body, 0)


def dense_back(rows, ins, outs, scratch):
    mine, other, s_in, ob, gains, shifts, cot, length, w2, slope, w1 = ins
    y_o, g_o, low_o, hid_o, part, sums, hid_sums = outs
    out_ref, g_ref, low_ref, hid_ref, part, sums, hid_sums = into(*outs)
    mine, other, s_in, ob, gains, shifts = use(mine, other, s_in, ob, gains, shifts)
    block = use(cot).at[rows]
    sums[0:3] = jnp.zeros((3, sums.shape[1]), F32)

    def work(here):
        stream = s_in[here] + (mine[here] + other[here]) + ob[2:3]
        unit, scale = standard(stream)
        row = lax.broadcasted_iota(jnp.int32, (stream.shape[0], 1), 0) + (rows.start + here.start)
        valid = (row < length[0]).astype(F32)
        out_ref[here] = ((unit * gains[3:4] + shifts[3:4]) * valid).astype(BF)
        incoming = block[here].astype(F32) * valid
        grad = norm_back(incoming, unit, scale, gains[3:4])
        g_ref[here] = grad
        low_ref[here] = grad.astype(BF)
        sums[0:1] += column_sums(incoming * unit)
        sums[1:2] += column_sums(incoming)
        sums[2:3] += column_sums(grad)

    by_rows(g_ref.shape[0], work)
    flush(y_o, g_o, low_o)
    w2, slope, w1 = use(w2, slope, w1)
    wide = 3 * LANES

    def body(step, carry):
        at = pl.ds(pl.multiple_of(step * wide, wide), wide)
        low = (slope[:, at] * nt(low_ref[...], w2[at, :])).astype(BF)
        hid_ref[:, at] = low
        hid_sums[0:1, at] = column_sums(low.astype(F32))
        part[...] += nt(low, w1[:, at])
        return carry

    part[...] = jnp.zeros_like(part)
    lax.fori_loop(0, w1.shape[1] // wide, body, 0)


def back_head(incoming_at, ins, outs, gm, gains, wo, sums, level, more):
    s_in, g_in = ins
    g_o, low_o = outs
    g_ref, low_ref = into(g_o, low_o)
    s_in, g_in, gains = use(s_in, g_in, gains)
    if not more:
        sums[0:3] = jnp.zeros((3, sums.shape[1]), F32)

    def work(here):
        incoming = incoming_at(here)
        unit, scale = standard(s_in[here])
        grad = g_in[here] + norm_back(incoming, unit, scale, gains[level : level + 1])
        g_ref[here] = grad
        low_ref[here] = grad.astype(BF)
        sums[0:1] += column_sums(incoming * unit)
        sums[1:2] += column_sums(incoming)
        sums[2:3] += column_sums(grad)

    by_rows(g_ref.shape[0], work)
    flush(g_o, low_o)
    gm[...] = nt(low_ref[...], use(wo)[...]).astype(BF)


def gather_heads(count, q_all, o_all, lse_all, refs):
    start = 0
    for q_ref, out_in, lse in refs:
        q_ref, out_in, lse = use(q_ref, out_in, lse)
        stop = start + out_in.shape[0]
        if q_all is not None:
            q_all[start:stop] = q_ref[...]
        o_all[start:stop] = out_in[...]
        lse_all[:, start:stop] = lse[...]
        start = stop


def cross_back(cut, real, ins, outs, scratch):
    blocks = (ins[:7], ins[7:14])
    gains, wo, k_in, v_in, which, kv = ins[14:20]
    lq_outs, part, sums, dk_o, dv_o = outs[4:6], outs[6], outs[7], outs[8], outs[9]
    gm, dq, q_all, o_all, lse_all, held, frame_sems = scratch
    part, sums, dk, dv = into(part, sums, dk_o, dv_o)
    start = 0
    for n, (mine, other, s_in, g_in, q_ref, out_in, lse) in enumerate(blocks):
        mine, other = use(mine, other)
        stop = start + mine.shape[0]
        back_head(lambda here, mine=mine, other=other: mine[here] + other[here], (s_in, g_in), outs[2 * n : 2 * n + 2], gm.at[start:stop], gains, wo, sums, 2, n > 0)
        start = stop
    gather_heads(start, q_all, o_all, lse_all, [b[4:7] for b in blocks])
    k_ref, v_ref = use(k_in, v_in)
    keys, width = k_ref.shape
    block = keys // BACK_BLOCKS

    def emit(pair, n, at, here, grad_k, grad_v):
        dk[here, at] = grad_k.astype(BF)
        dv[here, at] = grad_v.astype(BF)

    attend_back(q_all, gm, o_all, lse_all, k_ref, v_ref, slice(0, start), keys,
                lambda first: tail_bias(block, real, True, first), dq, emit, block)
    flush(dk_o, dv_o)
    low_q = (dq[...].astype(BF).astype(F32) * 0.125).astype(BF)
    part[...] = low_q.astype(F32)
    high = start - cut
    for o, rows in ((lq_outs[0], slice(0, high)), (lq_outs[1], slice(high, start))):
        into(o)[...] = low_q[rows]
        flush(o)
    sums[3:4, 0:width] = column_sums(low_q.astype(F32))
    sums[3:4, width : 2 * width] = column_sums(dv[0:real].astype(F32))
    width = held.shape[1]
    frames_terms(held, dk, dv, use(kv), pl.ds(pl.multiple_of((1 - which[0]) * width, width), width))
    start, copies = 0, []
    for n, out in enumerate(outs[10:]):
        copies.append(pltpu.make_async_copy(held.at[start : start + out.shape[0]], out, frame_sems.at[n]))
        copies[n].start()
        start += out.shape[0]
    for copy in copies:
        copy.wait()


def frames_terms(held, lk, lv, w, at):
    size = lk.shape[0] // 3

    def body(step, carry):
        rows = place(step, size)
        held[rows] = nt(lk[rows], w[0, at, :]) + nt(lv[rows], w[1, at, :])
        return carry

    lax.fori_loop(0, 3, body, 0)


def frames_kept(ins, outs, scratch):
    which, lk, lv, w = use(*ins[:4])
    held, final, sem = scratch
    start, width = 0, held.shape[1]
    frames_terms(held, lk, lv, w, pl.ds(pl.multiple_of(which[0] * width, width), width))
    for other in ins[4:]:
        other = use(other)
        rows = slice(start, min(start + other.shape[0], final.shape[0]))
        final[rows] = held[rows] + other[0 : rows.stop - start]
        start = rows.stop
    copy = pltpu.make_async_copy(final, outs[0].at[:, 0, :], sem)
    copy.start()
    copy.wait()


def self_back(cut, ins, outs, scratch):
    spot, mine, other, wq = ins[:4]
    pieces, (gains, wo, q_in, k_in, v_in, w, length) = ins[4:6], ins[6:13]
    blocks = (ins[13:17], ins[17:21])
    l3_outs, part_high, part_low, sums = outs[4:6], outs[6], outs[7], outs[8]
    gm, dq, wq_other, q_all, o_all, lse_all, lows, incoming = scratch
    l3_high, l3_low, part_high, part_low, sums = into(*l3_outs, part_high, part_low, sums)
    assemble(wq_other, spot, pieces)
    mine, other, wq = use(mine, other, wq)
    incoming[...] = nt(mine[...].astype(BF), wq[...]) + nt(other[...].astype(BF), wq_other[...])
    start = 0
    for n, (s_in, g_in, out_in, lse) in enumerate(blocks):
        stop = start + out_in.target.shape[0]
        block = incoming.at[start:stop]
        back_head(lambda here, block=block: block[here], (s_in, g_in), outs[2 * n : 2 * n + 2], gm.at[start:stop], gains, wo, sums, 1, n > 0)
        start = stop
    high = start - cut
    q_ref = use(q_in)
    q_all[0:high] = q_ref[cut:]
    q_all[high:] = q_ref[:cut]
    gather_heads(start, None, o_all, lse_all, [(b[2], b[2], b[3]) for b in blocks])
    k_ref, v_ref, w = use(k_in, v_in, w)
    width = k_ref.shape[1]
    block = start // 2

    def bias(first):
        lane = lax.broadcasted_iota(jnp.int32, (block, start), 1)
        query = jnp.where(lane < high, lane + cut, lane - high)
        key = lax.broadcasted_iota(jnp.int32, (block, start), 0) + first
        return jnp.where((key <= query) & (key < length[0]), 0.0, NEG).astype(F32)

    def emit(pair, n, at, here, grad_k, grad_v):
        lows[0, here, at] = grad_k.astype(BF)
        lows[1, here, at] = grad_v.astype(BF)

    attend_back(q_all, gm, o_all, lse_all, k_ref, v_ref, slice(0, start), start, bias, dq, emit, block)
    low_q = (dq[...].astype(BF).astype(F32) * 0.125).astype(BF)
    l3_high[0], l3_low[0] = low_q[:high], low_q[high:]
    for n in range(2):
        l3_high[1 + n], l3_low[1 + n] = lows[n, cut:], lows[n, :cut]
    flush(*l3_outs)
    for l3, part in ((l3_low, part_low), (l3_high, part_high)):
        part[...] = nt(l3[0], w[0]) + nt(l3[1], w[1]) + nt(l3[2], w[2])
    sums[3:4, 0:width] = column_sums(low_q.astype(F32))
    sums[3:4, width : 2 * width] = column_sums(lows[1].astype(F32))


def tokens_end(rows, ins, outs, scratch):
    tok, gains, g, mine, other = use(*ins[:5])
    block, (both,) = tok.at[rows], scratch
    target = into(outs[0]) if len(ins) == 6 else into(outs[0]).at[rows]
    both[...] = jnp.zeros_like(both)

    def work(here):
        unit, scale = standard(block[here].astype(F32))
        incoming = mine[here] + other[here]
        target[here] = g[here] + norm_back(incoming, unit, scale, gains[0:1])
        both[0:1] += column_sums(incoming * unit)
        both[1:2] += column_sums(incoming)

    by_rows(target.shape[0], work)
    if len(ins) == 6:
        flush(outs[0])
        into(outs[1])[...] = both[...]
        return
    out, total, y = into(*outs)
    gain, shift = both[0:1], both[1:2]
    earlier, first = use(*ins[5:7])
    sums, hid_sums, (y_low, y_high) = use(*ins[7:11]), use(*ins[11:13]), ins[13:15]
    out[rows.stop :] = earlier[...]
    flush(outs[0])
    y_low, y_high = use(y_low, y_high)
    y[0 : rows.stop] = y_low[...]
    y[rows.stop :] = y_high[...]
    flush(outs[2])
    total[0:1] = gain + first[0:1]
    total[4:5] = shift + first[1:2]
    for level, one in enumerate((sums[0][...], sums[1][...], sums[2][...] + sums[3][...])):
        total[1 + level : 2 + level] = one[0:1]
        total[5 + level : 6 + level] = one[1:2]
        total[8 + level : 9 + level] = one[2:3]
        if level < 2:
            total[11 + level : 12 + level] = one[3:4]
    model = total.shape[1]
    for piece in range(hid_sums[0].shape[1] // model):
        at = slice(piece * model, (piece + 1) * model)
        total[13 + piece : 14 + piece] = hid_sums[0][0:1, at] + hid_sums[1][0:1, at]


def small_end(ins, outs, scratch):
    mine, other = use(*ins)
    gain, shift, ob, svb, cvb, fb = into(*outs)
    total = mine[...] + other[...]
    half = svb.shape[1]
    gain[...] = total[0:4]
    shift[...] = total[4:8]
    ob[...] = total[8:11]
    for target, at in ((svb, 11), (cvb, 12)):
        target[0:1] = total[at : at + 1, :half]
        target[1:2] = total[at : at + 1, half:]
    fb[...] = total[13 : 13 + fb.shape[0]]


def blocks_of(rights, blocks, put):
    first = rights[0]
    if len(first.shape) == 3:
        low, wide = blocks[0], first.shape[2]

        def body(step, carry):
            put(step * wide, [r[low + step] for r in rights])
            return carry

        if len(blocks) == 1:
            body(0, 0)
        else:
            lax.fori_loop(0, len(blocks), body, 0)
        return len(blocks) * first.shape[2]
    put(0, [r[...] for r in rights])
    return first.shape[1]


def columns_at(start, width):
    return pl.ds(start if isinstance(start, int) else pl.multiple_of(start, LANES), width)


def grads_sent(plan, ins, outs, scratch):
    orders = ins[: 1 + max(which for which, _ in plan)]
    at, col = len(orders), 0
    out, turned = into(outs[0]), list(outs[1:])
    half = out.shape[0]
    for which, items in plan:
        for parts, done, blocks in items:
            lefts = ins[at : at + parts]
            at += parts
            made = []
            for left in lefts:
                left = use(left)
                if not done:
                    target = turned.pop(0)
                    ordered(into(target), use(orders[which]), left)
                    flush(target)
                    left = into(target)
                made.append(left)
            rights = [use(i) for i in ins[at : at + parts]]
            at += parts

            def put(start, values, col=col, made=made):
                total = None
                for left, value in zip(made, values):
                    term = nn(left[half:], value)
                    total = term if total is None else total + term
                out[:, columns_at(col + start, total.shape[1])] = total

            col += blocks_of(rights, blocks, put)


def grads_kept(plan, ins, outs, scratch):
    other, at, col = use(ins[0]), 1, 0
    half = other.shape[0]
    for n, (which, items) in enumerate(plan):
        sent, kept = into(outs[2 * n], outs[2 * n + 1])
        low, start = kept.shape[0], col
        for parts, done, blocks in items:
            lefts = [use(i) for i in ins[at : at + parts]]
            at += parts
            rights = [use(i) for i in ins[at : at + parts]]
            at += parts

            def put(first, values, col=col, lefts=lefts, sent=sent, kept=kept, start=start):
                total = None
                for left, value in zip(lefts, values):
                    term = nn(left[:half], value)
                    total = term if total is None else total + term
                width = total.shape[1]
                total = total + other[:, columns_at(col + first, width)]
                here = columns_at(col - start + first, width)
                sent[:, here] = total[low:]
                kept[:, here] = total[:low]

            col += blocks_of(rights, blocks, put)
        flush(outs[2 * n], outs[2 * n + 1])


def halve(ins, outs, scratch):
    for n in range(0, len(outs), 2):
        kept, other = use(*ins[n : n + 2])
        sent, out = into(*outs[n : n + 2])
        low = out.shape[0]
        out[...] = kept[0:low] + other[0:low]
        sent[...] = kept[low:] + other[low:]


def steps(chain, items, after=()):
    outs, args = [], []
    for h, n in items:
        half = shaped((h.kept[n].shape[0] // 2, h.columns[n]))
        outs += [(half, "v"), (half, "v")]
        args += [(h.kept[n], "v"), (h.other[n], "v")]
    made = chain(halve, outs, args, 0, "steps", after=after)
    for place, (h, n) in enumerate(items):
        h.kept[n] = made[2 * place + 1]
        h.swap(n, made[2 * place])


def ends(chain, items, shape):
    while items[0][0].bits[items[0][1]]:
        steps(chain, items)
    args = []
    for h, n in items:
        args += [(h.kept[n], "v"), (h.other[n], "v")]
    return chain(plain_end, [(shape, "v") for _ in items], args, 0, "ends")


def plain_end(ins, outs, scratch):
    for n, out in enumerate(outs):
        out[...] = use(ins[2 * n])[...] + use(ins[2 * n + 1])[...]


def cross_end(ins, outs, scratch):
    kept, other = use(*ins)
    own = outs[0].shape[1]
    out_grad, query_grad, key_value_grad = outs
    out_grad[...] = kept[:, :own] + other[:, :own]
    query_grad[...] = kept[:, own : 2 * own] + other[:, own : 2 * own]
    for n in range(2):
        at = slice((2 + n) * own, (3 + n) * own)
        key_value_grad[:, n, :] = kept[:, at] + other[:, at]


def self_end(ins, outs, scratch):
    kept, other = use(*ins)
    own = outs[0].shape[1]
    for n, out in enumerate(outs):
        at = slice(n * own, (n + 1) * own)
        out[...] = kept[:, at] + other[:, at]


def swap_mp(v):
    return lax.ppermute(v, "mp", [(0, 1), (1, 0)])


def swap_dp(v, bit, dp_size):
    return lax.ppermute(v, "dp", [(i, i ^ bit) for i in range(dp_size)])


def relative_source(width, bits):
    shard = width // (1 << len(bits))
    me = lax.axis_index("dp")
    place = jnp.arange(width, dtype=jnp.int32)
    block = place // shard
    owner = jnp.zeros_like(block)
    for step, bit in enumerate(bits):
        owner = owner + ((block >> (len(bits) - 1 - step)) & 1) * bit
    return (owner ^ me) * shard + place % shard


class Halving:
    def __init__(self, chain, orders, groups, dp_size, name):
        self.chain, self.groups, self.dp_size, self.name = chain, groups, dp_size, name
        self.plan = tuple(
            (place, tuple((len(lhs), ordered, blocks) for lhs, ordered, rhs, blocks in items)) for place, bits, items in groups
        )
        self.model = orders[0].shape[0]
        self.columns = [
            sum(rhs[0].shape[-1] * len(blocks) for lhs, ordered, rhs, blocks in items) for place, bits, items in groups
        ]
        orders = orders[: 1 + max(place for place, bits, items in groups)]
        args = [(order, "h") for order in orders]
        outs = [(shaped((self.model // 2, sum(self.columns))), "v")]
        for place, bits, items in groups:
            for lhs, ordered, rhs, blocks in items:
                args += [(p, "h") for p in lhs] + [(p, "h") for p in rhs]
                if not ordered:
                    outs += [(shaped(p.shape[::-1], BF), "h") for p in lhs]
        made = chain(partial(grads_sent, self.plan), outs, args, 0, name + "_sent")
        self.turned = list(made[1:])
        self.first = chain.swap_dp(made[0], groups[0][1][0], dp_size)
        self.bits = [list(bits[1:]) for place, bits, items in groups]
        self.kept, self.other = [None] * len(groups), [None] * len(groups)

    def swap(self, n, sent):
        self.other[n] = self.chain.swap_dp(sent, self.bits[n].pop(0), self.dp_size)

    def keep(self, after=()):
        args, outs = [(self.first, "v")], []
        turned = list(self.turned)
        for columns, (place, bits, items) in zip(self.columns, self.groups):
            for lhs, ordered, rhs, blocks in items:
                for p in lhs:
                    args.append((p if ordered else turned.pop(0), "h"))
                args += [(p, "h") for p in rhs]
            outs += [(shaped((self.model // 4, columns)), "v")] * 2
        made = self.chain(partial(grads_kept, self.plan), outs, args, 0, self.name + "_kept", after=after)
        for n in range(len(self.groups)):
            self.kept[n] = made[2 * n + 1]
            self.swap(n, made[2 * n])

    def step(self, n, after=()):
        half = shaped((self.kept[n].shape[0] // 2, self.columns[n]))
        sent, self.kept[n] = self.chain(
            halve, [(half, "v"), (half, "v")], [(self.kept[n], "v"), (self.other[n], "v")], 0, self.name + str(n) + "_step",
            after=after,
        )
        self.swap(n, sent)

    def end(self, n, finish, outs):
        while self.bits[n]:
            self.step(n)
        return self.chain(
            finish, [(o, "v") for o in outs], [(self.kept[n], "v"), (self.other[n], "v")], 0, self.name + str(n) + "_end"
        )


def on_device(
    dp_size,
    tokens,
    frames,
    lengths,
    out_cot,
    self_query_key_value,
    self_qv_bias,
    self_output_weight,
    cross_query_weight,
    cross_kv,
    cross_bias,
    cross_output_weight,
    first_dense_weight,
    first_dense_bias,
    second_dense_weight,
    out_biases,
    norm_gains,
    norm_biases,
):
    _, slot, model = tokens.shape
    tok, frames, cot = tokens[0], frames[0], out_cot[0]
    real = frames.shape[0]
    padded = -(-real // 256) * 256
    own = self_output_weight.shape[0]
    ff = second_dense_weight.shape[0]
    cut = slot // 2 // 64 * 64
    low_rows, high_rows = slice(0, cut), slice(cut, slot)
    w3 = self_query_key_value.transpose(1, 0, 2)
    w2kv = cross_kv.transpose(1, 0, 2)
    fb = first_dense_bias[None]
    gains, shifts, ob = norm_gains, norm_biases, out_biases
    bits = [1 << i for i in range(dp_size.bit_length() - 1)]
    turned_bits = bits[:1] + bits[2:] + bits[1:2]
    sources = jnp.stack([relative_source(model, bits), relative_source(model, turned_bits)], axis=1)
    chain = Chain(norm_gains)
    spot = (lax.axis_index("dp") & 3).astype(jnp.int32)
    spots = spot.reshape(1)

    def count(rows):
        return rows.stop - rows.start

    def sized(rows, width, dtype=F32):
        return shaped((count(rows), width), dtype)

    def attended(rows):
        return [(sized(rows, own, BF), "h"), (sized(rows, own), "h"), (shaped((8, count(rows))), "h"), (sized(rows, model), "v")]

    def fetched(weight, parts):
        block = weight.shape[0] // parts
        at = (spot & (parts - 1)) * block
        return swap_mp(lax.dynamic_slice_in_dim(weight, at, block, 0).astype(F32))

    made = chain(
        partial(self_start, cut),
        [(sized(low_rows, model, BF), "h"), (sized(high_rows, model, BF), "h")] + [(shaped((slot, own), BF), "h")] * 3
        + attended(high_rows),
        [(tok, "h"), (gains, "h"), (shifts, "h"), (self_qv_bias, "h"), (w3, "h"), (lengths, "s"), (self_output_weight, "h")],
        0,
        "self_start",
        scratch=[pltpu.VMEM((count(high_rows), LANES), F32), pltpu.VMEM((slot, model), BF)],
    )
    x1_l, x1_h, q1, k1, v1, mix1_h, out1_h, lse1_h, part1_h = made
    other1_h = chain.swap_mp(part1_h)
    mix1_l, out1_l, lse1_l, part1_l = chain(
        partial(self_next, low_rows),
        attended(low_rows),
        [(q1, "h"), (k1, "h"), (v1, "h"), (lengths, "s"), (self_output_weight, "h")],
        0,
        "self_next",
        scratch=[pltpu.VMEM((count(low_rows), LANES), F32)],
    )
    other1_l = chain.swap_mp(part1_l)
    k2, v2, turned_frames, order, order_turned = chain(
        frames_start,
        [(shaped((padded, own), BF), "h")] * 2 + [(shaped((model, padded), BF), "h")] + [(shaped((model, model), BF), "h")] * 2,
        [(frames, "h"), (w2kv, "h"), (cross_bias, "h"), (sources, "h")],
        0,
        "frames_start",
        scratch=[pltpu.VMEM((padded, model), BF)],
    )
    orders = (order, order_turned)

    def turned(plan, parts):
        used = orders[: 1 + max(place for place, _ in plan)]
        return chain(
            partial(turn, plan),
            [(shaped((model, parts[part].shape[0]), BF), "h") for _, part in plan],
            [(o, "h") for o in used] + [(p, "h") for p in parts],
            0,
            "turn",
        )


    def cross(rows, mine, other):
        return chain(
            partial(cross_start, rows, real),
            [(sized(rows, model), "h"), (sized(rows, model, BF), "h"), (sized(rows, own, BF), "h")] + attended(rows),
            [(mine, "v"), (other, "v"), (tok, "h"), (ob, "h"), (gains, "h"), (shifts, "h"), (cross_bias, "h"),
             (cross_query_weight, "h"), (k2, "h"), (v2, "h"), (cross_output_weight, "h")],
            0,
            "cross_start",
            scratch=[pltpu.VMEM((count(rows), LANES), F32)],
        )

    s1_h, x2_h, q2_h, mix2_h, out2_h, lse2_h, part2_h = cross(high_rows, part1_h, other1_h)
    other2_h = chain.swap_mp(part2_h)
    s1_l, x2_l, q2_l, mix2_l, out2_l, lse2_l, part2_l = cross(low_rows, part1_l, other1_l)
    other2_l = chain.swap_mp(part2_l)
    x1t_h, x1t_l, x2t_h, x2t_l = turned(((0, 0), (0, 1), (0, 2), (0, 3)), (x1_h, x1_l, x2_h, x2_l))

    def dense(rows, s1, mine, other):
        return chain(
            dense_start,
            [(sized(rows, model), "h"), (sized(rows, model, BF), "h"), (sized(rows, ff, BF), "h"), (sized(rows, ff), "h"),
             (sized(rows, model), "v")],
            [(mine, "v"), (other, "v"), (s1, "h"), (ob, "h"), (gains, "h"), (shifts, "h"), (fb, "h"),
             (first_dense_weight, "h"), (second_dense_weight, "h")],
            0,
            "dense_start",
        )

    s2_h, x3_h, act_h, slope_h, part3_h = dense(high_rows, s1_h, part2_h, other2_h)
    other3_h = chain.swap_mp(part3_h)
    s2_l, x3_l, act_l, slope_l, part3_l = dense(low_rows, s1_l, part2_l, other2_l)
    other3_l = chain.swap_mp(part3_l)
    x3o_h, x3o_l = turned(((1, 0), (1, 1)), (x3_h, x3_l))

    def dense_b(rows, s2, mine, other, slope):
        return chain(
            partial(dense_back, rows),
            [(sized(rows, model, BF), "h"), (sized(rows, model), "h"), (sized(rows, model, BF), "h"),
             (sized(rows, ff, BF), "h"), (sized(rows, model), "v"), (shaped((8, model)), "v"), (shaped((8, ff)), "v")],
            [(mine, "v"), (other, "v"), (s2, "h"), (ob, "h"), (gains, "h"), (shifts, "h"), (cot, "h"), (lengths, "s"),
             (second_dense_weight, "h"), (slope, "h"), (first_dense_weight, "h")],
            6 * count(rows) * model * ff,
            "dense_back",
        )

    y_h, g3_h, low3_h, hid_h, part4_h, sum3_h, hsum_h = dense_b(high_rows, s2_h, part3_h, other3_h, slope_h)
    other4_h = chain.swap_mp(part4_h)
    y_l, g3_l, low3_l, hid_l, part4_l, sum3_l, hsum_l = dense_b(low_rows, s2_l, part3_l, other3_l, slope_l)

    denses = Halving(
        chain,
        orders,
        [
            (0, bits, [((low3_h, low3_l), False, (act_h, act_l), (0,))]),
            (1, turned_bits, [((x3o_h, x3o_l), True, (hid_h, hid_l), (0,))]),
        ],
        dp_size,
        "dense",
    )
    other4_l = chain.swap_mp(chain.tie(part4_l))
    wq_0 = chain.later(lambda tied=chain.tie(cross_query_weight): fetched(tied, 2))
    chain.pause(other4_h)
    denses.keep()
    all_rows = slice(0, slot)

    def block_sizes(dtype, width):
        return [(sized(high_rows, width, dtype), "h"), (sized(low_rows, width, dtype), "h")]

    heads = [pltpu.VMEM((slot, own), BF), pltpu.VMEM((slot, own), F32)]
    joined = [pltpu.VMEM((slot, own), BF), pltpu.VMEM((slot, own), F32), pltpu.VMEM((8, slot), F32)]
    which = lax.axis_index("mp").astype(jnp.int32).reshape(1)
    half_width = model // 2
    cuts = [-(-real * n // (8 * PIECES)) * 8 for n in range(PIECES)] + [-(-real // 8) * 8]
    g2_h, low2_h, g2_l, low2_l, lq2_h, lq2_l, part5, sum2, lk2, lv2, *frames_parts = chain(
        partial(cross_back, cut, real),
        [(sized(high_rows, model), "h"), (sized(high_rows, model, BF), "h"), (sized(low_rows, model), "h"),
         (sized(low_rows, model, BF), "h")] + block_sizes(BF, own)
        + [(shaped((slot, own)), "v"), (shaped((8, model)), "v")] + [(shaped((padded, own), BF), "h")] * 2
        + [(shaped((cuts[n + 1] - cuts[n], half_width)), "r") for n in range(PIECES)],
        [(part4_h, "h"), (other4_h, "h"), (s2_h, "h"), (g3_h, "h"), (q2_h, "h"), (out2_h, "h"), (lse2_h, "h"),
         (part4_l, "h"), (other4_l, "h"), (s2_l, "h"), (g3_l, "h"), (q2_l, "h"), (out2_l, "h"), (lse2_l, "h"),
         (gains, "h"), (cross_output_weight, "h"), (k2, "h"), (v2, "h"), (which, "s"), (w2kv, "h")],
        0,
        "cross_back",
        scratch=heads + joined + [pltpu.VMEM((padded, half_width), F32), pltpu.SemaphoreType.DMA((PIECES,))],
    )
    other5 = chain.swap_mp(part5)
    wq_1 = chain.later(lambda tied=chain.link: swap_dp(lax.optimization_barrier((wq_0.value, tied))[0], 1, dp_size))
    steps(chain, [(denses, 0), (denses, 1)], (wq_0,))
    crosses = Halving(
        chain,
        orders,
        [
            (
                0,
                bits,
                [
                    ((low2_h, low2_l), False, (mix2_h, mix2_l), (0,)),
                    ((x2t_h, x2t_l), True, (lq2_h, lq2_l), (0,)),
                    ((turned_frames,), True, (lk2,), (0,)),
                    ((turned_frames,), True, (lv2,), (0,)),
                ],
            )
        ],
        dp_size,
        "cross",
    )
    frames_other = [chain.swap_mp(chain.tie(frames_parts[0]))]
    chain.pause(other5)
    crosses.keep()
    frames_other.append(chain.swap_mp(chain.tie(frames_parts[1])))
    g1_h, low1_h, g1_l, low1_l, l3_h, l3_l, part6_h, part6_l, sum1 = chain(
        partial(self_back, cut),
        [(sized(high_rows, model), "h"), (sized(high_rows, model, BF), "h"), (sized(low_rows, model), "h"),
         (sized(low_rows, model, BF), "h"), (shaped((3, count(high_rows), own), BF), "h"),
         (shaped((3, count(low_rows), own), BF), "h"), (sized(high_rows, model), "v"), (sized(low_rows, model), "v"),
         (shaped((8, model)), "v")],
        [(spots, "s"), (part5, "h"), (other5, "h"), (cross_query_weight, "h"), (wq_0, "h"), (wq_1, "h"), (gains, "h"),
         (self_output_weight, "h"), (q1, "h"), (k1, "h"), (v1, "h"), (w3, "h"), (lengths, "s"),
         (s1_h, "h"), (g2_h, "h"), (out1_h, "h"), (lse1_h, "h"), (s1_l, "h"), (g2_l, "h"), (out1_l, "h"), (lse1_l, "h")],
        0,
        "self_back",
        scratch=heads + [pltpu.VMEM((model, own), BF)] + joined + [pltpu.VMEM((2, slot, own), BF), pltpu.VMEM((slot, model), F32)],
    )
    other6_h = chain.swap_mp(part6_h)
    steps(chain, [(denses, 0), (denses, 1)], (frames_other[0],))
    selves = Halving(
        chain,
        orders,
        [
            (
                0,
                bits,
                [((low1_h, low1_l), False, (mix1_h, mix1_l), (0,)), ((x1t_h, x1t_l), True, (l3_h, l3_l), (0,))],
            ),
            (0, bits, [((x1t_h, x1t_l), True, (l3_h, l3_l), (1, 2))]),
        ],
        dp_size,
        "self",
    )
    other6_l = chain.swap_mp(chain.tie(part6_l))
    shard = model // dp_size
    crosses.step(0, (frames_other[1],))
    t_high, sum0_h = chain(
        partial(tokens_end, high_rows),
        [(sized(high_rows, model), "h"), (shaped((8, model)), "h")],
        [(tok, "h"), (gains, "h"), (g1_h, "h"), (part6_h, "v"), (other6_h, "v"), (lengths, "s")],
        0,
        "tokens_end",
        scratch=[pltpu.VMEM((8, model), F32)],
    )
    second_turned, first_grad = ends(chain, [(denses, 0), (denses, 1)], shaped((shard, ff)))
    selves.keep()
    tokens_grad, total, y = chain(
        partial(tokens_end, low_rows),
        [(shaped((slot, model)), "h"), (shaped((13 + ff // model, model)), "v"), (shaped((slot, model), BF), "h")],
        [(tok, "h"), (gains, "h"), (g1_l, "h"), (part6_l, "v"), (other6_l, "v"), (t_high, "h"), (sum0_h, "h"),
         (sum1, "h"), (sum2, "h"), (sum3_h, "h"), (sum3_l, "h"), (hsum_h, "h"), (hsum_l, "h"), (y_l, "h"), (y_h, "h")],
        0,
        "tokens_end",
        scratch=[pltpu.VMEM((8, model), F32)],
    )
    small_bits = list(bits)

    def small_step(total, other):
        (total,) = chain(plain_end, [(shaped(total.shape), "v")], [(total, "v"), (other, "v")], 0, "small_step")
        return total, chain.swap_dp(total, small_bits.pop(0), dp_size)

    small_other = chain.swap_dp(total, small_bits.pop(0), dp_size)
    frames_other.append(chain.swap_mp(chain.tie(frames_parts[2])))
    crosses.step(0)
    selves.step(0)
    total, small_other = small_step(total, small_other)
    frames_other.append(chain.swap_mp(chain.tie(frames_parts[3])))
    selves.step(1, (frames_other[2],))
    cross_out_grad, cross_q_grad, cross_kv_grad = crosses.end(
        0, cross_end, [shaped((shard, own)), shaped((shard, own)), shaped((shard, 2, own))]
    )
    selves.step(0)
    total, small_other = small_step(total, small_other)
    selves.step(1)
    while small_bits:
        total, small_other = small_step(total, small_other)
    (frames_grad,) = chain(
        frames_kept, [(shaped((real, 1, half_width)), "r")],
        [(which, "s"), (lk2, "h"), (lv2, "h"), (w2kv, "h")] + [(o, "h") for o in frames_other],
        0, "frames_kept",
        scratch=[pltpu.VMEM((padded, half_width), F32), pltpu.VMEM((real, half_width), F32), pltpu.SemaphoreType.DMA],
    )
    self_out_grad, q_grad = selves.end(0, self_end, [shaped((shard, own))] * 2)
    k_grad, v_grad = selves.end(1, self_end, [shaped((shard, own))] * 2)
    gains_grad, shifts_grad, ob_grad, svb_grad, cvb_grad, fb_grad = chain(
        small_end,
        [(shaped((4, model)), "v"), (shaped((4, model)), "v"), (shaped((3, model)), "v"), (shaped((2, own)), "v"),
         (shaped((2, own)), "v"), (shaped((ff // model, model)), "v")],
        [(total, "v"), (small_other, "v")],
        0,
        "small_end",
    )
    return (
        y[None],
        tokens_grad[None],
        frames_grad.transpose(1, 0, 2),
        jnp.stack([q_grad, k_grad, v_grad], axis=1),
        svb_grad,
        self_out_grad.T,
        cross_q_grad,
        cross_kv_grad,
        cvb_grad,
        cross_out_grad.T,
        first_grad,
        fb_grad.reshape(ff),
        second_turned.T,
        ob_grad,
        gains_grad,
        shifts_grad,
    )


def solution(mesh):
    in_specs = (
        P("dp", None, None),
        P("dp", None, None),
        P("dp"),
        P("dp", None, None),
        P(None, None, "mp"),
        P(None, "mp"),
        P("mp", None),
        P(None, "mp"),
        P(None, None, "mp"),
        P(None, "mp"),
        P("mp", None),
        P(None, "mp"),
        P("mp"),
        P("mp", None),
        P(),
        P(),
        P(),
    )
    out_specs = (
        P("dp", None, None),
        P("dp", None, None),
        P("dp", None, "mp"),
        P("dp", None, "mp"),
        P(None, "mp"),
        P("mp", "dp"),
        P("dp", "mp"),
        P("dp", None, "mp"),
        P(None, "mp"),
        P("mp", "dp"),
        P("dp", "mp"),
        P("mp"),
        P("mp", "dp"),
        P(),
        P(),
        P(),
    )
    return jax.shard_map(
        partial(on_device, mesh.shape["dp"]),
        mesh=mesh,
        in_specs=in_specs,
        out_specs=out_specs,
        check_vma=False,
    )
```

```python
from functools import partial

import jax
import jax.numpy as jnp
from jax import lax
from jax.experimental import pallas as pl
from jax.experimental.pallas import tpu as pltpu
from jax.sharding import PartitionSpec as P

F32 = jnp.float32
BF = jnp.bfloat16
HEAD_DIM = 64
LANES = 128
NEG = -1e30
COST = {"self_start": 2.0, "self_next": 1.3, "turn": 1.0, "frames_start": 3.0, "cross_start": 2.7, "dense_start": 2.4,
        "dense_back": 2.4, "dense_sent": 6.0, "dense_kept": 6.0, "cross_back": 20.0, "self_back": 12.0,
        "cross_sent": 6.0, "cross_kept": 5.0, "self_sent": 5.0, "self_kept": 4.0, "tokens_end": 5.0, "frames_kept": 6.0,
        "small_end": 1.0, "pause": 8.0}
SCALE = 1.5e10
PIECES = 4
BACK_BLOCKS = 2
ROW_BLOCKS = 1
BYTES = 6.4e-3
PINNED = ("h", "t", "r")


def shaped(shape, dtype=F32):
    return jax.ShapeDtypeStruct(tuple(shape), dtype)


def dg(a, b, ca, cb):
    return lax.dot_general(a, b, (((ca,), (cb,)), ((), ())), preferred_element_type=F32)


def nn(a, b):
    return dg(a, b, 1, 0)


def nt(a, b):
    return dg(a, b, 1, 1)


def tn(a, b):
    return dg(a, b, 0, 0)


class Feed:
    def __init__(self, source, target, sem):
        self.copy = pltpu.make_async_copy(source, target, sem)
        self.copy.start()
        self.target = target
        self.pending = True

    def ready(self):
        if self.pending:
            self.copy.wait()
            self.pending = False
        return self.target


class Drain:
    def __init__(self, source, target, sem):
        self.ref = source
        self.copy = pltpu.make_async_copy(source, target, sem)
        self.pending = True

    def flush(self):
        if self.pending:
            self.copy.start()
            self.pending = False


def use(*inputs):
    made = [i.ready() if isinstance(i, Feed) else i for i in inputs]
    return made if len(made) > 1 else made[0]


def flush(*outputs):
    for o in outputs:
        if isinstance(o, Drain):
            o.flush()


def into(*outputs):
    made = [o.ref if isinstance(o, Drain) else o for o in outputs]
    return made if len(made) > 1 else made[0]


class Pending:
    def __init__(self, make):
        self.make, self.value = make, None


class Chain:
    def __init__(self, seed):
        self.link = seed
        self.pending = []

    def pause(self, *after):
        self(lambda ins, outs, scratch: None, [], [], 0, "pause", after=after)

    def later(self, make):
        self.pending.append(Pending(make))
        return self.pending[-1]

    def settle(self):
        for item in reversed(self.pending):
            item.value = item.make()
        self.pending = []

    def swap_mp(self, v):
        return self.later(lambda: swap_mp(v))

    def swap_dp(self, v, bit, dp_size):
        return self.later(lambda: swap_dp(v, bit, dp_size))

    def tie(self, value):
        return lax.optimization_barrier((value, self.link))[0]

    def __call__(self, kernel, outs, args, flops, name, scratch=(), after=()):
        place = {
            "v": pl.BlockSpec(memory_space=pltpu.VMEM),
            "h": pl.BlockSpec(memory_space=pltpu.HBM),
            "s": pl.BlockSpec(memory_space=pltpu.SMEM),
        }
        args = [(self.link, "t")] + [(a, "t") for a in after] + list(args)
        first = 1 + len(after)
        if any(isinstance(a, Pending) and a.value is None for a, _ in args):
            self.settle()
        args = [(a.value if isinstance(a, Pending) else a, k) for a, k in args]
        outs = [(shaped((8, LANES)), "t")] + list(outs)
        held = []
        for item, kind in args[first:] + outs[1:]:
            if kind == "h":
                held.append(pltpu.VMEM(item.shape, item.dtype))
        n_in, n_out = len(args), len(outs)

        def body(*refs):
            ins, results = refs[first:n_in], refs[n_in + 1 : n_in + n_out]
            rest = refs[n_in + n_out :]
            own, bufs, sems = rest[: len(scratch)], list(rest[len(scratch) : -1]), rest[-1]
            at = 0
            feeds, drains = [], []
            for ref, (_, kind) in zip(ins, args[first:]):
                if kind == "h":
                    feeds.append(Feed(ref, bufs[at], sems.at[at]))
                    at += 1
                else:
                    feeds.append(ref)
            for ref, (_, kind) in zip(results, outs[1:]):
                if kind == "h":
                    drains.append(Drain(bufs[at], ref, sems.at[at]))
                    at += 1
                else:
                    drains.append(ref)
            kernel(feeds, drains, own)
            for feed in feeds:
                use(feed)
            flush(*drains)
            for d in drains:
                if isinstance(d, Drain):
                    d.copy.wait()

        moved = 0
        for item, kind in args + outs:
            size = jnp.dtype(item.dtype).itemsize
            for d in item.shape:
                size *= d
            moved += size
        place["t"] = place["r"] = place["h"]
        made = pl.pallas_call(
            body,
            out_shape=tuple(pltpu.HBM(o.shape, o.dtype) if k in PINNED else o for o, k in outs),
            in_specs=[place[k] for _, k in args],
            out_specs=tuple(place[k] for _, k in outs),
            scratch_shapes=list(scratch) + held + [pltpu.SemaphoreType.DMA((max(1, len(held)),))],
            compiler_params=pltpu.CompilerParams(vmem_limit_bytes=28 * 1024 * 1024),
            cost_estimate=pl.CostEstimate(flops=int(COST.get(name, 1.0) * SCALE), transcendentals=0, bytes_accessed=int(COST.get(name, 1.0) * SCALE * BYTES)),
            name=name,
        )(*[pltpu.with_memory_space_constraint(a, pltpu.HBM) if k in PINNED else a for a, k in args])
        self.link = made[0]
        return made[1:]


def standard(stream):
    centred = stream - jnp.mean(stream, axis=1, keepdims=True)
    spread = jnp.mean(centred * centred, axis=1, keepdims=True)
    scale = lax.rsqrt(spread + 1e-05)
    return centred * scale, scale


def norm_back(grad, unit, scale, gain):
    lifted = grad * gain
    mean_plain = jnp.mean(lifted, axis=1, keepdims=True)
    mean_cross = jnp.mean(lifted * unit, axis=1, keepdims=True)
    return scale * (lifted - mean_plain - unit * mean_cross)


def column_sums(values):
    return jnp.sum(values, axis=0, keepdims=True)


def head_lanes(which):
    lane = lax.broadcasted_iota(jnp.int32, (1, LANES), 1)
    return (lane < HEAD_DIM) if which == 0 else (lane >= HEAD_DIM)


def only(mask, values):
    return jnp.where(mask, values, jnp.zeros_like(values))


def pair_slice(pair):
    return pl.ds(pl.multiple_of(pair * LANES, LANES), LANES)


def attend_rows(q_ref, k_ref, v_ref, rows, keys, bias, mixed_ref, out_ref, lse_ref, lse_all, blocks):
    lane = lax.broadcasted_iota(jnp.int32, (1, LANES), 1)
    size = (rows.stop - rows.start) // blocks

    def body(step, carry):
        pair, part = (step, 0) if blocks == 1 else (step // blocks, step % blocks)
        at = pair_slice(pair)
        here = place(part, size) if blocks > 1 else slice(0, size)
        theirs = pl.ds(pl.multiple_of(rows.start + part * size, 16), size) if blocks > 1 else rows
        k_pair, v_pair, q_pair = k_ref[0:keys, at], v_ref[0:keys, at], q_ref[theirs, at]
        result, lse = None, lse_all[here]
        for which in range(2):
            mask = head_lanes(which)
            scores = nt(only(mask, q_pair), k_pair) + bias(part * size, size)
            top = jnp.max(scores, axis=1, keepdims=True)
            raised = jnp.exp(scores - top)
            total = jnp.sum(raised, axis=1, keepdims=True)
            value = nn(raised.astype(BF), v_pair) * (1.0 / total)
            result = value if which == 0 else jnp.where(mask, value, result)
            lse = jnp.where(lane == 2 * pair + which, top + jnp.log(total), lse)
        lse_all[here] = lse
        out_ref[here, at] = result
        mixed_ref[here, at] = result.astype(BF)
        return carry

    lse_all[...] = jnp.zeros_like(lse_all)
    lax.fori_loop(0, q_ref.shape[1] // LANES * blocks, body, 0)
    lse_ref[...] = lse_all[...].T[0 : lse_ref.shape[0]]


def attend_back(q_ref, g_ref, o_ref, lse_ref, k_ref, v_ref, rows, keys, bias, dq_ref, emit, block=None):
    block = keys if block is None else block
    blocks = keys // block

    def body(step, carry):
        pair, part = (step, 0) if blocks == 1 else (step // blocks, step % blocks)
        at = pair_slice(pair)
        here = pl.ds(0, keys) if blocks == 1 else pl.ds(pl.multiple_of(part * block, block), block)
        k_pair, v_pair = k_ref[here, at], v_ref[here, at]
        q_pair, g_pair = q_ref[rows, at], g_ref[:, at]
        product = (g_pair.astype(F32) * o_ref[:, at]).T
        k_turned = k_pair.T
        parts, grad_k, grad_v = [], None, None
        for which in range(2):
            mask = head_lanes(which)
            q_head, g_head = only(mask, q_pair), only(mask, g_pair)
            inner = column_sums(product[which * HEAD_DIM : (which + 1) * HEAD_DIM])
            scores = nt(k_pair, q_head) + bias(part * block)
            probs = jnp.exp(scores - lse_ref[pl.ds(2 * pair + which, 1), :])
            grad_probs = nt(v_pair, g_head)
            grad_scores = (probs * (grad_probs - inner)).astype(BF)
            here_v = nn(probs.astype(BF), g_head)
            here_k = nn(grad_scores, q_head)
            grad_v = here_v if which == 0 else grad_v + here_v
            grad_k = here_k if which == 0 else grad_k + here_k
            parts.append(nn(k_turned[which * HEAD_DIM : (which + 1) * HEAD_DIM], grad_scores))
        emit(pair, part, at, here, grad_k, grad_v)
        grad_q = jnp.concatenate(parts, axis=0).T
        if blocks == 1:
            dq_ref[:, at] = grad_q
        else:
            dq_ref[:, at] += grad_q
        return carry

    if blocks > 1:
        dq_ref[...] = jnp.zeros_like(dq_ref)
    lax.fori_loop(0, q_ref.shape[1] // LANES * blocks, body, 0)


def causal_bias(start, count, keys, length):
    shape = (count, keys)
    query = lax.broadcasted_iota(jnp.int32, shape, 0) + start
    key = lax.broadcasted_iota(jnp.int32, shape, 1)
    return jnp.where((key <= query) & (key < length), 0.0, NEG).astype(F32)


def tail_bias(keys, real, turned, start=0):
    shape = (keys, 1) if turned else (1, keys)
    key = lax.broadcasted_iota(jnp.int32, shape, 0 if turned else 1) + start
    return jnp.where(key < real, 0.0, NEG).astype(F32)


def place(step, size):
    return pl.ds(pl.multiple_of(step * size, size), size)


def by_rows(count, work):
    size = count // 2

    def body(step, carry):
        work(place(step, size))
        return carry

    lax.fori_loop(0, count // size, body, 0)


def ordered(out, order, left):
    size = 2 * LANES

    def body(step, carry):
        out[place(step, size)] = nt(order[place(step, size)], left[...]).astype(BF)
        return carry

    lax.fori_loop(0, order.shape[0] // size, body, 0)


def self_start(cut, ins, outs, scratch):
    tok, gains, shifts, vb, w, length, wo = ins
    x_lo, x_hi, q_o, k_o, v_o = outs[:5]
    rows = slice(cut, tok.target.shape[0])
    low_ref, high_ref, q_ref, k_ref, v_ref = into(*outs[:5])
    tok, gains, shifts, vb, w = use(tok, gains, shifts, vb, w)
    x_all, size = scratch[1], tok.shape[0] // 2

    def work(here):
        unit, _ = standard(tok[here].astype(F32))
        x_all[here] = (unit * gains[0:1] + shifts[0:1]).astype(BF)

    by_rows(tok.shape[0], work)

    def body(step, carry):
        here = place(step, size)
        x = x_all[here]
        q_ref[here] = ((nn(x, w[0]) + vb[0:1]) * 0.125).astype(BF)
        k_ref[here] = nn(x, w[1]).astype(BF)
        v_ref[here] = (nn(x, w[2]) + vb[1:2]).astype(BF)
        return carry

    lax.fori_loop(0, 2, body, 0)
    low_ref[...] = x_all[:cut]
    high_ref[...] = x_all[cut:]
    flush(x_lo, x_hi, q_o, k_o, v_o)
    self_rows(rows, q_ref, k_ref, v_ref, length, wo, outs[5:], scratch)


def self_next(rows, ins, outs, scratch):
    q_ref, k_ref, v_ref, length, wo = ins
    self_rows(rows, *use(q_ref, k_ref, v_ref), length, wo, outs, scratch)


def self_rows(rows, q_ref, k_ref, v_ref, length, wo, outs, scratch):
    def bias(start, size):
        return causal_bias(rows.start + start, size, rows.stop, length[0])

    mixed, out, lse, part = into(*outs)
    attend_rows(q_ref, k_ref, v_ref, rows, rows.stop, bias, mixed, out, lse, scratch[0], 1)
    flush(*outs[:3])
    part[...] = nn(mixed[...], use(wo)[...])


def turn(plan, ins, outs, scratch):
    orders = ins[: 1 + max(which for which, _ in plan)]
    parts = ins[len(orders) :]
    for (which, part), out in zip(plan, outs):
        ordered(into(out), use(orders[which]), use(parts[part]))
        flush(out)


def frames_start(ins, outs, scratch):
    frames, w, vb, sources = ins
    k_o, v_o, t_o, order_o, other_o = outs
    k_ref, v_ref, t_ref, order, other = into(*outs)
    (frames_all,) = scratch
    sources = use(sources)
    column = lax.broadcasted_iota(jnp.int32, order.shape, 1)
    order[...] = jnp.where(column == sources[:, 0:1], 1.0, 0.0).astype(BF)
    other[...] = jnp.where(column == sources[:, 1:2], 1.0, 0.0).astype(BF)
    flush(order_o, other_o)
    real, padded = frames.target.shape[0], k_ref.shape[0]
    if padded > real:
        low = real // 16 * 16
        frames_all[low:padded] = jnp.zeros((padded - low, frames_all.shape[1]), BF)
    frames, w, vb = use(frames, w, vb)
    frames_all[0:real] = frames[...]
    size = padded // 3

    def body(step, carry):
        rows = frames_all[place(step, size)]
        k_ref[place(step, size)] = nn(rows, w[0]).astype(BF)
        v_ref[place(step, size)] = (nn(rows, w[1]) + vb[1:2]).astype(BF)
        t_ref[:, place(step, size)] = nt(order[...], rows).astype(BF)
        return carry

    lax.fori_loop(0, 3, body, 0)


def assemble(out, spot, pieces):
    block = out.shape[0] // len(pieces)
    for j, piece in enumerate(pieces):
        at = pl.multiple_of(((spot[0] & (len(pieces) - 1)) ^ j) * block, 16)
        out[pl.ds(at, block), :] = use(piece)[...].astype(BF)


def cross_start(rows, real, ins, outs, scratch):
    mine, other, tok, ob, gains, shifts, vb, wq, k_in, v_in, wo = ins
    s_o, x_o, q_o, m_o, out_o, lse_o, part = outs
    mixed, out, lse, part = into(m_o, out_o, lse_o, part)
    s_ref, x_ref, q_ref = into(s_o, x_o, q_o)
    mine, other, tok, ob, gains, shifts = use(mine, other, tok, ob, gains, shifts)
    block = tok.at[rows]

    def work(here):
        stream = block[here].astype(F32) + (mine[here] + other[here]) + ob[0:1]
        s_ref[here] = stream
        unit, _ = standard(stream)
        x_ref[here] = (unit * gains[1:2] + shifts[1:2]).astype(BF)

    by_rows(s_ref.shape[0], work)
    flush(s_o)
    vb, wq = use(vb, wq)
    q_ref[...] = ((nn(x_ref[...], wq[...]) + vb[0:1]) * 0.125).astype(BF)
    flush(x_o, q_o)
    k_ref, v_ref = use(k_in, v_in)
    keys = k_ref.shape[0]
    tail = tail_bias(keys, real, False)
    attend_rows(q_ref, k_ref, v_ref, slice(0, x_ref.shape[0]), keys, lambda start, size: tail, mixed, out, lse, scratch[0], ROW_BLOCKS)
    flush(m_o, out_o, lse_o)
    part[...] = nn(mixed[...], use(wo)[...])


def dense_start(ins, outs, scratch):
    mine, other, s_in, ob, gains, shifts, fb, w1, w2 = ins
    s_o, x_o, a_o, d_o, part = outs
    s_ref, x_ref, active, slope, part = into(s_o, x_o, a_o, d_o, part)
    mine, other, s_in, ob, gains, shifts = use(mine, other, s_in, ob, gains, shifts)
    def work(here):
        stream = s_in[here] + (mine[here] + other[here]) + ob[1:2]
        s_ref[here] = stream
        unit, _ = standard(stream)
        x_ref[here] = (unit * gains[2:3] + shifts[2:3]).astype(BF)

    by_rows(s_ref.shape[0], work)
    flush(s_o, x_o)
    fb, w1, w2 = use(fb, w1, w2)
    wide = 3 * LANES

    def body(step, carry):
        at = pl.ds(pl.multiple_of(step * wide, wide), wide)
        hidden = nn(x_ref[...], w1[:, at]) + fb[:, at]
        below = 0.5 + 0.5 * lax.erf(hidden * 0.7071067811865476)
        slope[:, at] = below + hidden * (0.3989422804014327 * jnp.exp(-0.5 * hidden * hidden))
        value = (hidden * below).astype(BF)
        active[:, at] = value
        part[...] += nn(value, w2[at, :])
        return carry

    part[...] = jnp.zeros_like(part)
    lax.fori_loop(0, w1.shape[1] // wide, body, 0)


def dense_back(rows, ins, outs, scratch):
    mine, other, s_in, ob, gains, shifts, cot, length, w2, slope, w1 = ins
    y_o, g_o, low_o, hid_o, part, sums, hid_sums = outs
    out_ref, g_ref, low_ref, hid_ref, part, sums, hid_sums = into(*outs)
    mine, other, s_in, ob, gains, shifts = use(mine, other, s_in, ob, gains, shifts)
    block = use(cot).at[rows]
    sums[0:3] = jnp.zeros((3, sums.shape[1]), F32)

    def work(here):
        stream = s_in[here] + (mine[here] + other[here]) + ob[2:3]
        unit, scale = standard(stream)
        row = lax.broadcasted_iota(jnp.int32, (stream.shape[0], 1), 0) + (rows.start + here.start)
        valid = (row < length[0]).astype(F32)
        out_ref[here] = ((unit * gains[3:4] + shifts[3:4]) * valid).astype(BF)
        incoming = block[here].astype(F32) * valid
        grad = norm_back(incoming, unit, scale, gains[3:4])
        g_ref[here] = grad
        low_ref[here] = grad.astype(BF)
        sums[0:1] += column_sums(incoming * unit)
        sums[1:2] += column_sums(incoming)
        sums[2:3] += column_sums(grad)

    by_rows(g_ref.shape[0], work)
    flush(y_o, g_o, low_o)
    w2, slope, w1 = use(w2, slope, w1)
    wide = 3 * LANES

    def body(step, carry):
        at = pl.ds(pl.multiple_of(step * wide, wide), wide)
        low = (slope[:, at] * nt(low_ref[...], w2[at, :])).astype(BF)
        hid_ref[:, at] = low
        hid_sums[0:1, at] = column_sums(low.astype(F32))
        part[...] += nt(low, w1[:, at])
        return carry

    part[...] = jnp.zeros_like(part)
    lax.fori_loop(0, w1.shape[1] // wide, body, 0)


def back_head(incoming_at, ins, outs, gm, gains, wo, sums, level, more):
    s_in, g_in = ins
    g_o, low_o = outs
    g_ref, low_ref = into(g_o, low_o)
    s_in, g_in, gains = use(s_in, g_in, gains)
    if not more:
        sums[0:3] = jnp.zeros((3, sums.shape[1]), F32)

    def work(here):
        incoming = incoming_at(here)
        unit, scale = standard(s_in[here])
        grad = g_in[here] + norm_back(incoming, unit, scale, gains[level : level + 1])
        g_ref[here] = grad
        low_ref[here] = grad.astype(BF)
        sums[0:1] += column_sums(incoming * unit)
        sums[1:2] += column_sums(incoming)
        sums[2:3] += column_sums(grad)

    by_rows(g_ref.shape[0], work)
    flush(g_o, low_o)
    gm[...] = nt(low_ref[...], use(wo)[...]).astype(BF)


def gather_heads(count, q_all, o_all, lse_all, refs):
    start = 0
    for q_ref, out_in, lse in refs:
        q_ref, out_in, lse = use(q_ref, out_in, lse)
        stop = start + out_in.shape[0]
        if q_all is not None:
            q_all[start:stop] = q_ref[...]
        o_all[start:stop] = out_in[...]
        lse_all[:, start:stop] = lse[...]
        start = stop


def cross_back(cut, real, ins, outs, scratch):
    blocks = (ins[:7], ins[7:14])
    gains, wo, k_in, v_in, which, kv = ins[14:20]
    lq_outs, part, sums, dk_o, dv_o = outs[4:6], outs[6], outs[7], outs[8], outs[9]
    gm, dq, q_all, o_all, lse_all, held, frame_sems = scratch
    part, sums, dk, dv = into(part, sums, dk_o, dv_o)
    start = 0
    for n, (mine, other, s_in, g_in, q_ref, out_in, lse) in enumerate(blocks):
        mine, other = use(mine, other)
        stop = start + mine.shape[0]
        back_head(lambda here, mine=mine, other=other: mine[here] + other[here], (s_in, g_in), outs[2 * n : 2 * n + 2], gm.at[start:stop], gains, wo, sums, 2, n > 0)
        start = stop
    gather_heads(start, q_all, o_all, lse_all, [b[4:7] for b in blocks])
    k_ref, v_ref = use(k_in, v_in)
    keys, width = k_ref.shape
    block = keys // BACK_BLOCKS

    def emit(pair, n, at, here, grad_k, grad_v):
        dk[here, at] = grad_k.astype(BF)
        dv[here, at] = grad_v.astype(BF)

    attend_back(q_all, gm, o_all, lse_all, k_ref, v_ref, slice(0, start), keys,
                lambda first: tail_bias(block, real, True, first), dq, emit, block)
    flush(dk_o, dv_o)
    low_q = (dq[...].astype(BF).astype(F32) * 0.125).astype(BF)
    part[...] = low_q.astype(F32)
    high = start - cut
    for o, rows in ((lq_outs[0], slice(0, high)), (lq_outs[1], slice(high, start))):
        into(o)[...] = low_q[rows]
        flush(o)
    sums[3:4, 0:width] = column_sums(low_q.astype(F32))
    sums[3:4, width : 2 * width] = column_sums(dv[0:real].astype(F32))
    width = held.shape[1]
    frames_terms(held, dk, dv, use(kv), pl.ds(pl.multiple_of((1 - which[0]) * width, width), width))
    start, copies = 0, []
    for n, out in enumerate(outs[10:]):
        copies.append(pltpu.make_async_copy(held.at[start : start + out.shape[0]], out, frame_sems.at[n]))
        copies[n].start()
        start += out.shape[0]
    for copy in copies:
        copy.wait()


def frames_terms(held, lk, lv, w, at):
    size = lk.shape[0] // 3

    def body(step, carry):
        rows = place(step, size)
        held[rows] = nt(lk[rows], w[0, at, :]) + nt(lv[rows], w[1, at, :])
        return carry

    lax.fori_loop(0, 3, body, 0)


def frames_kept(ins, outs, scratch):
    which, lk, lv, w = use(*ins[:4])
    held, final, sem = scratch
    start, width = 0, held.shape[1]
    frames_terms(held, lk, lv, w, pl.ds(pl.multiple_of(which[0] * width, width), width))
    for other in ins[4:]:
        other = use(other)
        rows = slice(start, min(start + other.shape[0], final.shape[0]))
        final[rows] = held[rows] + other[0 : rows.stop - start]
        start = rows.stop
    copy = pltpu.make_async_copy(final, outs[0].at[:, 0, :], sem)
    copy.start()
    copy.wait()


def self_back(cut, ins, outs, scratch):
    spot, mine, other, wq = ins[:4]
    pieces, (gains, wo, q_in, k_in, v_in, w, length) = ins[4:6], ins[6:13]
    blocks = (ins[13:17], ins[17:21])
    l3_outs, part_high, part_low, sums = outs[4:6], outs[6], outs[7], outs[8]
    gm, dq, wq_other, q_all, o_all, lse_all, lows, incoming = scratch
    l3_high, l3_low, part_high, part_low, sums = into(*l3_outs, part_high, part_low, sums)
    assemble(wq_other, spot, pieces)
    mine, other, wq = use(mine, other, wq)
    incoming[...] = nt(mine[...].astype(BF), wq[...]) + nt(other[...].astype(BF), wq_other[...])
    start = 0
    for n, (s_in, g_in, out_in, lse) in enumerate(blocks):
        stop = start + out_in.target.shape[0]
        block = incoming.at[start:stop]
        back_head(lambda here, block=block: block[here], (s_in, g_in), outs[2 * n : 2 * n + 2], gm.at[start:stop], gains, wo, sums, 1, n > 0)
        start = stop
    high = start - cut
    q_ref = use(q_in)
    q_all[0:high] = q_ref[cut:]
    q_all[high:] = q_ref[:cut]
    gather_heads(start, None, o_all, lse_all, [(b[2], b[2], b[3]) for b in blocks])
    k_ref, v_ref, w = use(k_in, v_in, w)
    width = k_ref.shape[1]
    block = start // 2

    def bias(first):
        lane = lax.broadcasted_iota(jnp.int32, (block, start), 1)
        query = jnp.where(lane < high, lane + cut, lane - high)
        key = lax.broadcasted_iota(jnp.int32, (block, start), 0) + first
        return jnp.where((key <= query) & (key < length[0]), 0.0, NEG).astype(F32)

    def emit(pair, n, at, here, grad_k, grad_v):
        lows[0, here, at] = grad_k.astype(BF)
        lows[1, here, at] = grad_v.astype(BF)

    attend_back(q_all, gm, o_all, lse_all, k_ref, v_ref, slice(0, start), start, bias, dq, emit, block)
    low_q = (dq[...].astype(BF).astype(F32) * 0.125).astype(BF)
    l3_high[0], l3_low[0] = low_q[:high], low_q[high:]
    for n in range(2):
        l3_high[1 + n], l3_low[1 + n] = lows[n, cut:], lows[n, :cut]
    flush(*l3_outs)
    for l3, part in ((l3_low, part_low), (l3_high, part_high)):
        part[...] = nt(l3[0], w[0]) + nt(l3[1], w[1]) + nt(l3[2], w[2])
    sums[3:4, 0:width] = column_sums(low_q.astype(F32))
    sums[3:4, width : 2 * width] = column_sums(lows[1].astype(F32))


def tokens_end(rows, ins, outs, scratch):
    tok, gains, g, mine, other = use(*ins[:5])
    block, (both,) = tok.at[rows], scratch
    target = into(outs[0]) if len(ins) == 6 else into(outs[0]).at[rows]
    both[...] = jnp.zeros_like(both)

    def work(here):
        unit, scale = standard(block[here].astype(F32))
        incoming = mine[here] + other[here]
        target[here] = g[here] + norm_back(incoming, unit, scale, gains[0:1])
        both[0:1] += column_sums(incoming * unit)
        both[1:2] += column_sums(incoming)

    by_rows(target.shape[0], work)
    if len(ins) == 6:
        flush(outs[0])
        into(outs[1])[...] = both[...]
        return
    out, total, y = into(*outs)
    gain, shift = both[0:1], both[1:2]
    earlier, first = use(*ins[5:7])
    sums, hid_sums, (y_low, y_high) = use(*ins[7:11]), use(*ins[11:13]), ins[13:15]
    out[rows.stop :] = earlier[...]
    flush(outs[0])
    y_low, y_high = use(y_low, y_high)
    y[0 : rows.stop] = y_low[...]
    y[rows.stop :] = y_high[...]
    flush(outs[2])
    total[0:1] = gain + first[0:1]
    total[4:5] = shift + first[1:2]
    for level, one in enumerate((sums[0][...], sums[1][...], sums[2][...] + sums[3][...])):
        total[1 + level : 2 + level] = one[0:1]
        total[5 + level : 6 + level] = one[1:2]
        total[8 + level : 9 + level] = one[2:3]
        if level < 2:
            total[11 + level : 12 + level] = one[3:4]
    model = total.shape[1]
    for piece in range(hid_sums[0].shape[1] // model):
        at = slice(piece * model, (piece + 1) * model)
        total[13 + piece : 14 + piece] = hid_sums[0][0:1, at] + hid_sums[1][0:1, at]


def small_end(ins, outs, scratch):
    mine, other = use(*ins)
    gain, shift, ob, svb, cvb, fb = into(*outs)
    total = mine[...] + other[...]
    half = svb.shape[1]
    gain[...] = total[0:4]
    shift[...] = total[4:8]
    ob[...] = total[8:11]
    for target, at in ((svb, 11), (cvb, 12)):
        target[0:1] = total[at : at + 1, :half]
        target[1:2] = total[at : at + 1, half:]
    fb[...] = total[13 : 13 + fb.shape[0]]


def blocks_of(rights, blocks, put):
    first = rights[0]
    if len(first.shape) == 3:
        low, wide = blocks[0], first.shape[2]

        def body(step, carry):
            put(step * wide, [r[low + step] for r in rights])
            return carry

        if len(blocks) == 1:
            body(0, 0)
        else:
            lax.fori_loop(0, len(blocks), body, 0)
        return len(blocks) * first.shape[2]
    put(0, [r[...] for r in rights])
    return first.shape[1]


def columns_at(start, width):
    return pl.ds(start if isinstance(start, int) else pl.multiple_of(start, LANES), width)


def grads_sent(plan, ins, outs, scratch):
    orders = ins[: 1 + max(which for which, _ in plan)]
    at, col = len(orders), 0
    out, turned = into(outs[0]), list(outs[1:])
    half = out.shape[0]
    for which, items in plan:
        for parts, done, blocks in items:
            lefts = ins[at : at + parts]
            at += parts
            made = []
            for left in lefts:
                left = use(left)
                if not done:
                    target = turned.pop(0)
                    ordered(into(target), use(orders[which]), left)
                    flush(target)
                    left = into(target)
                made.append(left)
            rights = [use(i) for i in ins[at : at + parts]]
            at += parts

            def put(start, values, col=col, made=made):
                total = None
                for left, value in zip(made, values):
                    term = nn(left[half:], value)
                    total = term if total is None else total + term
                out[:, columns_at(col + start, total.shape[1])] = total

            col += blocks_of(rights, blocks, put)


def grads_kept(plan, ins, outs, scratch):
    other, at, col = use(ins[0]), 1, 0
    half = other.shape[0]
    for n, (which, items) in enumerate(plan):
        sent, kept = into(outs[2 * n], outs[2 * n + 1])
        low, start = kept.shape[0], col
        for parts, done, blocks in items:
            lefts = [use(i) for i in ins[at : at + parts]]
            at += parts
            rights = [use(i) for i in ins[at : at + parts]]
            at += parts

            def put(first, values, col=col, lefts=lefts, sent=sent, kept=kept, start=start):
                total = None
                for left, value in zip(lefts, values):
                    term = nn(left[:half], value)
                    total = term if total is None else total + term
                width = total.shape[1]
                total = total + other[:, columns_at(col + first, width)]
                here = columns_at(col - start + first, width)
                sent[:, here] = total[low:]
                kept[:, here] = total[:low]

            col += blocks_of(rights, blocks, put)
        flush(outs[2 * n], outs[2 * n + 1])


def halve(ins, outs, scratch):
    for n in range(0, len(outs), 2):
        kept, other = use(*ins[n : n + 2])
        sent, out = into(*outs[n : n + 2])
        low = out.shape[0]
        out[...] = kept[0:low] + other[0:low]
        sent[...] = kept[low:] + other[low:]


def steps(chain, items, after=()):
    outs, args = [], []
    for h, n in items:
        half = shaped((h.kept[n].shape[0] // 2, h.columns[n]))
        outs += [(half, "v"), (half, "v")]
        args += [(h.kept[n], "v"), (h.other[n], "v")]
    made = chain(halve, outs, args, 0, "steps", after=after)
    for place, (h, n) in enumerate(items):
        h.kept[n] = made[2 * place + 1]
        h.swap(n, made[2 * place])


def ends(chain, items, shape):
    while items[0][0].bits[items[0][1]]:
        steps(chain, items)
    args = []
    for h, n in items:
        args += [(h.kept[n], "v"), (h.other[n], "v")]
    return chain(plain_end, [(shape, "v") for _ in items], args, 0, "ends")


def plain_end(ins, outs, scratch):
    for n, out in enumerate(outs):
        out[...] = use(ins[2 * n])[...] + use(ins[2 * n + 1])[...]


def cross_end(ins, outs, scratch):
    kept, other = use(*ins)
    own = outs[0].shape[1]
    out_grad, query_grad, key_value_grad = outs
    out_grad[...] = kept[:, :own] + other[:, :own]
    query_grad[...] = kept[:, own : 2 * own] + other[:, own : 2 * own]
    for n in range(2):
        at = slice((2 + n) * own, (3 + n) * own)
        key_value_grad[:, n, :] = kept[:, at] + other[:, at]


def self_end(ins, outs, scratch):
    kept, other = use(*ins)
    own = outs[0].shape[1]
    for n, out in enumerate(outs):
        at = slice(n * own, (n + 1) * own)
        out[...] = kept[:, at] + other[:, at]


def swap_mp(v):
    return lax.ppermute(v, "mp", [(0, 1), (1, 0)])


def swap_dp(v, bit, dp_size):
    return lax.ppermute(v, "dp", [(i, i ^ bit) for i in range(dp_size)])


def relative_source(width, bits):
    shard = width // (1 << len(bits))
    me = lax.axis_index("dp")
    place = jnp.arange(width, dtype=jnp.int32)
    block = place // shard
    owner = jnp.zeros_like(block)
    for step, bit in enumerate(bits):
        owner = owner + ((block >> (len(bits) - 1 - step)) & 1) * bit
    return (owner ^ me) * shard + place % shard


class Halving:
    def __init__(self, chain, orders, groups, dp_size, name):
        self.chain, self.groups, self.dp_size, self.name = chain, groups, dp_size, name
        self.plan = tuple(
            (place, tuple((len(lhs), ordered, blocks) for lhs, ordered, rhs, blocks in items)) for place, bits, items in groups
        )
        self.model = orders[0].shape[0]
        self.columns = [
            sum(rhs[0].shape[-1] * len(blocks) for lhs, ordered, rhs, blocks in items) for place, bits, items in groups
        ]
        orders = orders[: 1 + max(place for place, bits, items in groups)]
        args = [(order, "h") for order in orders]
        outs = [(shaped((self.model // 2, sum(self.columns))), "v")]
        for place, bits, items in groups:
            for lhs, ordered, rhs, blocks in items:
                args += [(p, "h") for p in lhs] + [(p, "h") for p in rhs]
                if not ordered:
                    outs += [(shaped(p.shape[::-1], BF), "h") for p in lhs]
        made = chain(partial(grads_sent, self.plan), outs, args, 0, name + "_sent")
        self.turned = list(made[1:])
        self.first = chain.swap_dp(made[0], groups[0][1][0], dp_size)
        self.bits = [list(bits[1:]) for place, bits, items in groups]
        self.kept, self.other = [None] * len(groups), [None] * len(groups)

    def swap(self, n, sent):
        self.other[n] = self.chain.swap_dp(sent, self.bits[n].pop(0), self.dp_size)

    def keep(self, after=()):
        args, outs = [(self.first, "v")], []
        turned = list(self.turned)
        for columns, (place, bits, items) in zip(self.columns, self.groups):
            for lhs, ordered, rhs, blocks in items:
                for p in lhs:
                    args.append((p if ordered else turned.pop(0), "h"))
                args += [(p, "h") for p in rhs]
            outs += [(shaped((self.model // 4, columns)), "v")] * 2
        made = self.chain(partial(grads_kept, self.plan), outs, args, 0, self.name + "_kept", after=after)
        for n in range(len(self.groups)):
            self.kept[n] = made[2 * n + 1]
            self.swap(n, made[2 * n])

    def step(self, n, after=()):
        half = shaped((self.kept[n].shape[0] // 2, self.columns[n]))
        sent, self.kept[n] = self.chain(
            halve, [(half, "v"), (half, "v")], [(self.kept[n], "v"), (self.other[n], "v")], 0, self.name + str(n) + "_step",
            after=after,
        )
        self.swap(n, sent)

    def end(self, n, finish, outs):
        while self.bits[n]:
            self.step(n)
        return self.chain(
            finish, [(o, "v") for o in outs], [(self.kept[n], "v"), (self.other[n], "v")], 0, self.name + str(n) + "_end"
        )


def on_device(
    dp_size,
    tokens,
    frames,
    lengths,
    out_cot,
    self_query_key_value,
    self_qv_bias,
    self_output_weight,
    cross_query_weight,
    cross_kv,
    cross_bias,
    cross_output_weight,
    first_dense_weight,
    first_dense_bias,
    second_dense_weight,
    out_biases,
    norm_gains,
    norm_biases,
):
    _, slot, model = tokens.shape
    tok, frames, cot = tokens[0], frames[0], out_cot[0]
    real = frames.shape[0]
    padded = -(-real // 256) * 256
    own = self_output_weight.shape[0]
    ff = second_dense_weight.shape[0]
    cut = slot // 2 // 64 * 64
    low_rows, high_rows = slice(0, cut), slice(cut, slot)
    w3 = self_query_key_value.transpose(1, 0, 2)
    w2kv = cross_kv.transpose(1, 0, 2)
    fb = first_dense_bias[None]
    gains, shifts, ob = norm_gains, norm_biases, out_biases
    bits = [1 << i for i in range(dp_size.bit_length() - 1)]
    turned_bits = bits[:1] + bits[2:] + bits[1:2]
    sources = jnp.stack([relative_source(model, bits), relative_source(model, turned_bits)], axis=1)
    chain = Chain(norm_gains)
    spot = (lax.axis_index("dp") & 3).astype(jnp.int32)
    spots = spot.reshape(1)

    def count(rows):
        return rows.stop - rows.start

    def sized(rows, width, dtype=F32):
        return shaped((count(rows), width), dtype)

    def attended(rows):
        return [(sized(rows, own, BF), "h"), (sized(rows, own), "h"), (shaped((8, count(rows))), "h"), (sized(rows, model), "v")]

    def fetched(weight, parts):
        block = weight.shape[0] // parts
        at = (spot & (parts - 1)) * block
        return lax.dynamic_slice_in_dim(weight, at, block, 0).astype(F32)

    made = chain(
        partial(self_start, cut),
        [(sized(low_rows, model, BF), "h"), (sized(high_rows, model, BF), "h")] + [(shaped((slot, own), BF), "h")] * 3
        + attended(high_rows),
        [(tok, "h"), (gains, "h"), (shifts, "h"), (self_qv_bias, "h"), (w3, "h"), (lengths, "s"), (self_output_weight, "h")],
        0,
        "self_start",
        scratch=[pltpu.VMEM((count(high_rows), LANES), F32), pltpu.VMEM((slot, model), BF)],
    )
    x1_l, x1_h, q1, k1, v1, mix1_h, out1_h, lse1_h, part1_h = made
    other1_h = chain.swap_mp(part1_h)
    mix1_l, out1_l, lse1_l, part1_l = chain(
        partial(self_next, low_rows),
        attended(low_rows),
        [(q1, "h"), (k1, "h"), (v1, "h"), (lengths, "s"), (self_output_weight, "h")],
        0,
        "self_next",
        scratch=[pltpu.VMEM((count(low_rows), LANES), F32)],
    )
    other1_l = chain.swap_mp(part1_l)
    k2, v2, turned_frames, order, order_turned = chain(
        frames_start,
        [(shaped((padded, own), BF), "h")] * 2 + [(shaped((model, padded), BF), "h")] + [(shaped((model, model), BF), "h")] * 2,
        [(frames, "h"), (w2kv, "h"), (cross_bias, "h"), (sources, "h")],
        0,
        "frames_start",
        scratch=[pltpu.VMEM((padded, model), BF)],
    )
    orders = (order, order_turned)

    def turned(plan, parts):
        used = orders[: 1 + max(place for place, _ in plan)]
        return chain(
            partial(turn, plan),
            [(shaped((model, parts[part].shape[0]), BF), "h") for _, part in plan],
            [(o, "h") for o in used] + [(p, "h") for p in parts],
            0,
            "turn",
        )


    def cross(rows, mine, other):
        return chain(
            partial(cross_start, rows, real),
            [(sized(rows, model), "h"), (sized(rows, model, BF), "h"), (sized(rows, own, BF), "h")] + attended(rows),
            [(mine, "v"), (other, "v"), (tok, "h"), (ob, "h"), (gains, "h"), (shifts, "h"), (cross_bias, "h"),
             (cross_query_weight, "h"), (k2, "h"), (v2, "h"), (cross_output_weight, "h")],
            0,
            "cross_start",
            scratch=[pltpu.VMEM((count(rows), LANES), F32)],
        )

    s1_h, x2_h, q2_h, mix2_h, out2_h, lse2_h, part2_h = cross(high_rows, part1_h, other1_h)
    other2_h = chain.swap_mp(part2_h)
    s1_l, x2_l, q2_l, mix2_l, out2_l, lse2_l, part2_l = cross(low_rows, part1_l, other1_l)
    other2_l = chain.swap_mp(part2_l)
    x1t_h, x1t_l, x2t_h, x2t_l = turned(((0, 0), (0, 1), (0, 2), (0, 3)), (x1_h, x1_l, x2_h, x2_l))

    def dense(rows, s1, mine, other):
        return chain(
            dense_start,
            [(sized(rows, model), "h"), (sized(rows, model, BF), "h"), (sized(rows, ff, BF), "h"), (sized(rows, ff), "h"),
             (sized(rows, model), "v")],
            [(mine, "v"), (other, "v"), (s1, "h"), (ob, "h"), (gains, "h"), (shifts, "h"), (fb, "h"),
             (first_dense_weight, "h"), (second_dense_weight, "h")],
            0,
            "dense_start",
        )

    s2_h, x3_h, act_h, slope_h, part3_h = dense(high_rows, s1_h, part2_h, other2_h)
    other3_h = chain.swap_mp(part3_h)
    s2_l, x3_l, act_l, slope_l, part3_l = dense(low_rows, s1_l, part2_l, other2_l)
    other3_l = chain.swap_mp(part3_l)
    x3o_h, x3o_l = turned(((1, 0), (1, 1)), (x3_h, x3_l))

    def dense_b(rows, s2, mine, other, slope):
        return chain(
            partial(dense_back, rows),
            [(sized(rows, model, BF), "h"), (sized(rows, model), "h"), (sized(rows, model, BF), "h"),
             (sized(rows, ff, BF), "h"), (sized(rows, model), "v"), (shaped((8, model)), "v"), (shaped((8, ff)), "v")],
            [(mine, "v"), (other, "v"), (s2, "h"), (ob, "h"), (gains, "h"), (shifts, "h"), (cot, "h"), (lengths, "s"),
             (second_dense_weight, "h"), (slope, "h"), (first_dense_weight, "h")],
            6 * count(rows) * model * ff,
            "dense_back",
        )

    y_h, g3_h, low3_h, hid_h, part4_h, sum3_h, hsum_h = dense_b(high_rows, s2_h, part3_h, other3_h, slope_h)
    other4_h = chain.swap_mp(part4_h)
    y_l, g3_l, low3_l, hid_l, part4_l, sum3_l, hsum_l = dense_b(low_rows, s2_l, part3_l, other3_l, slope_l)

    denses = Halving(
        chain,
        orders,
        [
            (0, bits, [((low3_h, low3_l), False, (act_h, act_l), (0,))]),
            (1, turned_bits, [((x3o_h, x3o_l), True, (hid_h, hid_l), (0,))]),
        ],
        dp_size,
        "dense",
    )
    other4_l = chain.swap_mp(chain.tie(part4_l))
    wq_0 = chain.swap_mp(chain.tie(fetched(cross_query_weight, 2)))
    chain.pause(other4_h)
    denses.keep()
    all_rows = slice(0, slot)

    def block_sizes(dtype, width):
        return [(sized(high_rows, width, dtype), "h"), (sized(low_rows, width, dtype), "h")]

    heads = [pltpu.VMEM((slot, own), BF), pltpu.VMEM((slot, own), F32)]
    joined = [pltpu.VMEM((slot, own), BF), pltpu.VMEM((slot, own), F32), pltpu.VMEM((8, slot), F32)]
    which = lax.axis_index("mp").astype(jnp.int32).reshape(1)
    half_width = model // 2
    cuts = [-(-real * n // (8 * PIECES)) * 8 for n in range(PIECES)] + [-(-real // 8) * 8]
    g2_h, low2_h, g2_l, low2_l, lq2_h, lq2_l, part5, sum2, lk2, lv2, *frames_parts = chain(
        partial(cross_back, cut, real),
        [(sized(high_rows, model), "h"), (sized(high_rows, model, BF), "h"), (sized(low_rows, model), "h"),
         (sized(low_rows, model, BF), "h")] + block_sizes(BF, own)
        + [(shaped((slot, own)), "v"), (shaped((8, model)), "v")] + [(shaped((padded, own), BF), "h")] * 2
        + [(shaped((cuts[n + 1] - cuts[n], half_width)), "r") for n in range(PIECES)],
        [(part4_h, "h"), (other4_h, "h"), (s2_h, "h"), (g3_h, "h"), (q2_h, "h"), (out2_h, "h"), (lse2_h, "h"),
         (part4_l, "h"), (other4_l, "h"), (s2_l, "h"), (g3_l, "h"), (q2_l, "h"), (out2_l, "h"), (lse2_l, "h"),
         (gains, "h"), (cross_output_weight, "h"), (k2, "h"), (v2, "h"), (which, "s"), (w2kv, "h")],
        0,
        "cross_back",
        scratch=heads + joined + [pltpu.VMEM((padded, half_width), F32), pltpu.SemaphoreType.DMA((PIECES,))],
    )
    other5 = chain.swap_mp(part5)
    wq_1 = chain.later(lambda tied=chain.link: swap_dp(lax.optimization_barrier((wq_0.value, tied))[0], 1, dp_size))
    steps(chain, [(denses, 0), (denses, 1)], (wq_0,))
    crosses = Halving(
        chain,
        orders,
        [
            (
                0,
                bits,
                [
                    ((low2_h, low2_l), False, (mix2_h, mix2_l), (0,)),
                    ((x2t_h, x2t_l), True, (lq2_h, lq2_l), (0,)),
                    ((turned_frames,), True, (lk2,), (0,)),
                    ((turned_frames,), True, (lv2,), (0,)),
                ],
            )
        ],
        dp_size,
        "cross",
    )
    frames_other = [chain.swap_mp(chain.tie(frames_parts[0]))]
    chain.pause(other5)
    crosses.keep()
    frames_other.append(chain.swap_mp(chain.tie(frames_parts[1])))
    g1_h, low1_h, g1_l, low1_l, l3_h, l3_l, part6_h, part6_l, sum1 = chain(
        partial(self_back, cut),
        [(sized(high_rows, model), "h"), (sized(high_rows, model, BF), "h"), (sized(low_rows, model), "h"),
         (sized(low_rows, model, BF), "h"), (shaped((3, count(high_rows), own), BF), "h"),
         (shaped((3, count(low_rows), own), BF), "h"), (sized(high_rows, model), "v"), (sized(low_rows, model), "v"),
         (shaped((8, model)), "v")],
        [(spots, "s"), (part5, "h"), (other5, "h"), (cross_query_weight, "h"), (wq_0, "h"), (wq_1, "h"), (gains, "h"),
         (self_output_weight, "h"), (q1, "h"), (k1, "h"), (v1, "h"), (w3, "h"), (lengths, "s"),
         (s1_h, "h"), (g2_h, "h"), (out1_h, "h"), (lse1_h, "h"), (s1_l, "h"), (g2_l, "h"), (out1_l, "h"), (lse1_l, "h")],
        0,
        "self_back",
        scratch=heads + [pltpu.VMEM((model, own), BF)] + joined + [pltpu.VMEM((2, slot, own), BF), pltpu.VMEM((slot, model), F32)],
    )
    other6_h = chain.swap_mp(part6_h)
    steps(chain, [(denses, 0), (denses, 1)], (frames_other[0],))
    selves = Halving(
        chain,
        orders,
        [
            (
                0,
                bits,
                [((low1_h, low1_l), False, (mix1_h, mix1_l), (0,)), ((x1t_h, x1t_l), True, (l3_h, l3_l), (0,))],
            ),
            (0, bits, [((x1t_h, x1t_l), True, (l3_h, l3_l), (1, 2))]),
        ],
        dp_size,
        "self",
    )
    other6_l = chain.swap_mp(chain.tie(part6_l))
    shard = model // dp_size
    crosses.step(0, (frames_other[1],))
    t_high, sum0_h = chain(
        partial(tokens_end, high_rows),
        [(sized(high_rows, model), "h"), (shaped((8, model)), "h")],
        [(tok, "h"), (gains, "h"), (g1_h, "h"), (part6_h, "v"), (other6_h, "v"), (lengths, "s")],
        0,
        "tokens_end",
        scratch=[pltpu.VMEM((8, model), F32)],
    )
    second_turned, first_grad = ends(chain, [(denses, 0), (denses, 1)], shaped((shard, ff)))
    selves.keep()
    tokens_grad, total, y = chain(
        partial(tokens_end, low_rows),
        [(shaped((slot, model)), "h"), (shaped((13 + ff // model, model)), "v"), (shaped((slot, model), BF), "h")],
        [(tok, "h"), (gains, "h"), (g1_l, "h"), (part6_l, "v"), (other6_l, "v"), (t_high, "h"), (sum0_h, "h"),
         (sum1, "h"), (sum2, "h"), (sum3_h, "h"), (sum3_l, "h"), (hsum_h, "h"), (hsum_l, "h"), (y_l, "h"), (y_h, "h")],
        0,
        "tokens_end",
        scratch=[pltpu.VMEM((8, model), F32)],
    )
    small_bits = bits[:1] + bits[2:] + bits[1:2]

    def small_step(total, other):
        (total,) = chain(plain_end, [(shaped(total.shape), "v")], [(total, "v"), (other, "v")], 0, "small_step")
        return total, chain.swap_dp(total, small_bits.pop(0), dp_size)

    small_other = chain.swap_dp(total, small_bits.pop(0), dp_size)
    frames_other.append(chain.swap_mp(chain.tie(frames_parts[2])))
    crosses.step(0)
    selves.step(0)
    total, small_other = small_step(total, small_other)
    frames_other.append(chain.swap_mp(chain.tie(frames_parts[3])))
    selves.step(1, (frames_other[2],))
    cross_out_grad, cross_q_grad, cross_kv_grad = crosses.end(
        0, cross_end, [shaped((shard, own)), shaped((shard, own)), shaped((shard, 2, own))]
    )
    selves.step(0)
    total, small_other = small_step(total, small_other)
    selves.step(1)
    while small_bits:
        total, small_other = small_step(total, small_other)
    (frames_grad,) = chain(
        frames_kept, [(shaped((real, 1, half_width)), "r")],
        [(which, "s"), (lk2, "h"), (lv2, "h"), (w2kv, "h")] + [(o, "h") for o in frames_other],
        0, "frames_kept",
        scratch=[pltpu.VMEM((padded, half_width), F32), pltpu.VMEM((real, half_width), F32), pltpu.SemaphoreType.DMA],
    )
    self_out_grad, q_grad = selves.end(0, self_end, [shaped((shard, own))] * 2)
    k_grad, v_grad = selves.end(1, self_end, [shaped((shard, own))] * 2)
    gains_grad, shifts_grad, ob_grad, svb_grad, cvb_grad, fb_grad = chain(
        small_end,
        [(shaped((4, model)), "v"), (shaped((4, model)), "v"), (shaped((3, model)), "v"), (shaped((2, own)), "v"),
         (shaped((2, own)), "v"), (shaped((ff // model, model)), "v")],
        [(total, "v"), (small_other, "v")],
        0,
        "small_end",
    )
    return (
        y[None],
        tokens_grad[None],
        frames_grad.transpose(1, 0, 2),
        jnp.stack([q_grad, k_grad, v_grad], axis=1),
        svb_grad,
        self_out_grad.T,
        cross_q_grad,
        cross_kv_grad,
        cvb_grad,
        cross_out_grad.T,
        first_grad,
        fb_grad.reshape(ff),
        second_turned.T,
        ob_grad,
        gains_grad,
        shifts_grad,
    )


def solution(mesh):
    in_specs = (
        P("dp", None, None),
        P("dp", None, None),
        P("dp"),
        P("dp", None, None),
        P(None, None, "mp"),
        P(None, "mp"),
        P("mp", None),
        P(None, "mp"),
        P(None, None, "mp"),
        P(None, "mp"),
        P("mp", None),
        P(None, "mp"),
        P("mp"),
        P("mp", None),
        P(),
        P(),
        P(),
    )
    out_specs = (
        P("dp", None, None),
        P("dp", None, None),
        P("dp", None, "mp"),
        P("dp", None, "mp"),
        P(None, "mp"),
        P("mp", "dp"),
        P("dp", "mp"),
        P("dp", None, "mp"),
        P(None, "mp"),
        P("mp", "dp"),
        P("dp", "mp"),
        P("mp"),
        P("mp", "dp"),
        P(),
        P(),
        P(),
    )
    return jax.shard_map(
        partial(on_device, mesh.shape["dp"]),
        mesh=mesh,
        in_specs=in_specs,
        out_specs=out_specs,
        check_vma=False,
    )
```

```python
from functools import partial

import jax
import jax.numpy as jnp
from jax import lax
from jax.experimental import pallas as pl
from jax.experimental.pallas import tpu as pltpu
from jax.sharding import PartitionSpec as P

F32 = jnp.float32
BF = jnp.bfloat16
HEAD_DIM = 64
LANES = 128
NEG = -1e30
COST = {"self_start": 2.0, "self_next": 1.3, "turn": 1.0, "frames_start": 3.0, "cross_start": 2.7, "dense_start": 2.4,
        "dense_back": 2.4, "dense_sent": 6.0, "dense_kept": 6.0, "cross_back": 20.0, "self_back": 12.0,
        "cross_sent": 6.0, "cross_kept": 5.0, "self_sent": 5.0, "self_kept": 4.0, "tokens_end": 5.0, "frames_kept": 6.0,
        "small_end": 1.0, "pause": 8.0}
SCALE = 1.5e10
PIECES = 4
BACK_BLOCKS = 2
ROW_BLOCKS = 1
BYTES = 6.4e-3
PINNED = ("h", "t", "r")


def shaped(shape, dtype=F32):
    return jax.ShapeDtypeStruct(tuple(shape), dtype)


def dg(a, b, ca, cb):
    return lax.dot_general(a, b, (((ca,), (cb,)), ((), ())), preferred_element_type=F32)


def nn(a, b):
    return dg(a, b, 1, 0)


def nt(a, b):
    return dg(a, b, 1, 1)


def tn(a, b):
    return dg(a, b, 0, 0)


class Feed:
    def __init__(self, source, target, sem):
        self.copy = pltpu.make_async_copy(source, target, sem)
        self.copy.start()
        self.target = target
        self.pending = True

    def ready(self):
        if self.pending:
            self.copy.wait()
            self.pending = False
        return self.target


class Drain:
    def __init__(self, source, target, sem):
        self.ref = source
        self.copy = pltpu.make_async_copy(source, target, sem)
        self.pending = True

    def flush(self):
        if self.pending:
            self.copy.start()
            self.pending = False


def use(*inputs):
    made = [i.ready() if isinstance(i, Feed) else i for i in inputs]
    return made if len(made) > 1 else made[0]


def flush(*outputs):
    for o in outputs:
        if isinstance(o, Drain):
            o.flush()


def into(*outputs):
    made = [o.ref if isinstance(o, Drain) else o for o in outputs]
    return made if len(made) > 1 else made[0]


class Pending:
    def __init__(self, make):
        self.make, self.value = make, None


class Chain:
    def __init__(self, seed):
        self.link = seed
        self.pending = []

    def pause(self, *after):
        self(lambda ins, outs, scratch: None, [], [], 0, "pause", after=after)

    def later(self, make):
        self.pending.append(Pending(make))
        return self.pending[-1]

    def settle(self):
        for item in reversed(self.pending):
            item.value = item.make()
        self.pending = []

    def swap_mp(self, v):
        return self.later(lambda: swap_mp(v))

    def swap_dp(self, v, bit, dp_size):
        return self.later(lambda: swap_dp(v, bit, dp_size))

    def tie(self, value):
        return lax.optimization_barrier((value, self.link))[0]

    def __call__(self, kernel, outs, args, flops, name, scratch=(), after=()):
        place = {
            "v": pl.BlockSpec(memory_space=pltpu.VMEM),
            "h": pl.BlockSpec(memory_space=pltpu.HBM),
            "s": pl.BlockSpec(memory_space=pltpu.SMEM),
        }
        args = [(self.link, "t")] + [(a, "t") for a in after] + list(args)
        first = 1 + len(after)
        if any(isinstance(a, Pending) and a.value is None for a, _ in args):
            self.settle()
        args = [(a.value if isinstance(a, Pending) else a, k) for a, k in args]
        outs = [(shaped((8, LANES)), "t")] + list(outs)
        held = []
        for item, kind in args[first:] + outs[1:]:
            if kind == "h":
                held.append(pltpu.VMEM(item.shape, item.dtype))
        n_in, n_out = len(args), len(outs)

        def body(*refs):
            ins, results = refs[first:n_in], refs[n_in + 1 : n_in + n_out]
            rest = refs[n_in + n_out :]
            own, bufs, sems = rest[: len(scratch)], list(rest[len(scratch) : -1]), rest[-1]
            at = 0
            feeds, drains = [], []
            for ref, (_, kind) in zip(ins, args[first:]):
                if kind == "h":
                    feeds.append(Feed(ref, bufs[at], sems.at[at]))
                    at += 1
                else:
                    feeds.append(ref)
            for ref, (_, kind) in zip(results, outs[1:]):
                if kind == "h":
                    drains.append(Drain(bufs[at], ref, sems.at[at]))
                    at += 1
                else:
                    drains.append(ref)
            kernel(feeds, drains, own)
            for feed in feeds:
                use(feed)
            flush(*drains)
            for d in drains:
                if isinstance(d, Drain):
                    d.copy.wait()

        moved = 0
        for item, kind in args + outs:
            size = jnp.dtype(item.dtype).itemsize
            for d in item.shape:
                size *= d
            moved += size
        place["t"] = place["r"] = place["h"]
        made = pl.pallas_call(
            body,
            out_shape=tuple(pltpu.HBM(o.shape, o.dtype) if k in PINNED else o for o, k in outs),
            in_specs=[place[k] for _, k in args],
            out_specs=tuple(place[k] for _, k in outs),
            scratch_shapes=list(scratch) + held + [pltpu.SemaphoreType.DMA((max(1, len(held)),))],
            compiler_params=pltpu.CompilerParams(vmem_limit_bytes=28 * 1024 * 1024),
            cost_estimate=pl.CostEstimate(flops=int(COST.get(name, 1.0) * SCALE), transcendentals=0, bytes_accessed=int(COST.get(name, 1.0) * SCALE * BYTES)),
            name=name,
        )(*[pltpu.with_memory_space_constraint(a, pltpu.HBM) if k in PINNED else a for a, k in args])
        self.link = made[0]
        return made[1:]


def standard(stream):
    centred = stream - jnp.mean(stream, axis=1, keepdims=True)
    spread = jnp.mean(centred * centred, axis=1, keepdims=True)
    scale = lax.rsqrt(spread + 1e-05)
    return centred * scale, scale


def norm_back(grad, unit, scale, gain):
    lifted = grad * gain
    mean_plain = jnp.mean(lifted, axis=1, keepdims=True)
    mean_cross = jnp.mean(lifted * unit, axis=1, keepdims=True)
    return scale * (lifted - mean_plain - unit * mean_cross)


def column_sums(values):
    return jnp.sum(values, axis=0, keepdims=True)


def head_lanes(which):
    lane = lax.broadcasted_iota(jnp.int32, (1, LANES), 1)
    return (lane < HEAD_DIM) if which == 0 else (lane >= HEAD_DIM)


def only(mask, values):
    return jnp.where(mask, values, jnp.zeros_like(values))


def pair_slice(pair):
    return pl.ds(pl.multiple_of(pair * LANES, LANES), LANES)


def attend_rows(q_ref, k_ref, v_ref, rows, keys, bias, mixed_ref, out_ref, lse_ref, lse_all, blocks):
    lane = lax.broadcasted_iota(jnp.int32, (1, LANES), 1)
    size = (rows.stop - rows.start) // blocks

    def body(step, carry):
        pair, part = (step, 0) if blocks == 1 else (step // blocks, step % blocks)
        at = pair_slice(pair)
        here = place(part, size) if blocks > 1 else slice(0, size)
        theirs = pl.ds(pl.multiple_of(rows.start + part * size, 16), size) if blocks > 1 else rows
        k_pair, v_pair, q_pair = k_ref[0:keys, at], v_ref[0:keys, at], q_ref[theirs, at]
        result, lse = None, lse_all[here]
        for which in range(2):
            mask = head_lanes(which)
            scores = nt(only(mask, q_pair), k_pair) + bias(part * size, size)
            top = jnp.max(scores, axis=1, keepdims=True)
            raised = jnp.exp(scores - top)
            total = jnp.sum(raised, axis=1, keepdims=True)
            value = nn(raised.astype(BF), v_pair) * (1.0 / total)
            result = value if which == 0 else jnp.where(mask, value, result)
            lse = jnp.where(lane == 2 * pair + which, top + jnp.log(total), lse)
        lse_all[here] = lse
        out_ref[here, at] = result
        mixed_ref[here, at] = result.astype(BF)
        return carry

    lse_all[...] = jnp.zeros_like(lse_all)
    lax.fori_loop(0, q_ref.shape[1] // LANES * blocks, body, 0)
    lse_ref[...] = lse_all[...].T[0 : lse_ref.shape[0]]


def attend_back(q_ref, g_ref, o_ref, lse_ref, k_ref, v_ref, rows, keys, bias, dq_ref, emit, block=None):
    block = keys if block is None else block
    blocks = keys // block

    def body(step, carry):
        pair, part = (step, 0) if blocks == 1 else (step // blocks, step % blocks)
        at = pair_slice(pair)
        here = pl.ds(0, keys) if blocks == 1 else pl.ds(pl.multiple_of(part * block, block), block)
        k_pair, v_pair = k_ref[here, at], v_ref[here, at]
        q_pair, g_pair = q_ref[rows, at], g_ref[:, at]
        product = (g_pair.astype(F32) * o_ref[:, at]).T
        k_turned = k_pair.T
        parts, grad_k, grad_v = [], None, None
        for which in range(2):
            mask = head_lanes(which)
            q_head, g_head = only(mask, q_pair), only(mask, g_pair)
            inner = column_sums(product[which * HEAD_DIM : (which + 1) * HEAD_DIM])
            scores = nt(k_pair, q_head) + bias(part * block)
            probs = jnp.exp(scores - lse_ref[pl.ds(2 * pair + which, 1), :])
            grad_probs = nt(v_pair, g_head)
            grad_scores = (probs * (grad_probs - inner)).astype(BF)
            here_v = nn(probs.astype(BF), g_head)
            here_k = nn(grad_scores, q_head)
            grad_v = here_v if which == 0 else grad_v + here_v
            grad_k = here_k if which == 0 else grad_k + here_k
            parts.append(nn(k_turned[which * HEAD_DIM : (which + 1) * HEAD_DIM], grad_scores))
        emit(pair, part, at, here, grad_k, grad_v)
        grad_q = jnp.concatenate(parts, axis=0).T
        if blocks == 1:
            dq_ref[:, at] = grad_q
        else:
            dq_ref[:, at] += grad_q
        return carry

    if blocks > 1:
        dq_ref[...] = jnp.zeros_like(dq_ref)
    lax.fori_loop(0, q_ref.shape[1] // LANES * blocks, body, 0)


def causal_bias(start, count, keys, length):
    shape = (count, keys)
    query = lax.broadcasted_iota(jnp.int32, shape, 0) + start
    key = lax.broadcasted_iota(jnp.int32, shape, 1)
    return jnp.where((key <= query) & (key < length), 0.0, NEG).astype(F32)


def tail_bias(keys, real, turned, start=0):
    shape = (keys, 1) if turned else (1, keys)
    key = lax.broadcasted_iota(jnp.int32, shape, 0 if turned else 1) + start
    return jnp.where(key < real, 0.0, NEG).astype(F32)


def place(step, size):
    return pl.ds(pl.multiple_of(step * size, size), size)


def by_rows(count, work):
    size = count // 2

    def body(step, carry):
        work(place(step, size))
        return carry

    lax.fori_loop(0, count // size, body, 0)


def ordered(out, order, left):
    size = 2 * LANES

    def body(step, carry):
        out[place(step, size)] = nt(order[place(step, size)], left[...]).astype(BF)
        return carry

    lax.fori_loop(0, order.shape[0] // size, body, 0)


def self_start(cut, ins, outs, scratch):
    tok, gains, shifts, vb, w, length, wo = ins
    x_lo, x_hi, q_o, k_o, v_o = outs[:5]
    rows = slice(cut, tok.target.shape[0])
    low_ref, high_ref, q_ref, k_ref, v_ref = into(*outs[:5])
    tok, gains, shifts, vb, w = use(tok, gains, shifts, vb, w)
    x_all, size = scratch[1], tok.shape[0] // 2

    def work(here):
        unit, _ = standard(tok[here].astype(F32))
        x_all[here] = (unit * gains[0:1] + shifts[0:1]).astype(BF)

    by_rows(tok.shape[0], work)

    def body(step, carry):
        here = place(step, size)
        x = x_all[here]
        q_ref[here] = ((nn(x, w[0]) + vb[0:1]) * 0.125).astype(BF)
        k_ref[here] = nn(x, w[1]).astype(BF)
        v_ref[here] = (nn(x, w[2]) + vb[1:2]).astype(BF)
        return carry

    lax.fori_loop(0, 2, body, 0)
    low_ref[...] = x_all[:cut]
    high_ref[...] = x_all[cut:]
    flush(x_lo, x_hi, q_o, k_o, v_o)
    self_rows(rows, q_ref, k_ref, v_ref, length, wo, outs[5:], scratch)


def self_next(rows, ins, outs, scratch):
    q_ref, k_ref, v_ref, length, wo = ins
    self_rows(rows, *use(q_ref, k_ref, v_ref), length, wo, outs, scratch)


def self_rows(rows, q_ref, k_ref, v_ref, length, wo, outs, scratch):
    def bias(start, size):
        return causal_bias(rows.start + start, size, rows.stop, length[0])

    mixed, out, lse, part = into(*outs)
    attend_rows(q_ref, k_ref, v_ref, rows, rows.stop, bias, mixed, out, lse, scratch[0], 1)
    flush(*outs[:3])
    part[...] = nn(mixed[...], use(wo)[...])


def turn(plan, ins, outs, scratch):
    orders = ins[: 1 + max(which for which, _ in plan)]
    parts = ins[len(orders) :]
    for (which, part), out in zip(plan, outs):
        ordered(into(out), use(orders[which]), use(parts[part]))
        flush(out)


def frames_start(ins, outs, scratch):
    frames, w, vb, sources = ins
    k_o, v_o, t_o, order_o, other_o = outs
    k_ref, v_ref, t_ref, order, other = into(*outs)
    (frames_all,) = scratch
    sources = use(sources)
    column = lax.broadcasted_iota(jnp.int32, order.shape, 1)
    order[...] = jnp.where(column == sources[:, 0:1], 1.0, 0.0).astype(BF)
    other[...] = jnp.where(column == sources[:, 1:2], 1.0, 0.0).astype(BF)
    flush(order_o, other_o)
    real, padded = frames.target.shape[0], k_ref.shape[0]
    if padded > real:
        low = real // 16 * 16
        frames_all[low:padded] = jnp.zeros((padded - low, frames_all.shape[1]), BF)
    frames, w, vb = use(frames, w, vb)
    frames_all[0:real] = frames[...]
    size = padded // 3

    def body(step, carry):
        rows = frames_all[place(step, size)]
        k_ref[place(step, size)] = nn(rows, w[0]).astype(BF)
        v_ref[place(step, size)] = (nn(rows, w[1]) + vb[1:2]).astype(BF)
        t_ref[:, place(step, size)] = nt(order[...], rows).astype(BF)
        return carry

    lax.fori_loop(0, 3, body, 0)


def assemble(out, spot, pieces):
    block = out.shape[0] // len(pieces)
    for j, piece in enumerate(pieces):
        at = pl.multiple_of(((spot[0] & (len(pieces) - 1)) ^ j) * block, 16)
        out[pl.ds(at, block), :] = use(piece)[...].astype(BF)


def cross_start(rows, real, ins, outs, scratch):
    mine, other, tok, ob, gains, shifts, vb, wq, k_in, v_in, wo = ins
    s_o, x_o, q_o, m_o, out_o, lse_o, part = outs
    mixed, out, lse, part = into(m_o, out_o, lse_o, part)
    s_ref, x_ref, q_ref = into(s_o, x_o, q_o)
    mine, other, tok, ob, gains, shifts = use(mine, other, tok, ob, gains, shifts)
    block = tok.at[rows]

    def work(here):
        stream = block[here].astype(F32) + (mine[here] + other[here]) + ob[0:1]
        s_ref[here] = stream
        unit, _ = standard(stream)
        x_ref[here] = (unit * gains[1:2] + shifts[1:2]).astype(BF)

    by_rows(s_ref.shape[0], work)
    flush(s_o)
    vb, wq = use(vb, wq)
    q_ref[...] = ((nn(x_ref[...], wq[...]) + vb[0:1]) * 0.125).astype(BF)
    flush(x_o, q_o)
    k_ref, v_ref = use(k_in, v_in)
    keys = k_ref.shape[0]
    tail = tail_bias(keys, real, False)
    attend_rows(q_ref, k_ref, v_ref, slice(0, x_ref.shape[0]), keys, lambda start, size: tail, mixed, out, lse, scratch[0], ROW_BLOCKS)
    flush(m_o, out_o, lse_o)
    part[...] = nn(mixed[...], use(wo)[...])


def dense_start(ins, outs, scratch):
    mine, other, s_in, ob, gains, shifts, fb, w1, w2 = ins
    s_o, x_o, a_o, d_o, part = outs
    s_ref, x_ref, active, slope, part = into(s_o, x_o, a_o, d_o, part)
    mine, other, s_in, ob, gains, shifts = use(mine, other, s_in, ob, gains, shifts)
    def work(here):
        stream = s_in[here] + (mine[here] + other[here]) + ob[1:2]
        s_ref[here] = stream
        unit, _ = standard(stream)
        x_ref[here] = (unit * gains[2:3] + shifts[2:3]).astype(BF)

    by_rows(s_ref.shape[0], work)
    flush(s_o, x_o)
    fb, w1, w2 = use(fb, w1, w2)
    wide = 3 * LANES

    def body(step, carry):
        at = pl.ds(pl.multiple_of(step * wide, wide), wide)
        hidden = nn(x_ref[...], w1[:, at]) + fb[:, at]
        below = 0.5 + 0.5 * lax.erf(hidden * 0.7071067811865476)
        slope[:, at] = below + hidden * (0.3989422804014327 * jnp.exp(-0.5 * hidden * hidden))
        value = (hidden * below).astype(BF)
        active[:, at] = value
        part[...] += nn(value, w2[at, :])
        return carry

    part[...] = jnp.zeros_like(part)
    lax.fori_loop(0, w1.shape[1] // wide, body, 0)


def dense_back(rows, ins, outs, scratch):
    mine, other, s_in, ob, gains, shifts, cot, length, w2, slope, w1 = ins
    y_o, g_o, low_o, hid_o, part, sums, hid_sums = outs
    out_ref, g_ref, low_ref, hid_ref, part, sums, hid_sums = into(*outs)
    mine, other, s_in, ob, gains, shifts = use(mine, other, s_in, ob, gains, shifts)
    block = use(cot).at[rows]
    sums[0:3] = jnp.zeros((3, sums.shape[1]), F32)

    def work(here):
        stream = s_in[here] + (mine[here] + other[here]) + ob[2:3]
        unit, scale = standard(stream)
        row = lax.broadcasted_iota(jnp.int32, (stream.shape[0], 1), 0) + (rows.start + here.start)
        valid = (row < length[0]).astype(F32)
        out_ref[here] = ((unit * gains[3:4] + shifts[3:4]) * valid).astype(BF)
        incoming = block[here].astype(F32) * valid
        grad = norm_back(incoming, unit, scale, gains[3:4])
        g_ref[here] = grad
        low_ref[here] = grad.astype(BF)
        sums[0:1] += column_sums(incoming * unit)
        sums[1:2] += column_sums(incoming)
        sums[2:3] += column_sums(grad)

    by_rows(g_ref.shape[0], work)
    flush(y_o, g_o, low_o)
    w2, slope, w1 = use(w2, slope, w1)
    wide = 3 * LANES

    def body(step, carry):
        at = pl.ds(pl.multiple_of(step * wide, wide), wide)
        low = (slope[:, at] * nt(low_ref[...], w2[at, :])).astype(BF)
        hid_ref[:, at] = low
        hid_sums[0:1, at] = column_sums(low.astype(F32))
        part[...] += nt(low, w1[:, at])
        return carry

    part[...] = jnp.zeros_like(part)
    lax.fori_loop(0, w1.shape[1] // wide, body, 0)


def back_head(incoming_at, ins, outs, gm, gains, wo, sums, level, more):
    s_in, g_in = ins
    g_o, low_o = outs
    g_ref, low_ref = into(g_o, low_o)
    s_in, g_in, gains = use(s_in, g_in, gains)
    if not more:
        sums[0:3] = jnp.zeros((3, sums.shape[1]), F32)

    def work(here):
        incoming = incoming_at(here)
        unit, scale = standard(s_in[here])
        grad = g_in[here] + norm_back(incoming, unit, scale, gains[level : level + 1])
        g_ref[here] = grad
        low_ref[here] = grad.astype(BF)
        sums[0:1] += column_sums(incoming * unit)
        sums[1:2] += column_sums(incoming)
        sums[2:3] += column_sums(grad)

    by_rows(g_ref.shape[0], work)
    flush(g_o, low_o)
    gm[...] = nt(low_ref[...], use(wo)[...]).astype(BF)


def gather_heads(count, q_all, o_all, lse_all, refs):
    start = 0
    for q_ref, out_in, lse in refs:
        q_ref, out_in, lse = use(q_ref, out_in, lse)
        stop = start + out_in.shape[0]
        if q_all is not None:
            q_all[start:stop] = q_ref[...]
        o_all[start:stop] = out_in[...]
        lse_all[:, start:stop] = lse[...]
        start = stop


def cross_back(cut, real, ins, outs, scratch):
    blocks = (ins[:7], ins[7:14])
    gains, wo, k_in, v_in, which, kv = ins[14:20]
    lq_outs, part, sums, dk_o, dv_o = outs[4:6], outs[6], outs[7], outs[8], outs[9]
    gm, dq, q_all, o_all, lse_all, held, frame_sems = scratch
    part, sums, dk, dv = into(part, sums, dk_o, dv_o)
    start = 0
    for n, (mine, other, s_in, g_in, q_ref, out_in, lse) in enumerate(blocks):
        mine, other = use(mine, other)
        stop = start + mine.shape[0]
        back_head(lambda here, mine=mine, other=other: mine[here] + other[here], (s_in, g_in), outs[2 * n : 2 * n + 2], gm.at[start:stop], gains, wo, sums, 2, n > 0)
        start = stop
    gather_heads(start, q_all, o_all, lse_all, [b[4:7] for b in blocks])
    k_ref, v_ref = use(k_in, v_in)
    keys, width = k_ref.shape
    block = keys // BACK_BLOCKS

    def emit(pair, n, at, here, grad_k, grad_v):
        dk[here, at] = grad_k.astype(BF)
        dv[here, at] = grad_v.astype(BF)

    attend_back(q_all, gm, o_all, lse_all, k_ref, v_ref, slice(0, start), keys,
                lambda first: tail_bias(block, real, True, first), dq, emit, block)
    flush(dk_o, dv_o)
    low_q = (dq[...].astype(BF).astype(F32) * 0.125).astype(BF)
    part[...] = low_q.astype(F32)
    high = start - cut
    for o, rows in ((lq_outs[0], slice(0, high)), (lq_outs[1], slice(high, start))):
        into(o)[...] = low_q[rows]
        flush(o)
    sums[3:4, 0:width] = column_sums(low_q.astype(F32))
    sums[3:4, width : 2 * width] = column_sums(dv[0:real].astype(F32))
    width = held.shape[1]
    frames_terms(held, dk, dv, use(kv), pl.ds(pl.multiple_of((1 - which[0]) * width, width), width))
    start, copies = 0, []
    for n, out in enumerate(outs[10:]):
        copies.append(pltpu.make_async_copy(held.at[start : start + out.shape[0]], out, frame_sems.at[n]))
        copies[n].start()
        start += out.shape[0]
    for copy in copies:
        copy.wait()


def frames_terms(held, lk, lv, w, at):
    size = lk.shape[0] // 3

    def body(step, carry):
        rows = place(step, size)
        held[rows] = nt(lk[rows], w[0, at, :]) + nt(lv[rows], w[1, at, :])
        return carry

    lax.fori_loop(0, 3, body, 0)


def frames_kept(ins, outs, scratch):
    which, lk, lv, w = use(*ins[:4])
    held, final, sem = scratch
    start, width = 0, held.shape[1]
    frames_terms(held, lk, lv, w, pl.ds(pl.multiple_of(which[0] * width, width), width))
    for other in ins[4:]:
        other = use(other)
        rows = slice(start, min(start + other.shape[0], final.shape[0]))
        final[rows] = held[rows] + other[0 : rows.stop - start]
        start = rows.stop
    copy = pltpu.make_async_copy(final, outs[0].at[:, 0, :], sem)
    copy.start()
    copy.wait()


def self_back(cut, ins, outs, scratch):
    spot, mine, other, wq = ins[:4]
    pieces, (gains, wo, q_in, k_in, v_in, w, length) = ins[4:6], ins[6:13]
    blocks = (ins[13:17], ins[17:21])
    l3_outs, part_high, part_low, sums = outs[4:6], outs[6], outs[7], outs[8]
    gm, dq, wq_other, q_all, o_all, lse_all, lows, incoming = scratch
    l3_high, l3_low, part_high, part_low, sums = into(*l3_outs, part_high, part_low, sums)
    assemble(wq_other, spot, pieces)
    mine, other, wq = use(mine, other, wq)
    incoming[...] = nt(mine[...].astype(BF), wq[...]) + nt(other[...].astype(BF), wq_other[...])
    start = 0
    for n, (s_in, g_in, out_in, lse) in enumerate(blocks):
        stop = start + out_in.target.shape[0]
        block = incoming.at[start:stop]
        back_head(lambda here, block=block: block[here], (s_in, g_in), outs[2 * n : 2 * n + 2], gm.at[start:stop], gains, wo, sums, 1, n > 0)
        start = stop
    high = start - cut
    q_ref = use(q_in)
    q_all[0:high] = q_ref[cut:]
    q_all[high:] = q_ref[:cut]
    gather_heads(start, None, o_all, lse_all, [(b[2], b[2], b[3]) for b in blocks])
    k_ref, v_ref, w = use(k_in, v_in, w)
    width = k_ref.shape[1]
    block = start // 2

    def bias(first):
        lane = lax.broadcasted_iota(jnp.int32, (block, start), 1)
        query = jnp.where(lane < high, lane + cut, lane - high)
        key = lax.broadcasted_iota(jnp.int32, (block, start), 0) + first
        return jnp.where((key <= query) & (key < length[0]), 0.0, NEG).astype(F32)

    def emit(pair, n, at, here, grad_k, grad_v):
        lows[0, here, at] = grad_k.astype(BF)
        lows[1, here, at] = grad_v.astype(BF)

    attend_back(q_all, gm, o_all, lse_all, k_ref, v_ref, slice(0, start), start, bias, dq, emit, block)
    low_q = (dq[...].astype(BF).astype(F32) * 0.125).astype(BF)
    l3_high[0], l3_low[0] = low_q[:high], low_q[high:]
    for n in range(2):
        l3_high[1 + n], l3_low[1 + n] = lows[n, cut:], lows[n, :cut]
    flush(*l3_outs)
    for l3, part in ((l3_low, part_low), (l3_high, part_high)):
        part[...] = nt(l3[0], w[0]) + nt(l3[1], w[1]) + nt(l3[2], w[2])
    sums[3:4, 0:width] = column_sums(low_q.astype(F32))
    sums[3:4, width : 2 * width] = column_sums(lows[1].astype(F32))


def tokens_end(rows, ins, outs, scratch):
    tok, gains, g, mine, other = use(*ins[:5])
    block, (both,) = tok.at[rows], scratch
    target = into(outs[0]) if len(ins) == 6 else into(outs[0]).at[rows]
    both[...] = jnp.zeros_like(both)

    def work(here):
        unit, scale = standard(block[here].astype(F32))
        incoming = mine[here] + other[here]
        target[here] = g[here] + norm_back(incoming, unit, scale, gains[0:1])
        both[0:1] += column_sums(incoming * unit)
        both[1:2] += column_sums(incoming)

    by_rows(target.shape[0], work)
    if len(ins) == 6:
        flush(outs[0])
        into(outs[1])[...] = both[...]
        return
    out, total, y = into(*outs)
    gain, shift = both[0:1], both[1:2]
    earlier, first = use(*ins[5:7])
    sums, hid_sums, (y_low, y_high) = use(*ins[7:11]), use(*ins[11:13]), ins[13:15]
    out[rows.stop :] = earlier[...]
    flush(outs[0])
    y_low, y_high = use(y_low, y_high)
    y[0 : rows.stop] = y_low[...]
    y[rows.stop :] = y_high[...]
    flush(outs[2])
    total[0:1] = gain + first[0:1]
    total[4:5] = shift + first[1:2]
    for level, one in enumerate((sums[0][...], sums[1][...], sums[2][...] + sums[3][...])):
        total[1 + level : 2 + level] = one[0:1]
        total[5 + level : 6 + level] = one[1:2]
        total[8 + level : 9 + level] = one[2:3]
        if level < 2:
            total[11 + level : 12 + level] = one[3:4]
    model = total.shape[1]
    for piece in range(hid_sums[0].shape[1] // model):
        at = slice(piece * model, (piece + 1) * model)
        total[13 + piece : 14 + piece] = hid_sums[0][0:1, at] + hid_sums[1][0:1, at]


def small_end(ins, outs, scratch):
    mine, other = use(*ins)
    gain, shift, ob, svb, cvb, fb = into(*outs)
    total = mine[...] + other[...]
    half = svb.shape[1]
    gain[...] = total[0:4]
    shift[...] = total[4:8]
    ob[...] = total[8:11]
    for target, at in ((svb, 11), (cvb, 12)):
        target[0:1] = total[at : at + 1, :half]
        target[1:2] = total[at : at + 1, half:]
    fb[...] = total[13 : 13 + fb.shape[0]]


def blocks_of(rights, blocks, put):
    first = rights[0]
    if len(first.shape) == 3:
        low, wide = blocks[0], first.shape[2]

        def body(step, carry):
            put(step * wide, [r[low + step] for r in rights])
            return carry

        if len(blocks) == 1:
            body(0, 0)
        else:
            lax.fori_loop(0, len(blocks), body, 0)
        return len(blocks) * first.shape[2]
    put(0, [r[...] for r in rights])
    return first.shape[1]


def columns_at(start, width):
    return pl.ds(start if isinstance(start, int) else pl.multiple_of(start, LANES), width)


def grads_sent(plan, ins, outs, scratch):
    orders = ins[: 1 + max(which for which, _ in plan)]
    at, col = len(orders), 0
    out, turned = into(outs[0]), list(outs[1:])
    half = out.shape[0]
    for which, items in plan:
        for parts, done, blocks in items:
            lefts = ins[at : at + parts]
            at += parts
            made = []
            for left in lefts:
                left = use(left)
                if not done:
                    target = turned.pop(0)
                    ordered(into(target), use(orders[which]), left)
                    flush(target)
                    left = into(target)
                made.append(left)
            rights = [use(i) for i in ins[at : at + parts]]
            at += parts

            def put(start, values, col=col, made=made):
                total = None
                for left, value in zip(made, values):
                    term = nn(left[half:], value)
                    total = term if total is None else total + term
                out[:, columns_at(col + start, total.shape[1])] = total

            col += blocks_of(rights, blocks, put)


def grads_kept(plan, ins, outs, scratch):
    other, at, col = use(ins[0]), 1, 0
    half = other.shape[0]
    for n, (which, items) in enumerate(plan):
        sent, kept = into(outs[2 * n], outs[2 * n + 1])
        low, start = kept.shape[0], col
        for parts, done, blocks in items:
            lefts = [use(i) for i in ins[at : at + parts]]
            at += parts
            rights = [use(i) for i in ins[at : at + parts]]
            at += parts

            def put(first, values, col=col, lefts=lefts, sent=sent, kept=kept, start=start):
                total = None
                for left, value in zip(lefts, values):
                    term = nn(left[:half], value)
                    total = term if total is None else total + term
                width = total.shape[1]
                total = total + other[:, columns_at(col + first, width)]
                here = columns_at(col - start + first, width)
                sent[:, here] = total[low:]
                kept[:, here] = total[:low]

            col += blocks_of(rights, blocks, put)
        flush(outs[2 * n], outs[2 * n + 1])


def halve(ins, outs, scratch):
    for n in range(0, len(outs), 2):
        kept, other = use(*ins[n : n + 2])
        sent, out = into(*outs[n : n + 2])
        low = out.shape[0]
        out[...] = kept[0:low] + other[0:low]
        sent[...] = kept[low:] + other[low:]


def steps(chain, items, after=()):
    outs, args = [], []
    for h, n in items:
        half = shaped((h.kept[n].shape[0] // 2, h.columns[n]))
        outs += [(half, "v"), (half, "v")]
        args += [(h.kept[n], "v"), (h.other[n], "v")]
    made = chain(halve, outs, args, 0, "steps", after=after)
    for place, (h, n) in enumerate(items):
        h.kept[n] = made[2 * place + 1]
        h.swap(n, made[2 * place])


def ends(chain, items, shape):
    while items[0][0].bits[items[0][1]]:
        steps(chain, items)
    args = []
    for h, n in items:
        args += [(h.kept[n], "v"), (h.other[n], "v")]
    return chain(plain_end, [(shape, "v") for _ in items], args, 0, "ends")


def plain_end(ins, outs, scratch):
    for n, out in enumerate(outs):
        out[...] = use(ins[2 * n])[...] + use(ins[2 * n + 1])[...]


def cross_end(ins, outs, scratch):
    kept, other = use(*ins)
    own = outs[0].shape[1]
    out_grad, query_grad, key_value_grad = outs
    out_grad[...] = kept[:, :own] + other[:, :own]
    query_grad[...] = kept[:, own : 2 * own] + other[:, own : 2 * own]
    for n in range(2):
        at = slice((2 + n) * own, (3 + n) * own)
        key_value_grad[:, n, :] = kept[:, at] + other[:, at]


def self_end(ins, outs, scratch):
    kept, other = use(*ins)
    own = outs[0].shape[1]
    for n, out in enumerate(outs):
        at = slice(n * own, (n + 1) * own)
        out[...] = kept[:, at] + other[:, at]


def swap_mp(v):
    return lax.ppermute(v, "mp", [(0, 1), (1, 0)])


def swap_dp(v, bit, dp_size):
    return lax.ppermute(v, "dp", [(i, i ^ bit) for i in range(dp_size)])


def relative_source(width, bits):
    shard = width // (1 << len(bits))
    me = lax.axis_index("dp")
    place = jnp.arange(width, dtype=jnp.int32)
    block = place // shard
    owner = jnp.zeros_like(block)
    for step, bit in enumerate(bits):
        owner = owner + ((block >> (len(bits) - 1 - step)) & 1) * bit
    return (owner ^ me) * shard + place % shard


class Halving:
    def __init__(self, chain, orders, groups, dp_size, name):
        self.chain, self.groups, self.dp_size, self.name = chain, groups, dp_size, name
        self.plan = tuple(
            (place, tuple((len(lhs), ordered, blocks) for lhs, ordered, rhs, blocks in items)) for place, bits, items in groups
        )
        self.model = orders[0].shape[0]
        self.columns = [
            sum(rhs[0].shape[-1] * len(blocks) for lhs, ordered, rhs, blocks in items) for place, bits, items in groups
        ]
        orders = orders[: 1 + max(place for place, bits, items in groups)]
        args = [(order, "h") for order in orders]
        outs = [(shaped((self.model // 2, sum(self.columns))), "v")]
        for place, bits, items in groups:
            for lhs, ordered, rhs, blocks in items:
                args += [(p, "h") for p in lhs] + [(p, "h") for p in rhs]
                if not ordered:
                    outs += [(shaped(p.shape[::-1], BF), "h") for p in lhs]
        made = chain(partial(grads_sent, self.plan), outs, args, 0, name + "_sent")
        self.turned = list(made[1:])
        self.first = chain.swap_dp(made[0], groups[0][1][0], dp_size)
        self.bits = [list(bits[1:]) for place, bits, items in groups]
        self.kept, self.other = [None] * len(groups), [None] * len(groups)

    def swap(self, n, sent):
        self.other[n] = self.chain.swap_dp(sent, self.bits[n].pop(0), self.dp_size)

    def keep(self, after=()):
        args, outs = [(self.first, "v")], []
        turned = list(self.turned)
        for columns, (place, bits, items) in zip(self.columns, self.groups):
            for lhs, ordered, rhs, blocks in items:
                for p in lhs:
                    args.append((p if ordered else turned.pop(0), "h"))
                args += [(p, "h") for p in rhs]
            outs += [(shaped((self.model // 4, columns)), "v")] * 2
        made = self.chain(partial(grads_kept, self.plan), outs, args, 0, self.name + "_kept", after=after)
        for n in range(len(self.groups)):
            self.kept[n] = made[2 * n + 1]
            self.swap(n, made[2 * n])

    def step(self, n, after=()):
        half = shaped((self.kept[n].shape[0] // 2, self.columns[n]))
        sent, self.kept[n] = self.chain(
            halve, [(half, "v"), (half, "v")], [(self.kept[n], "v"), (self.other[n], "v")], 0, self.name + str(n) + "_step",
            after=after,
        )
        self.swap(n, sent)

    def end(self, n, finish, outs):
        while self.bits[n]:
            self.step(n)
        return self.chain(
            finish, [(o, "v") for o in outs], [(self.kept[n], "v"), (self.other[n], "v")], 0, self.name + str(n) + "_end"
        )


def on_device(
    dp_size,
    tokens,
    frames,
    lengths,
    out_cot,
    self_query_key_value,
    self_qv_bias,
    self_output_weight,
    cross_query_weight,
    cross_kv,
    cross_bias,
    cross_output_weight,
    first_dense_weight,
    first_dense_bias,
    second_dense_weight,
    out_biases,
    norm_gains,
    norm_biases,
):
    _, slot, model = tokens.shape
    tok, frames, cot = tokens[0], frames[0], out_cot[0]
    real = frames.shape[0]
    padded = -(-real // 256) * 256
    own = self_output_weight.shape[0]
    ff = second_dense_weight.shape[0]
    cut = slot // 2 // 64 * 64
    low_rows, high_rows = slice(0, cut), slice(cut, slot)
    w3 = self_query_key_value.transpose(1, 0, 2)
    w2kv = cross_kv.transpose(1, 0, 2)
    fb = first_dense_bias[None]
    gains, shifts, ob = norm_gains, norm_biases, out_biases
    bits = [1 << i for i in range(dp_size.bit_length() - 1)]
    turned_bits = bits[:1] + bits[2:] + bits[1:2]
    sources = jnp.stack([relative_source(model, bits), relative_source(model, turned_bits)], axis=1)
    chain = Chain(norm_gains)
    spot = (lax.axis_index("dp") & 3).astype(jnp.int32)
    spots = spot.reshape(1)

    def count(rows):
        return rows.stop - rows.start

    def sized(rows, width, dtype=F32):
        return shaped((count(rows), width), dtype)

    def attended(rows):
        return [(sized(rows, own, BF), "h"), (sized(rows, own), "h"), (shaped((8, count(rows))), "h"), (sized(rows, model), "v")]

    def fetched(weight, parts):
        block = weight.shape[0] // parts
        at = (spot & (parts - 1)) * block
        return lax.dynamic_slice_in_dim(weight, at, block, 0).astype(F32)

    made = chain(
        partial(self_start, cut),
        [(sized(low_rows, model, BF), "h"), (sized(high_rows, model, BF), "h")] + [(shaped((slot, own), BF), "h")] * 3
        + attended(high_rows),
        [(tok, "h"), (gains, "h"), (shifts, "h"), (self_qv_bias, "h"), (w3, "h"), (lengths, "s"), (self_output_weight, "h")],
        0,
        "self_start",
        scratch=[pltpu.VMEM((count(high_rows), LANES), F32), pltpu.VMEM((slot, model), BF)],
    )
    x1_l, x1_h, q1, k1, v1, mix1_h, out1_h, lse1_h, part1_h = made
    other1_h = chain.swap_mp(part1_h)
    mix1_l, out1_l, lse1_l, part1_l = chain(
        partial(self_next, low_rows),
        attended(low_rows),
        [(q1, "h"), (k1, "h"), (v1, "h"), (lengths, "s"), (self_output_weight, "h")],
        0,
        "self_next",
        scratch=[pltpu.VMEM((count(low_rows), LANES), F32)],
    )
    other1_l = chain.swap_mp(part1_l)
    k2, v2, turned_frames, order, order_turned = chain(
        frames_start,
        [(shaped((padded, own), BF), "h")] * 2 + [(shaped((model, padded), BF), "h")] + [(shaped((model, model), BF), "h")] * 2,
        [(frames, "h"), (w2kv, "h"), (cross_bias, "h"), (sources, "h")],
        0,
        "frames_start",
        scratch=[pltpu.VMEM((padded, model), BF)],
    )
    orders = (order, order_turned)

    def turned(plan, parts):
        used = orders[: 1 + max(place for place, _ in plan)]
        return chain(
            partial(turn, plan),
            [(shaped((model, parts[part].shape[0]), BF), "h") for _, part in plan],
            [(o, "h") for o in used] + [(p, "h") for p in parts],
            0,
            "turn",
        )


    def cross(rows, mine, other):
        return chain(
            partial(cross_start, rows, real),
            [(sized(rows, model), "h"), (sized(rows, model, BF), "h"), (sized(rows, own, BF), "h")] + attended(rows),
            [(mine, "v"), (other, "v"), (tok, "h"), (ob, "h"), (gains, "h"), (shifts, "h"), (cross_bias, "h"),
             (cross_query_weight, "h"), (k2, "h"), (v2, "h"), (cross_output_weight, "h")],
            0,
            "cross_start",
            scratch=[pltpu.VMEM((count(rows), LANES), F32)],
        )

    s1_h, x2_h, q2_h, mix2_h, out2_h, lse2_h, part2_h = cross(high_rows, part1_h, other1_h)
    other2_h = chain.swap_mp(part2_h)
    s1_l, x2_l, q2_l, mix2_l, out2_l, lse2_l, part2_l = cross(low_rows, part1_l, other1_l)
    other2_l = chain.swap_mp(part2_l)
    x1t_h, x1t_l, x2t_h, x2t_l = turned(((0, 0), (0, 1), (0, 2), (0, 3)), (x1_h, x1_l, x2_h, x2_l))

    def dense(rows, s1, mine, other):
        return chain(
            dense_start,
            [(sized(rows, model), "h"), (sized(rows, model, BF), "h"), (sized(rows, ff, BF), "h"), (sized(rows, ff), "h"),
             (sized(rows, model), "v")],
            [(mine, "v"), (other, "v"), (s1, "h"), (ob, "h"), (gains, "h"), (shifts, "h"), (fb, "h"),
             (first_dense_weight, "h"), (second_dense_weight, "h")],
            0,
            "dense_start",
        )

    s2_h, x3_h, act_h, slope_h, part3_h = dense(high_rows, s1_h, part2_h, other2_h)
    other3_h = chain.swap_mp(part3_h)
    s2_l, x3_l, act_l, slope_l, part3_l = dense(low_rows, s1_l, part2_l, other2_l)
    other3_l = chain.swap_mp(part3_l)
    x3o_h, x3o_l = turned(((1, 0), (1, 1)), (x3_h, x3_l))

    def dense_b(rows, s2, mine, other, slope):
        return chain(
            partial(dense_back, rows),
            [(sized(rows, model, BF), "h"), (sized(rows, model), "h"), (sized(rows, model, BF), "h"),
             (sized(rows, ff, BF), "h"), (sized(rows, model), "v"), (shaped((8, model)), "v"), (shaped((8, ff)), "v")],
            [(mine, "v"), (other, "v"), (s2, "h"), (ob, "h"), (gains, "h"), (shifts, "h"), (cot, "h"), (lengths, "s"),
             (second_dense_weight, "h"), (slope, "h"), (first_dense_weight, "h")],
            6 * count(rows) * model * ff,
            "dense_back",
        )

    y_h, g3_h, low3_h, hid_h, part4_h, sum3_h, hsum_h = dense_b(high_rows, s2_h, part3_h, other3_h, slope_h)
    other4_h = chain.swap_mp(part4_h)
    y_l, g3_l, low3_l, hid_l, part4_l, sum3_l, hsum_l = dense_b(low_rows, s2_l, part3_l, other3_l, slope_l)

    denses = Halving(
        chain,
        orders,
        [
            (0, bits, [((low3_h, low3_l), False, (act_h, act_l), (0,))]),
            (1, turned_bits, [((x3o_h, x3o_l), True, (hid_h, hid_l), (0,))]),
        ],
        dp_size,
        "dense",
    )
    other4_l = chain.swap_mp(chain.tie(part4_l))
    wq_0 = chain.swap_mp(chain.tie(fetched(cross_query_weight, 2)))
    chain.pause(other4_h)
    denses.keep()
    all_rows = slice(0, slot)

    def block_sizes(dtype, width):
        return [(sized(high_rows, width, dtype), "h"), (sized(low_rows, width, dtype), "h")]

    heads = [pltpu.VMEM((slot, own), BF), pltpu.VMEM((slot, own), F32)]
    joined = [pltpu.VMEM((slot, own), BF), pltpu.VMEM((slot, own), F32), pltpu.VMEM((8, slot), F32)]
    which = lax.axis_index("mp").astype(jnp.int32).reshape(1)
    half_width = model // 2
    cuts = [-(-real * n // (8 * PIECES)) * 8 for n in range(PIECES)] + [-(-real // 8) * 8]
    g2_h, low2_h, g2_l, low2_l, lq2_h, lq2_l, part5, sum2, lk2, lv2, *frames_parts = chain(
        partial(cross_back, cut, real),
        [(sized(high_rows, model), "h"), (sized(high_rows, model, BF), "h"), (sized(low_rows, model), "h"),
         (sized(low_rows, model, BF), "h")] + block_sizes(BF, own)
        + [(shaped((slot, own)), "v"), (shaped((8, model)), "v")] + [(shaped((padded, own), BF), "h")] * 2
        + [(shaped((cuts[n + 1] - cuts[n], half_width)), "r") for n in range(PIECES)],
        [(part4_h, "h"), (other4_h, "h"), (s2_h, "h"), (g3_h, "h"), (q2_h, "h"), (out2_h, "h"), (lse2_h, "h"),
         (part4_l, "h"), (other4_l, "h"), (s2_l, "h"), (g3_l, "h"), (q2_l, "h"), (out2_l, "h"), (lse2_l, "h"),
         (gains, "h"), (cross_output_weight, "h"), (k2, "h"), (v2, "h"), (which, "s"), (w2kv, "h")],
        0,
        "cross_back",
        scratch=heads + joined + [pltpu.VMEM((padded, half_width), F32), pltpu.SemaphoreType.DMA((PIECES,))],
    )
    other5 = chain.swap_mp(part5)
    wq_1 = chain.later(lambda tied=chain.link: swap_dp(lax.optimization_barrier((wq_0.value, tied))[0], 1, dp_size))
    steps(chain, [(denses, 0), (denses, 1)], (wq_0,))
    crosses = Halving(
        chain,
        orders,
        [
            (
                0,
                bits,
                [
                    ((low2_h, low2_l), False, (mix2_h, mix2_l), (0,)),
                    ((x2t_h, x2t_l), True, (lq2_h, lq2_l), (0,)),
                    ((turned_frames,), True, (lk2,), (0,)),
                    ((turned_frames,), True, (lv2,), (0,)),
                ],
            )
        ],
        dp_size,
        "cross",
    )
    frames_other = [chain.swap_mp(chain.tie(frames_parts[0]))]
    chain.pause(other5)
    crosses.keep()
    frames_other.append(chain.swap_mp(chain.tie(frames_parts[1])))
    g1_h, low1_h, g1_l, low1_l, l3_h, l3_l, part6_h, part6_l, sum1 = chain(
        partial(self_back, cut),
        [(sized(high_rows, model), "h"), (sized(high_rows, model, BF), "h"), (sized(low_rows, model), "h"),
         (sized(low_rows, model, BF), "h"), (shaped((3, count(high_rows), own), BF), "h"),
         (shaped((3, count(low_rows), own), BF), "h"), (sized(high_rows, model), "v"), (sized(low_rows, model), "v"),
         (shaped((8, model)), "v")],
        [(spots, "s"), (part5, "h"), (other5, "h"), (cross_query_weight, "h"), (wq_0, "h"), (wq_1, "h"), (gains, "h"),
         (self_output_weight, "h"), (q1, "h"), (k1, "h"), (v1, "h"), (w3, "h"), (lengths, "s"),
         (s1_h, "h"), (g2_h, "h"), (out1_h, "h"), (lse1_h, "h"), (s1_l, "h"), (g2_l, "h"), (out1_l, "h"), (lse1_l, "h")],
        0,
        "self_back",
        scratch=heads + [pltpu.VMEM((model, own), BF)] + joined + [pltpu.VMEM((2, slot, own), BF), pltpu.VMEM((slot, model), F32)],
    )
    other6_h = chain.swap_mp(part6_h)
    steps(chain, [(denses, 0), (denses, 1)], (frames_other[0],))
    selves = Halving(
        chain,
        orders,
        [
            (
                0,
                bits,
                [((low1_h, low1_l), False, (mix1_h, mix1_l), (0,)), ((x1t_h, x1t_l), True, (l3_h, l3_l), (0,))],
            ),
            (0, bits, [((x1t_h, x1t_l), True, (l3_h, l3_l), (1, 2))]),
        ],
        dp_size,
        "self",
    )
    other6_l = chain.swap_mp(chain.tie(part6_l))
    shard = model // dp_size
    crosses.step(0, (frames_other[1],))
    t_high, sum0_h = chain(
        partial(tokens_end, high_rows),
        [(sized(high_rows, model), "h"), (shaped((8, model)), "h")],
        [(tok, "h"), (gains, "h"), (g1_h, "h"), (part6_h, "v"), (other6_h, "v"), (lengths, "s")],
        0,
        "tokens_end",
        scratch=[pltpu.VMEM((8, model), F32)],
    )
    second_turned, first_grad = ends(chain, [(denses, 0), (denses, 1)], shaped((shard, ff)))
    selves.keep()
    tokens_grad, total, y = chain(
        partial(tokens_end, low_rows),
        [(shaped((slot, model)), "h"), (shaped((13 + ff // model, model)), "v"), (shaped((slot, model), BF), "h")],
        [(tok, "h"), (gains, "h"), (g1_l, "h"), (part6_l, "v"), (other6_l, "v"), (t_high, "h"), (sum0_h, "h"),
         (sum1, "h"), (sum2, "h"), (sum3_h, "h"), (sum3_l, "h"), (hsum_h, "h"), (hsum_l, "h"), (y_l, "h"), (y_h, "h")],
        0,
        "tokens_end",
        scratch=[pltpu.VMEM((8, model), F32)],
    )
    small_bits = bits[2:] + bits[:2]

    def small_step(total, other):
        (total,) = chain(plain_end, [(shaped(total.shape), "v")], [(total, "v"), (other, "v")], 0, "small_step")
        return total, chain.swap_dp(total, small_bits.pop(0), dp_size)

    small_other = chain.swap_dp(total, small_bits.pop(0), dp_size)
    frames_other.append(chain.swap_mp(chain.tie(frames_parts[2])))
    crosses.step(0)
    selves.step(0)
    total, small_other = small_step(total, small_other)
    frames_other.append(chain.swap_mp(chain.tie(frames_parts[3])))
    selves.step(1, (frames_other[2],))
    cross_out_grad, cross_q_grad, cross_kv_grad = crosses.end(
        0, cross_end, [shaped((shard, own)), shaped((shard, own)), shaped((shard, 2, own))]
    )
    selves.step(0)
    total, small_other = small_step(total, small_other)
    selves.step(1)
    while small_bits:
        total, small_other = small_step(total, small_other)
    (frames_grad,) = chain(
        frames_kept, [(shaped((real, 1, half_width)), "r")],
        [(which, "s"), (lk2, "h"), (lv2, "h"), (w2kv, "h")] + [(o, "h") for o in frames_other],
        0, "frames_kept",
        scratch=[pltpu.VMEM((padded, half_width), F32), pltpu.VMEM((real, half_width), F32), pltpu.SemaphoreType.DMA],
    )
    self_out_grad, q_grad = selves.end(0, self_end, [shaped((shard, own))] * 2)
    k_grad, v_grad = selves.end(1, self_end, [shaped((shard, own))] * 2)
    gains_grad, shifts_grad, ob_grad, svb_grad, cvb_grad, fb_grad = chain(
        small_end,
        [(shaped((4, model)), "v"), (shaped((4, model)), "v"), (shaped((3, model)), "v"), (shaped((2, own)), "v"),
         (shaped((2, own)), "v"), (shaped((ff // model, model)), "v")],
        [(total, "v"), (small_other, "v")],
        0,
        "small_end",
    )
    return (
        y[None],
        tokens_grad[None],
        frames_grad.transpose(1, 0, 2),
        jnp.stack([q_grad, k_grad, v_grad], axis=1),
        svb_grad,
        self_out_grad.T,
        cross_q_grad,
        cross_kv_grad,
        cvb_grad,
        cross_out_grad.T,
        first_grad,
        fb_grad.reshape(ff),
        second_turned.T,
        ob_grad,
        gains_grad,
        shifts_grad,
    )


def solution(mesh):
    in_specs = (
        P("dp", None, None),
        P("dp", None, None),
        P("dp"),
        P("dp", None, None),
        P(None, None, "mp"),
        P(None, "mp"),
        P("mp", None),
        P(None, "mp"),
        P(None, None, "mp"),
        P(None, "mp"),
        P("mp", None),
        P(None, "mp"),
        P("mp"),
        P("mp", None),
        P(),
        P(),
        P(),
    )
    out_specs = (
        P("dp", None, None),
        P("dp", None, None),
        P("dp", None, "mp"),
        P("dp", None, "mp"),
        P(None, "mp"),
        P("mp", "dp"),
        P("dp", "mp"),
        P("dp", None, "mp"),
        P(None, "mp"),
        P("mp", "dp"),
        P("dp", "mp"),
        P("mp"),
        P("mp", "dp"),
        P(),
        P(),
        P(),
    )
    return jax.shard_map(
        partial(on_device, mesh.shape["dp"]),
        mesh=mesh,
        in_specs=in_specs,
        out_specs=out_specs,
        check_vma=False,
    )
```
